32 devices in a mesh: dp: 8 (over z, y), tensor: 4 (over x, core).
Axes of the slice: x: 2, y: 2, z: 4, core: 2. Of those that a mesh axis runs over, the one named last changes fastest.
Arguments:
- tokens: bfloat16 [16, 1024, 768], P('dp', 'tensor'), may hold values from -6 to 6
- lengths: int32 [16], P('dp'), may hold values from 256 to 1024, as said below
- times: int32 [16], P('dp'), may hold values from 0 to 999
- cotangent: bfloat16 [16, 1024, 768], P('dp', 'tensor'), may hold values from -6 to 6
- w_qkv: bfloat16 [3, 768, 768], P(None, 'dp', 'tensor'), may hold values from -0.21875 to 0.21875
- w_out: bfloat16 [768, 768], P('tensor', 'dp'), may hold values from -2 to 2
- w_up: bfloat16 [768, 3072], P('dp', 'tensor'), may hold values from -0.21875 to 0.21875
- up_bias: bfloat16 [3072], P('dp'), may hold values from -3 to 3
- w_down: bfloat16 [3072, 768], P('tensor', 'dp'), may hold values from -0.109375 to 0.109375
- down_bias: bfloat16 [768], P('dp'), may hold values from -3 to 3
- norm1_gain: bfloat16 [768], P('dp'), may hold values from 0.5 to 1.5
- norm2_gain: bfloat16 [768], P('dp'), may hold values from 0.5 to 1.5
- ada_weight: bfloat16 [128, 4608], P(None, 'dp'), may hold values from -0.5 to 0.5
- ada_bias: bfloat16 [4608], P('dp'), may hold values from -3 to 3
Outputs:
- out: bfloat16 [16, 1024, 768], P('dp', 'tensor')
- grad_tokens: bfloat16 [16, 1024, 768], P('dp', 'tensor')
- grad_w_qkv: float32 [3, 768, 768], P(None, 'dp', 'tensor')
- grad_w_out: float32 [768, 768], P('tensor', 'dp')
- grad_w_up: float32 [768, 3072], P('dp', 'tensor')
- grad_up_bias: float32 [3072], P('dp')
- grad_w_down: float32 [3072, 768], P('tensor', 'dp')
- grad_down_bias: float32 [768], P('dp')
- grad_norm1_gain: float32 [768], P('dp')
- grad_norm2_gain: float32 [768], P('dp')
- grad_ada_weight: float32 [128, 4608], P(None, 'dp')
- grad_ada_bias: float32 [4608], P('dp')
The draws below stay inside these ranges and needn't reach their ends.
Inputs may be any that keep to these rules, and one draw needn't show every extreme that they name: A sequence's real tokens fill its first lengths slots; at least one sequence has exactly 1024.
All inputs are finite; a program needn't handle non-finite values.
Results may differ from the reference program's by a relative error of at most 0.015.
The reference program's roundings to bfloat16 on the way count: a program that leaves them out, or rounds other values in their place, can miss the bound.
Values may be sent and summed in bfloat16 or wider, within the bound.
No kernel may reach another device: no remote copies, remote signals or barrier semaphores. Data moves between devices by JAX's collectives and lax.ppermute only.
A program may use at most 128 MiB of HBM per device.

```python
import math
import jax
import jax.numpy as jnp
from jax import lax

D = 768
HEADS = 12
HEAD = 64
FF = 3072
COND = 128
SEQ_LEN = 1024
SEQ_GRP = 2
MIN_LEN = 256
SEQS = 16
N_DP = 8


def draw_lengths(key, part):
    first_key, second_key = jax.random.split(jax.random.fold_in(key, 17))
    drawn = jax.random.randint(first_key, (SEQS,), MIN_LEN, SEQ_LEN + 1)
    chosen = jax.random.randint(second_key, (), 0, SEQS)
    return jnp.where(jnp.arange(SEQS) == chosen, SEQ_LEN, drawn).astype(jnp.int32)


def place_ends(array, own_key, smallest, high):
    spot = [jax.random.randint(jax.random.fold_in(own_key, axis), (), 0, length) for axis, length in enumerate(array.shape)]
    main_axis = array.shape.index(max(array.shape))
    beside = spot[:main_axis] + [(spot[main_axis] + 1) % array.shape[main_axis]] + spot[main_axis + 1:]
    return array.at[tuple(spot)].set(smallest).at[tuple(beside)].set(high)


def spiked(entries, rng, source, target, shards_of, factor):
    owner, partner = [(jnp.arange(entries.shape[dim]) // (entries.shape[dim] // shards_of)).reshape([-1 if axis == dim else 1 for axis in range(entries.ndim)]) for dim in (source, target)]
    chosen = jax.random.permutation(rng, shards_of)[partner]
    strong = (owner == chosen) | (owner == (partner + shards_of // 2) % shards_of)
    return jnp.where(strong, factor * entries, entries)


def shard_levels(own_key, dims, cuts, low, high):
    factor_of, own = 1.0, jax.random.fold_in(own_key, 6)
    for dim, shards_of in cuts:
        draws = jnp.exp(jax.random.uniform(jax.random.fold_in(own, dim), (shards_of,), jnp.float32, low / len(cuts), high / len(cuts)))
        factor_of = factor_of * jnp.repeat(draws, dims[dim] // shards_of).reshape([-1 if axis == dim else 1 for axis in range(len(dims))])
    return factor_of


def normal_values(own_key, shape, deviation, limit, cuts=(), held_as=jnp.bfloat16):
    values = jax.random.normal(own_key, shape, jnp.float32) * deviation
    if len(cuts) > 0:
        values = shard_levels(own_key, shape, cuts, -0.22, 0.18) * values
    return jnp.clip(values, min=-limit, max=limit).astype(held_as)


def bell_draw_with(rng, shape, width, most, cuts, heavy, held_as=jnp.bfloat16):
    entries = width * jax.random.normal(rng, shape, jnp.float32)
    if cuts:
        entries = entries * shard_levels(rng, shape, cuts, -0.22, 0.18)
    return jnp.clip(spiked(entries, jax.random.fold_in(rng, 3), *heavy), -most, most).astype(held_as)


def setup_inputs(seed: int = 0) -> dict:
    streams_of = jax.random.split(jax.random.key(seed), 15)
    tokens = normal_values(streams_of[0], (SEQS, SEQ_LEN, D), 1.0, 6.0, ((0, 8), (1, 4)))
    lengths = draw_lengths(jax.random.fold_in(streams_of[14], 71), 0)
    times = place_ends(jax.random.randint(streams_of[2], (SEQS,), 0, 1000), jax.random.fold_in(streams_of[2], 1), 0, 999).astype(jnp.int32)
    cotangent = bell_draw_with(streams_of[3], (SEQS, SEQ_LEN, D), 1.0, 6.0, ((0, 8), (1, 4)), (0, 2, 8, 2.0))
    w_qkv = normal_values(streams_of[4], (3, D, D), D ** -0.5, 0.21875, ((1, 8), (2, 4)))
    w_out = normal_values(streams_of[5], (D, D), 8 ** -0.5, 2.0, ((0, 4), (1, 8)))
    w_up = normal_values(streams_of[6], (D, FF), D ** -0.5, 0.21875, ((0, 8), (1, 4)))
    up_bias = normal_values(streams_of[7], (FF,), 0.5, 3.0, ((0, 8),))
    w_down = normal_values(streams_of[8], (FF, D), FF ** -0.5, 0.109375, ((0, 4), (1, 8)))
    down_bias = normal_values(streams_of[9], (D,), 0.5, 3.0, ((0, 8),))
    norm1_gain = jnp.clip(0.5 + 1.0 * jax.random.uniform(streams_of[10], (D,), jnp.float32) ** shard_levels(streams_of[10], (D,), ((0, 8),), -0.2, 0.2), 0.5, 1.5).astype(jnp.bfloat16)
    norm2_gain = jnp.clip(0.5 + 1.0 * jax.random.uniform(streams_of[11], (D,), jnp.float32) ** shard_levels(streams_of[11], (D,), ((0, 8),), -0.2, 0.2), 0.5, 1.5).astype(jnp.bfloat16)
    ada_weight = normal_values(streams_of[12], (COND, 6 * D), COND ** -0.5, 0.5, ((1, 8),))
    ada_bias = normal_values(streams_of[13], (6 * D,), 0.5, 3.0, ((0, 8),))
    return {"tokens": tokens, "lengths": lengths, "times": times, "cotangent": cotangent, "w_qkv": w_qkv, "w_out": w_out, "w_up": w_up, "up_bias": up_bias, "w_down": w_down, "down_bias": down_bias, "norm1_gain": norm1_gain, "norm2_gain": norm2_gain, "ada_weight": ada_weight, "ada_bias": ada_bias}


@jax.custom_vjp
def low(v):
    return lax.optimization_barrier(v.astype(jnp.bfloat16)).astype(jnp.float32)

@jax.custom_vjp
def low_back(v):
    return v

def low_keep(v):
    return (low(v), None)

def low_pass(kept, grad):
    return (grad,)

def back_keep(v):
    return (v, None)

def back_low(kept, grad):
    return (low(grad),)
low.defvjp(low_keep, low_pass)
low_back.defvjp(back_keep, back_low)
norm_epsilon = 1e-05
masked_score = -1e+30

def time_embedding(time_steps, width_total):
    half_width = width_total // 2
    frequency = jnp.exp(-math.log(10000.0) * jnp.arange(half_width, dtype=jnp.float32) / half_width)
    angles = time_steps.astype(jnp.float32)[:, None] * frequency[None, :]
    return jnp.concatenate([jnp.cos(angles), jnp.sin(angles)], axis=-1)

def rotary_tables(length_total, head_width):
    half_width = head_width // 2
    inverse = jnp.exp(-math.log(10000.0) * 2.0 * jnp.arange(half_width, dtype=jnp.float32) / head_width)
    angles = jnp.arange(length_total, dtype=jnp.float32)[:, None] * inverse[None, :]
    cosine = jnp.concatenate([jnp.cos(angles), jnp.cos(angles)], axis=-1)
    sine = jnp.concatenate([jnp.sin(angles), jnp.sin(angles)], axis=-1)
    return (cosine, sine)

def rotate(vectors, cosine, sine):
    half_width = vectors.shape[-1] // 2
    turned = jnp.concatenate([-vectors[..., half_width:], vectors[..., :half_width]], axis=-1)
    return vectors * cosine[:, None, :] + turned * sine[:, None, :]

def modulate(token_rows, gain_vec, scale_vec, shift_vec):
    centered = token_rows - lax.optimization_barrier(jnp.mean(token_rows, axis=-1, keepdims=True))
    variance = lax.optimization_barrier(jnp.mean(centered * centered, axis=-1, keepdims=True))
    return centered * lax.rsqrt(variance + norm_epsilon) * gain_vec * (1.0 + scale_vec) + shift_vec

def gelu_tanh(values_in):
    return 0.5 * values_in * (1.0 + jnp.tanh(math.sqrt(2.0 / math.pi) * (values_in + 0.044715 * values_in * values_in * values_in)))

def layer(params, token_rows, condition, seq_lengths):
    w_qkv, w_out, w_up, up_bias, w_down, down_bias, norm1_gain, norm2_gain, ada_weight, ada_bias = params
    highest = lax.Precision.HIGHEST
    batch_seqs = token_rows.shape[0]
    modulation = jnp.dot(condition, ada_weight, precision=highest) + ada_bias
    shift_one, scale_one, gate_one, shift_two, scale_two, gate_two = [modulation[:, None, index * D:(index + 1) * D] for index in range(6)]
    first_in = low(modulate(token_rows, norm1_gain, scale_one, shift_one))
    projected = low_back(jnp.einsum('bld,jde->jble', first_in, w_qkv, precision=highest))
    cosine, sine = rotary_tables(SEQ_LEN, HEAD)
    shape_heads = (batch_seqs, SEQ_LEN, HEADS, HEAD)
    query_rows = low(rotate(projected[0].reshape(shape_heads), cosine, sine))
    key_rows = low(rotate(projected[1].reshape(shape_heads), cosine, sine))
    value_rows = low(projected[2].reshape(shape_heads))
    scores = low_back(jnp.einsum('bqhd,bkhd->bhqk', query_rows, key_rows, precision=highest) * HEAD ** (-0.5))
    live_keys = jnp.arange(SEQ_LEN)[None, :] < seq_lengths[:, None]
    scores = jnp.where(live_keys[:, None, None, :], scores, masked_score)
    largest = lax.optimization_barrier(jnp.max(scores, axis=-1, keepdims=True))
    weights_exp = jnp.exp(scores - largest)
    weights_soft = low(weights_exp / lax.optimization_barrier(jnp.sum(weights_exp, axis=-1, keepdims=True)))
    mixed_rows = jnp.einsum('bhqk,bkhd->bqhd', weights_soft, value_rows, precision=highest).reshape(batch_seqs, SEQ_LEN, D)
    mixed_rows = low(low_back(mixed_rows))
    attended = low_back(jnp.einsum('bld,de->ble', mixed_rows, w_out, precision=highest))
    after_attn = token_rows + gate_one * attended
    second_in = low(modulate(after_attn, norm2_gain, scale_two, shift_two))
    hidden_pre = low_back(jnp.einsum('bld,df->blf', second_in, w_up, precision=highest) + up_bias)
    active_rows = low(gelu_tanh(hidden_pre))
    branch_out = low_back(jnp.einsum('blf,fd->bld', active_rows, w_down, precision=highest) + down_bias)
    return after_attn + gate_two * branch_out

def reference(tokens, lengths, times, cotangent, w_qkv, w_out, w_up, up_bias, w_down, down_bias, norm1_gain, norm2_gain, ada_weight, ada_bias):
    condition = time_embedding(times, COND)
    params = (w_qkv.astype(jnp.float32), w_out.astype(jnp.float32), w_up.astype(jnp.float32), up_bias.astype(jnp.float32), w_down.astype(jnp.float32), down_bias.astype(jnp.float32), norm1_gain.astype(jnp.float32), norm2_gain.astype(jnp.float32), ada_weight.astype(jnp.float32), ada_bias.astype(jnp.float32))
    token_rows = tokens.astype(jnp.float32)

    def forward(param_set, input_rows):

        def one_group(group_item):
            return layer(param_set, group_item[0], group_item[1], group_item[2])
        grouped = (input_rows.reshape(N_DP, SEQ_GRP, SEQ_LEN, D), condition.reshape(N_DP, SEQ_GRP, COND), lengths.reshape(N_DP, SEQ_GRP))
        return lax.map(jax.checkpoint(one_group), grouped).reshape(SEQS, SEQ_LEN, D)
    result, pullback = jax.vjp(forward, params, token_rows)
    live_rows = (jnp.arange(SEQ_LEN)[None, :] < lengths[:, None]).astype(jnp.float32)
    grad_params, grad_rows = pullback(cotangent.astype(jnp.float32) * live_rows[:, :, None])
    return (result.astype(jnp.bfloat16), grad_rows.astype(jnp.bfloat16), grad_params[0], grad_params[1], grad_params[2], grad_params[3], grad_params[4], grad_params[5], grad_params[6], grad_params[7], grad_params[8], grad_params[9])
```

```python
import functools
import math

import jax
import jax.numpy as jnp
import numpy as np
from jax import lax
from jax.experimental import pallas as pl
from jax.experimental.pallas import tpu as pltpu
from jax.sharding import PartitionSpec as P

HEAD = 64
EPS = 1e-05
MASKED = -1e30
BF = jnp.bfloat16
F32 = jnp.float32
VMEM_MAX = 60 * 1024 * 1024
NBLK = 8
NT = (((1,), (1,)), ((), ()))


def spec(block, index_map):
    return pl.BlockSpec(block, index_map)


def whole(shape):
    return pl.BlockSpec(shape, lambda *_: (0,) * len(shape))


ANY = pl.BlockSpec(memory_space=pl.ANY)


def params():
    return pltpu.CompilerParams(vmem_limit_bytes=VMEM_MAX)


def cost(flops, moved, trans=0):
    return pl.CostEstimate(flops=flops, bytes_accessed=moved, transcendentals=trans)


def norm_rows(rows):
    centered = rows - jnp.mean(rows, axis=1, keepdims=True)
    variance = jnp.mean(centered * centered, axis=1, keepdims=True)
    inverse = lax.rsqrt(variance + EPS)
    return centered * inverse, inverse


def qkv_kernel(tab, tok, mod, gain, cos, sin, w0, w1, first, q, k, v, kt, vt, w, sem):
    heads, block = q.shape[1], q.shape[2]
    step = pl.program_id(0) * pl.num_programs(1) + pl.program_id(1)
    rows = w0.shape[2]

    @pl.when(step == 0)
    def _():
        copies = []
        for p, ref in enumerate((w0, w1)):
            for j in range(4):
                row = pl.multiple_of(tab[p * 4 + j] * rows, 16)
                copies.append(
                    pltpu.make_async_copy(
                        ref.at[j], w.at[:, pl.ds(row, rows), :], sem.at[p * 4 + j]
                    )
                )
        for copy in copies:
            copy.start()
        for copy in copies:
            copy.wait()

    normed, _ = norm_rows(tok[0].astype(F32))
    factor = gain[...] * (1.0 + mod[0, 1:2, :])
    x = (normed * factor + mod[0, 0:1, :]).astype(BF)
    first[0] = x
    wide = w.shape[2]
    low = lax.rem(lax.broadcasted_iota(jnp.int32, (block, wide), 1), HEAD) < HEAD // 2

    def rotate(vec):
        turned = jnp.where(
            low, pltpu.roll(vec, wide - HEAD // 2, 1), pltpu.roll(vec, HEAD // 2, 1)
        )
        return vec * cos[...] + turned * sin[...]

    def store_heads(ref, vec):
        for h in range(heads):
            shifted = vec if h == 0 else pltpu.roll(vec, wide - h * HEAD, 1)
            ref[0, h] = shifted[:, :HEAD].astype(BF)

    query = rotate(jnp.dot(x, w[0], preferred_element_type=F32))
    store_heads(q, query * (HEAD**-0.5))
    key = rotate(jnp.dot(x, w[1], preferred_element_type=F32))
    store_heads(k, key)
    kt[0] = key.T[: heads * HEAD].astype(BF)
    value = jnp.dot(x, w[2], preferred_element_type=F32)
    store_heads(v, value)
    vt[0] = value.T[: heads * HEAD].astype(BF)


def qkv_call(tab, tok_all, mod, gain, cos, sin, w0, w1):
    groups, seq, width = tok_all.shape
    block = seq // 4
    wide = w0.shape[3]
    heads = (wide // HEAD) * 3 // 4
    feats = heads * HEAD
    grid_spec = pltpu.PrefetchScalarGridSpec(
        num_scalar_prefetch=1,
        grid=(groups, 4),
        in_specs=[
            spec((1, block, width), lambda g, j, _: (g, j, 0)),
            spec((1, 6, width), lambda g, j, _: (g, 0, 0)),
            whole((1, width)),
            spec((block, wide), lambda g, j, _: (j, 0)),
            spec((block, wide), lambda g, j, _: (j, 0)),
            ANY,
            ANY,
        ],
        out_specs=[
            spec((1, block, width), lambda g, j, _: (g, j, 0)),
            spec((1, heads, block, HEAD), lambda g, j, _: (g, 0, j, 0)),
            spec((1, heads, block, HEAD), lambda g, j, _: (g, 0, j, 0)),
            spec((1, heads, block, HEAD), lambda g, j, _: (g, 0, j, 0)),
            spec((1, feats, block), lambda g, j, _: (g, 0, j)),
            spec((1, feats, block), lambda g, j, _: (g, 0, j)),
            whole((3, width, wide)),
        ],
        scratch_shapes=[pltpu.SemaphoreType.DMA((8,))],
    )
    head_shape = jax.ShapeDtypeStruct((groups, heads, seq, HEAD), BF)
    turned = jax.ShapeDtypeStruct((groups, feats, seq), BF)
    return pl.pallas_call(
        qkv_kernel,
        grid_spec=grid_spec,
        out_shape=[
            jax.ShapeDtypeStruct((groups, seq, width), BF),
            head_shape,
            head_shape,
            head_shape,
            turned,
            turned,
            jax.ShapeDtypeStruct((3, width, wide), BF),
        ],
        compiler_params=params(),
        cost_estimate=cost(2 * groups * seq * width * wide * 3, 16 * 2**20),
        name="qkv",
    )(tab, tok_all, mod, gain, cos, sin, w0, w1)


def attend_kernel(lens, q, k, vt, mixed, probs):
    heads, seq = k.shape[1], k.shape[2]
    block = q.shape[2]
    live = lax.broadcasted_iota(jnp.int32, (seq, block), 0) < lens[pl.program_id(0)]
    parts = []
    for h in range(heads):
        scores = lax.dot_general(k[0, h], q[0, h], NT, preferred_element_type=F32)
        scores = jnp.where(live, scores, MASKED)
        largest = jnp.max(scores, axis=0, keepdims=True)
        weights = jnp.exp(scores - largest)
        total = jnp.sum(weights, axis=0, keepdims=True)
        low = (weights * (1.0 / total)).astype(BF)
        probs[0, h] = low
        parts.append(
            jnp.dot(vt[0, h * HEAD : (h + 1) * HEAD, :], low, preferred_element_type=F32)
        )
    pad = (-heads * HEAD) % 128
    if pad:
        parts.append(jnp.zeros((pad, block), F32))
    mixed[0, 0] = jnp.concatenate(parts, axis=0).T[:, : heads * HEAD].astype(BF)


def attend_call(lens, q, k, vt):
    groups, heads, seq, _ = q.shape
    block = seq // 4
    feats = heads * HEAD
    grid_spec = pltpu.PrefetchScalarGridSpec(
        num_scalar_prefetch=1,
        grid=(groups, 4),
        in_specs=[
            spec((1, heads, block, HEAD), lambda g, j, _: (g, 0, j, 0)),
            spec((1, heads, seq, HEAD), lambda g, j, _: (g, 0, 0, 0)),
            spec((1, feats, seq), lambda g, j, _: (g, 0, 0)),
        ],
        out_specs=[
            spec((1, 1, block, feats), lambda g, j, _: (j, g, 0, 0)),
            spec((1, heads, seq, block), lambda g, j, _: (g, 0, 0, j)),
        ],
    )
    return pl.pallas_call(
        attend_kernel,
        grid_spec=grid_spec,
        out_shape=[
            jax.ShapeDtypeStruct((4, groups, block, feats), BF),
            jax.ShapeDtypeStruct((groups, heads, seq, seq), BF),
        ],
        compiler_params=params(),
        cost_estimate=cost(
            16 * groups * heads * seq * seq * HEAD, 20 * 2**20, groups * heads * seq * seq
        ),
        name="attend",
    )(lens, q, k, vt)


def attend_back_kernel(q, kt, v, probs, gm, cos, sin, out, dk, dv):
    heads, block = q.shape[1], q.shape[2]
    half = HEAD // 2
    j = pl.program_id(1)

    @pl.when(j == 0)
    def _():
        dk[...] = jnp.zeros_like(dk)
        dv[...] = jnp.zeros_like(dv)

    columns = pl.ds(pl.multiple_of(j * block, 128), block)
    cos_here, sin_here = cos[:, columns], sin[:, columns]

    def store_turned(plane, h, vec, c, s, where):
        low, high = vec[:half], vec[half:]
        base = h * HEAD
        out[0, plane, base : base + half, where] = (low * c + high * s).astype(BF)
        out[0, plane, base + half : base + HEAD, where] = (high * c - low * s).astype(BF)

    for h in range(heads):
        tile = h // 2 * 128
        stop = min(tile + 128, heads * HEAD)
        part = gm[0, 0, :, tile:stop].astype(F32)
        if h % 2:
            part = pltpu.roll(part, HEAD, 1)
        grad = part[:, :HEAD].astype(BF)
        low = probs[0, h]
        dp = lax.dot_general(v[0, h], grad, NT, preferred_element_type=F32)
        soft = low.astype(F32)
        prod = soft * dp
        inner = jnp.sum(prod, axis=0, keepdims=True)
        ds = (prod - soft * inner).astype(BF)
        dv[h] += jnp.dot(low, grad, preferred_element_type=F32)
        dk[h] += jnp.dot(ds, q[0, h], preferred_element_type=F32)
        dq = jnp.dot(kt[0, h * HEAD : (h + 1) * HEAD, :], ds, preferred_element_type=F32)
        store_turned(0, h, dq * (HEAD**-0.5), cos_here, sin_here, columns)

    @pl.when(j == pl.num_programs(1) - 1)
    def _():
        for h in range(heads):
            store_turned(1, h, dk[h].T, cos[...], sin[...], slice(None))
            out[0, 2, h * HEAD : (h + 1) * HEAD, :] = dv[h].T.astype(BF)


def attend_back_call(q, kt, v, probs, gm, cos, sin):
    groups, heads, seq, _ = q.shape
    block = seq // 4
    feats = heads * HEAD
    half = HEAD // 2
    return pl.pallas_call(
        attend_back_kernel,
        grid=(groups, 4),
        in_specs=[
            spec((1, heads, block, HEAD), lambda g, j: (g, 0, j, 0)),
            spec((1, feats, seq), lambda g, j: (g, 0, 0)),
            spec((1, heads, seq, HEAD), lambda g, j: (g, 0, 0, 0)),
            spec((1, heads, seq, block), lambda g, j: (g, 0, 0, j)),
            spec((1, 1, block, feats), lambda g, j: (j, g, 0, 0)),
            whole((half, seq)),
            whole((half, seq)),
        ],
        out_specs=spec((1, 3, feats, seq), lambda g, j: (g, 0, 0, 0)),
        out_shape=jax.ShapeDtypeStruct((groups, 3, feats, seq), BF),
        scratch_shapes=[
            pltpu.VMEM((heads, seq, HEAD), F32),
            pltpu.VMEM((heads, seq, HEAD), F32),
        ],
        compiler_params=params(),
        cost_estimate=cost(32 * groups * heads * seq * seq * HEAD, 20 * 2**20),
        name="attend_back",
    )(q, kt, v, probs, gm, cos, sin)


def qkv_back_kernel(tab, gt, first, tok, w, fts, ftk, sums, dw, acc):
    i = pl.program_id(0)
    feats, block = gt.shape[2], gt.shape[3]
    wide, width = w.shape[2], w.shape[1]
    rows = dw.shape[2]
    g = lax.rem(i, 2)

    @pl.when(i == 0)
    def _():
        acc[...] = jnp.zeros_like(acc)
        sums[...] = jnp.zeros_like(sums)

    total = None
    for j in range(3):
        part = gt[0, j]
        tall = part.astype(F32)
        if wide > feats:
            tall = jnp.concatenate([tall, jnp.zeros((wide - feats, block), F32)], axis=0)
        term = lax.dot_general(tall.T.astype(BF), w[j], NT, preferred_element_type=F32)
        total = term if total is None else total + term
        acc[j, :feats] += jnp.dot(part, first[0], preferred_element_type=F32)
    normed, _ = norm_rows(tok[0].astype(F32))
    sums[g, 0:1, :] += jnp.sum(total, axis=0, keepdims=True)
    sums[g, 1:2, :] += jnp.sum(total * normed, axis=0, keepdims=True)
    low = total.astype(BF)

    @pl.when(i < 4)
    def _():
        fts[0, 0] = low

    @pl.when(i >= 4)
    def _():
        ftk[0, 0] = low

    @pl.when(i == pl.num_programs(0) - 1)
    def _():
        for j in range(3):
            flat = acc[j].T.astype(BF)
            for b in range(NBLK):
                dw[tab[b], j] = flat[b * rows : (b + 1) * rows]


def qkv_back_call(tab, gt, first, tok_all, w):
    groups, _, feats, seq = gt.shape
    block = seq // 4
    width = first.shape[2]
    wide = w.shape[2]
    rows = width // NBLK

    def piece(i, tab):
        return lax.bitwise_xor(tab[NBLK], lax.rem(i, 4) // 2 * 2 + (1 - i // 4))

    grid_spec = pltpu.PrefetchScalarGridSpec(
        num_scalar_prefetch=1,
        grid=(8,),
        in_specs=[
            spec((1, 3, feats, block), lambda i, tab: (lax.rem(i, 2), 0, 0, piece(i, tab))),
            spec((1, block, width), lambda i, tab: (lax.rem(i, 2), piece(i, tab), 0)),
            spec((1, block, width), lambda i, tab: (lax.rem(i, 2), piece(i, tab), 0)),
            whole((3, width, wide)),
        ],
        out_specs=[
            spec(
                (1, 1, block, width),
                lambda i, tab: (jnp.minimum(i, 3) // 2, lax.rem(jnp.minimum(i, 3), 2), 0, 0),
            ),
            spec(
                (1, 1, block, width),
                lambda i, tab: (
                    jnp.maximum(i - 4, 0) // 2,
                    lax.rem(jnp.maximum(i - 4, 0), 2),
                    0,
                    0,
                ),
            ),
            whole((groups, 2, width)),
            whole((NBLK, 3, rows, wide)),
        ],
        scratch_shapes=[pltpu.VMEM((3, wide, width), F32)],
    )
    terms = jax.ShapeDtypeStruct((2, groups, block, width), BF)
    return pl.pallas_call(
        qkv_back_kernel,
        grid_spec=grid_spec,
        out_shape=[
            terms,
            terms,
            jax.ShapeDtypeStruct((groups, 2, width), F32),
            jax.ShapeDtypeStruct((NBLK, 3, rows, wide), BF),
        ],
        compiler_params=params(),
        cost_estimate=cost(4 * groups * seq * width * wide * 3, 16 * 2**20),
        name="qkv_back",
    )(tab, gt, first, tok_all, w)


def mlp_kernel(
    tab,
    tok,
    cot,
    mixed,
    mod,
    gain,
    upb,
    downb,
    *rest,
):
    pieces = rest[:8]
    (
        out,
        gafter,
        gmixed,
        sums,
        upsum,
        gu_s,
        gu_k,
        gd_s,
        gd_k,
        w,
        gu,
        gd,
        after,
        normed,
        inverse,
        second,
        second_t,
        gbr,
        gbr_t,
        att,
        branch,
        gsec,
        act,
        gh,
        sem_w,
        sem_g,
        sem_d,
    ) = rest[8:]
    groups, block, width = tok.shape
    feats = mixed.shape[3]
    rows = pieces[0].shape[1]
    fh = upb.shape[1]
    total_rows = groups * block
    t_part, t_row, t_slot, t_dst = 3, 7, 39, 47

    loads = []
    for p in range(8):
        for j in range(4):
            row = pl.multiple_of(tab[t_row + p * 4 + j] * rows, 16)
            loads.append(
                pltpu.make_async_copy(
                    pieces[p].at[j],
                    w.at[tab[t_slot + p], pl.ds(row, rows), :],
                    sem_w.at[p * 4 + j],
                )
            )
    for load in loads:
        load.start()
    for load in loads:
        load.wait()

    def span(g):
        return pl.ds(pl.multiple_of(g * block, block), block)

    def prepare(g, _):
        here = span(g)
        total = jnp.zeros((block, width), F32)
        for k in range(4):
            total += lax.dot_general(
                mixed[tab[t_part + k], g],
                w[k, :, 2 * fh : 2 * fh + feats],
                NT,
                preferred_element_type=F32,
            )
        att[here, :] = total
        rows_after = tok[g].astype(F32) + mod[g, 2:3, :] * total
        after[here, :] = rows_after
        n, inv = norm_rows(rows_after)
        normed[here, :] = n
        inverse[here, :] = jnp.broadcast_to(inv, (block, 128))
        x = n * (gain[...] * (1.0 + mod[g, 4:5, :])) + mod[g, 3:4, :]
        second[here, :] = x.astype(BF)
        position = tab[2] + lax.broadcasted_iota(jnp.int32, (block, width), 0)
        grad_y = jnp.where(position < tab[g], cot[g].astype(F32), 0.0)
        gb = (mod[g, 5:6, :] * grad_y).astype(BF)
        gbr[here, :] = gb
        sums[g, 4:5, :] = jnp.sum(gb.astype(F32), axis=0, keepdims=True)
        branch[here, :] = jnp.broadcast_to(downb[...], (block, width))
        gsec[here, :] = jnp.zeros((block, width), F32)
        return 0

    lax.fori_loop(0, groups, prepare, 0)
    second_t[...] = second[...].T
    gbr_t[...] = gbr[...].T

    c1, c3 = math.sqrt(2.0 / math.pi), 0.044715

    def store_grads(k, src, send, keep, sem):
        for b in range(NBLK):
            there = tab[t_dst + k * NBLK + b]
            piece = src.at[k, pl.ds(b * rows, rows), :]

            @pl.when(k < 2)
            def _():
                pltpu.make_async_copy(piece, keep.at[there], sem.at[k, b]).start()

            @pl.when(k >= 2)
            def _():
                pltpu.make_async_copy(piece, send.at[there], sem.at[k, b]).start()

    def slot(k, _):
        part = tab[t_part + k]
        bias = upb[pl.ds(part, 1), :]

        def half(g, total):
            here = span(g)
            hidden = jnp.dot(second[here, :], w[k, :, :fh], preferred_element_type=F32) + bias
            square = hidden * hidden
            th = jnp.tanh(c1 * hidden * (1.0 + c3 * square))
            up = 0.5 * (1.0 + th)
            active = (hidden * up).astype(BF)
            act[here, :] = active
            slope = up + (0.5 * c1) * hidden * (1.0 - th * th) * (1.0 + (3.0 * c3) * square)
            branch[here, :] += lax.dot_general(
                active, w[k, :, fh : 2 * fh], NT, preferred_element_type=F32
            )
            ga = jnp.dot(gbr[here, :], w[k, :, fh : 2 * fh], preferred_element_type=F32)
            grad = (ga * slope).astype(BF)
            gh[here, :] = grad
            gsec[here, :] += lax.dot_general(
                grad, w[k, :, :fh], NT, preferred_element_type=F32
            )
            return total + jnp.sum(grad.astype(F32), axis=0, keepdims=True)

        upsum[pl.ds(part, 1), :] = lax.fori_loop(0, groups, half, jnp.zeros((1, fh), F32))

        def grads(r, _):
            these = pl.ds(pl.multiple_of(r * 256, 256), 256)
            gu[k, these, :] = jnp.dot(
                second_t[these, :], gh[...], preferred_element_type=F32
            ).astype(BF)
            gd[k, these, :fh] = jnp.dot(
                gbr_t[these, :], act[...], preferred_element_type=F32
            ).astype(BF)
            return 0

        lax.fori_loop(0, width // 256, grads, 0)
        store_grads(k, gu, gu_s, gu_k, sem_g)
        return 0

    lax.fori_loop(0, 4, slot, 0)

    def finish(g, _):
        here = span(g)
        position = tab[2] + lax.broadcasted_iota(jnp.int32, (block, width), 0)
        grad_y = jnp.where(position < tab[g], cot[g].astype(F32), 0.0)
        out[g] = (after[here, :] + mod[g, 5:6, :] * branch[here, :]).astype(BF)
        sums[g, 2:3, :] = jnp.sum(grad_y * branch[here, :], axis=0, keepdims=True)
        n = normed[here, :]
        gs = gsec[here, :]
        sums[g, 0:1, :] = jnp.sum(gs, axis=0, keepdims=True)
        sums[g, 1:2, :] = jnp.sum(gs * n, axis=0, keepdims=True)
        scaled = gs * (gain[...] * (1.0 + mod[g, 4:5, :]))
        mean = jnp.mean(scaled, axis=1, keepdims=True)
        along = jnp.mean(scaled * n, axis=1, keepdims=True)
        grad = grad_y + inverse[here, 0:1] * (scaled - mean - n * along)
        gafter[g] = grad
        sums[g, 3:4, :] = jnp.sum(grad * att[here, :], axis=0, keepdims=True)
        low = (mod[g, 2:3, :] * grad).astype(BF)
        gbr[here, :] = low
        for k in range(4):
            gmixed[tab[t_part + k], g] = jnp.dot(
                low, w[k, :, 2 * fh : 2 * fh + feats], preferred_element_type=F32
            ).astype(BF)
        return 0

    lax.fori_loop(0, groups, finish, 0)
    gbr_t[...] = gbr[...].T

    def last(k, _):
        part = mixed[tab[t_part + k]].reshape(total_rows, feats)
        gd[k, :, fh : fh + feats] = jnp.dot(
            gbr_t[...], part, preferred_element_type=F32
        ).astype(BF)
        store_grads(k, gd, gd_s, gd_k, sem_d)
        return 0

    lax.fori_loop(0, 4, last, 0)
    for k in range(4):
        for b in range(NBLK):
            pltpu.make_async_copy(
                gu.at[k, pl.ds(b * rows, rows), :], gu_s.at[0], sem_g.at[k, b]
            ).wait()
            pltpu.make_async_copy(
                gd.at[k, pl.ds(b * rows, rows), :], gd_s.at[0], sem_d.at[k, b]
            ).wait()


def mlp_call(tab, tok, cot, mixed, mod, gain, upb, downb, pieces):
    groups, block, width = tok.shape
    feats = mixed.shape[3]
    fh = upb.shape[1]
    lanes = pieces[0].shape[2]
    rows = width // NBLK
    total = groups * block
    vm = pl.BlockSpec(memory_space=pltpu.VMEM)
    sm = pl.BlockSpec(memory_space=pltpu.SMEM)
    up = jax.ShapeDtypeStruct((16, rows, fh), BF)
    down = jax.ShapeDtypeStruct((16, rows, fh + feats), BF)
    return pl.pallas_call(
        mlp_kernel,
        in_specs=[sm] + [vm] * 7 + [ANY] * 8,
        out_specs=[vm] * 5 + [ANY] * 4,
        out_shape=[
            jax.ShapeDtypeStruct((groups, block, width), BF),
            jax.ShapeDtypeStruct((groups, block, width), F32),
            jax.ShapeDtypeStruct((4, groups, block, feats), BF),
            jax.ShapeDtypeStruct((groups, 8, width), F32),
            jax.ShapeDtypeStruct((4, fh), F32),
            up,
            up,
            down,
            down,
        ],
        scratch_shapes=[
            pltpu.VMEM((4, width, lanes), BF),
            pltpu.VMEM((4, width, fh), BF),
            pltpu.VMEM((4, width, fh + feats), BF),
            pltpu.VMEM((total, width), F32),
            pltpu.VMEM((total, width), F32),
            pltpu.VMEM((total, 128), F32),
            pltpu.VMEM((total, width), BF),
            pltpu.VMEM((width, total), BF),
            pltpu.VMEM((total, width), BF),
            pltpu.VMEM((width, total), BF),
            pltpu.VMEM((total, width), F32),
            pltpu.VMEM((total, width), F32),
            pltpu.VMEM((total, width), F32),
            pltpu.VMEM((total, fh), BF),
            pltpu.VMEM((total, fh), BF),
            pltpu.SemaphoreType.DMA((32,)),
            pltpu.SemaphoreType.DMA((4, NBLK)),
            pltpu.SemaphoreType.DMA((4, NBLK)),
        ],
        compiler_params=params(),
        cost_estimate=cost(12 * total * width * fh * 4, 28 * 2**20, total * fh * 4),
        name="mlp",
    )(tab, tok, cot, mixed, mod, gain, upb, downb, *pieces)


def time_embedding(time_steps, width_total):
    half_width = width_total // 2
    frequency = jnp.exp(-math.log(10000.0) * jnp.arange(half_width, dtype=F32) / half_width)
    angles = time_steps.astype(F32)[:, None] * frequency[None, :]
    return jnp.concatenate([jnp.cos(angles), jnp.sin(angles)], axis=-1)


def rotary_halves(length_total):
    half = HEAD // 2
    inverse = jnp.exp(-math.log(10000.0) * 2.0 * jnp.arange(half, dtype=F32) / HEAD)
    angles = jnp.arange(length_total, dtype=F32)[:, None] * inverse[None, :]
    return jnp.cos(angles), jnp.sin(angles)


def device_index(z, y, x, c):
    return ((z * 2 + y) * 2 + x) * 2 + c


def permutation(move):
    pairs = []
    for z in range(4):
        for y in range(2):
            for x in range(2):
                for c in range(2):
                    pairs.append((device_index(z, y, x, c), device_index(*move(z, y, x, c))))
    return pairs


CORE = permutation(lambda z, y, x, c: (z, y, x, 1 - c))
FLIP_X = permutation(lambda z, y, x, c: (z, y, 1 - x, c))
FLIP_Y = permutation(lambda z, y, x, c: (z, 1 - y, x, c))
FIRST = permutation(lambda z, y, x, c: (z, 1 - y, x, c) if c == 0 else (z, y, 1 - x, c))
SECOND = permutation(lambda z, y, x, c: (z, y, 1 - x, c) if c == 0 else (z, 1 - y, x, c))
ALONG_Z = [permutation(lambda z, y, x, c, s=s: ((z + s) % 4, y, x, c)) for s in range(4)]


def send(array, pairs):
    return lax.ppermute(array, ("dp", "tensor"), pairs)


def gather_z(shard):
    parts = [shard] + [send(shard, ALONG_Z[s]) for s in (1, 2, 3)]
    return jnp.stack(parts)


def reduce_chunk(sent, kept):
    shape = (2, 2, 4) + sent.shape[1:]
    kept = kept.reshape(shape)
    got = send(sent, CORE).reshape(shape)
    first_half = (kept[1].astype(F32) + got[1].astype(F32)).astype(BF)
    got_two = send(first_half, SECOND)
    second_half = (
        kept[0, 1].astype(F32) + got[0, 1].astype(F32) + got_two[1].astype(F32)
    ).astype(BF)
    got_three = send(second_half, FIRST)
    summed = (
        kept[0, 0].astype(F32)
        + got[0, 0].astype(F32)
        + got_two[0].astype(F32)
        + got_three.astype(F32)
    )
    result = summed[0]
    for s in (1, 2, 3):
        result = result + send(summed[s].astype(BF), ALONG_Z[s]).astype(F32)
    return result


def tables(z, y, x, c):
    far_core = np.array([0, 0, 0, 0, 1, 1, 1, 1])
    kind = np.array([0, 1, 2, 3] * 2)
    core = jnp.bitwise_xor(c, far_core)
    rel_x = jnp.where(kind == 0, 0, jnp.where(kind == 3, 1, jnp.where(kind == 1, core, 1 - core)))
    rel_y = jnp.where(kind == 0, 0, jnp.where(kind == 3, 1, jnp.where(kind == 1, 1 - core, core)))
    slots = far_core * 2 + rel_x
    back = np.arange(4)
    from_z = jnp.remainder(z - back, 4)
    weight_rows = (from_z[None, :] * 2 + jnp.bitwise_xor(y, rel_y)[:, None]).reshape(32)
    slot = np.arange(4)
    parts = jnp.bitwise_xor(x, slot % 2) * 2 + jnp.bitwise_xor(c, slot // 2)
    block = np.arange(NBLK)
    to_z = jnp.remainder(block // 2 - z, 4)
    to_y = jnp.bitwise_xor(block % 2, y)
    slot_core = jnp.bitwise_xor(c, slot // 2)[:, None]
    to_x = (slot % 2)[:, None]
    major = jnp.where(slot_core == 0, to_x, to_y[None, :])
    minor = jnp.where(slot_core == 0, to_y[None, :], to_x)
    targets = (major * 8 + minor * 4 + to_z[None, :]).reshape(4 * NBLK)
    qkv_rows = jnp.concatenate(
        [from_z * 2 + y, from_z * 2 + (1 - y)]
    )
    qkv_targets = to_y * 4 + to_z
    return parts, weight_rows, slots, targets, qkv_rows, qkv_targets


def shards(
    tokens,
    lengths,
    times,
    cotangent,
    w_qkv,
    w_out,
    w_up,
    up_bias,
    w_down,
    down_bias,
    norm1_gain,
    norm2_gain,
    ada_weight,
    ada_bias,
):
    groups, block, width = tokens.shape
    dp, tp = lax.axis_size("dp"), lax.axis_size("tensor")
    seq = block * tp
    t = lax.axis_index("tensor")
    d = lax.axis_index("dp")
    fast = dp == 8 and tp == 4
    feats = w_qkv.shape[2]
    fh = w_up.shape[1]
    rows = width // NBLK
    zero = jnp.zeros((), jnp.int32)
    z, y, x, c = (d // 2, d % 2, t // 2, t % 2) if fast else (zero, zero, zero, zero)
    here = t if fast else zero
    parts, weight_rows, slots, targets, qkv_rows, qkv_targets = tables(z, y, x, c)

    pad = (-feats) % 128
    qkv_shard = jnp.pad(w_qkv, ((0, 0), (0, 0), (0, pad)))
    mlp_shard = jnp.concatenate([w_up, w_down.T, w_out.T], axis=1)
    if fast:
        near = gather_z(qkv_shard)
        qkv_pieces = (near, send(near, FLIP_Y))
        base = gather_z(mlp_shard)
        one = send(base, FIRST)
        two = send(base, SECOND)
        both = send(one, SECOND)
        own = (base, one, two, both)
        pieces = own + tuple(send(piece, CORE) for piece in own)
    else:
        full = lax.all_gather(qkv_shard, "dp", axis=1, tiled=True)
        full = full.reshape(3, NBLK, rows, feats + pad).transpose(1, 0, 2, 3)
        order = [[(-j) % 4 * 2 + p for j in range(4)] for p in range(2)]
        qkv_pieces = tuple(jnp.stack([full[b] for b in order[p]]) for p in range(2))
        full = lax.all_gather(mlp_shard, "dp", axis=0, tiled=True)
        full = lax.all_gather(full, "tensor", axis=0, tiled=False)
        full = full.reshape(tp, NBLK, rows, full.shape[2])
        pieces = []
        for far in range(2):
            for rel_x, rel_y in ((0, 0), (far, 1 - far), (1 - far, far), (1, 1)):
                pieces.append(
                    jnp.stack([full[rel_x * 2 + far, b] for b in order[rel_y]])
                )
        pieces = tuple(pieces)
    tok_all = lax.all_gather(tokens, "tensor", axis=1, tiled=True)

    all_times = lax.all_to_all(
        jnp.broadcast_to(times[None, :], (dp, groups)), "dp", 0, 0, tiled=True
    ).reshape(-1)
    condition = time_embedding(all_times, ada_weight.shape[0])
    part = jnp.dot(
        condition, ada_weight.astype(F32), precision=lax.Precision.HIGHEST
    ) + ada_bias.astype(F32)
    cols = part.shape[1]
    vectors = jnp.concatenate([up_bias, down_bias, norm1_gain, norm2_gain]).astype(F32)
    payload = jnp.concatenate(
        [
            part.reshape(dp, groups * cols),
            jnp.broadcast_to(vectors[None, :], (dp, vectors.shape[0])),
        ],
        axis=1,
    )
    payload = lax.all_to_all(payload, "dp", 0, 0, tiled=True)
    mod = (
        payload[:, : groups * cols]
        .reshape(dp, groups, cols)
        .transpose(1, 0, 2)
        .reshape(groups, 6, width)
    )
    at = groups * cols
    small = []
    for count in (up_bias.shape[0], down_bias.shape[0], norm1_gain.shape[0], norm2_gain.shape[0]):
        small.append(payload[:, at : at + count].reshape(-1))
        at += count
    upb_all = small[0].reshape(tp, fh)
    downb_all, gain_one, gain_two = (v.reshape(1, width) for v in small[1:])

    cos, sin = rotary_halves(seq)
    heads_wide = (feats + pad) // HEAD
    cos_wide = jnp.tile(jnp.concatenate([cos, cos], axis=1), (1, heads_wide))
    sin_wide = jnp.tile(jnp.concatenate([-sin, sin], axis=1), (1, heads_wide))
    first_all, q, k, v, kt, vt, w_all = qkv_call(
        qkv_rows.astype(jnp.int32), tok_all, mod, gain_one, cos_wide, sin_wide, *qkv_pieces
    )
    mixed, probs = attend_call(lengths, q, k, vt)
    mixed = lax.all_to_all(mixed, "tensor", 0, 0, tiled=True)

    tab = jnp.concatenate(
        [
            lengths,
            (t * block).reshape(1),
            parts,
            weight_rows,
            slots,
            targets,
        ]
    ).astype(jnp.int32)
    out, grad_after, grad_mixed, sums, upsum, gu_s, gu_k, gd_s, gd_k = mlp_call(
        tab, tokens, cotangent, mixed, mod, gain_two, upb_all, downb_all, pieces
    )
    grad_mixed = lax.all_to_all(grad_mixed, "tensor", 0, 0, tiled=True)
    grad_t = attend_back_call(q, kt, v, probs, grad_mixed, cos.T, sin.T)
    fts, ftk, sums_one, dw = qkv_back_call(
        jnp.concatenate([qkv_targets, here.reshape(1)]).astype(jnp.int32),
        grad_t,
        first_all,
        tok_all,
        w_all,
    )

    if fast:
        sum_up = reduce_chunk(gu_s, gu_k)
        sum_down = reduce_chunk(gd_s, gd_k)
        near, far = dw[:4], dw[4:]
        near = near.astype(F32) + send(far, FLIP_Y).astype(F32)
        sum_qkv = near[0]
        for s in (1, 2, 3):
            sum_qkv = sum_qkv + send(near[s].astype(BF), ALONG_Z[s]).astype(F32)
        got = send(fts, CORE)
        far = (ftk[1].astype(F32) + got[1].astype(F32)).astype(BF)
        grad_first = ftk[0].astype(F32) + got[0].astype(F32) + send(far, FLIP_X).astype(F32)
    else:

        def absolute(sent, kept):
            lanes = sent.shape[2]
            near = kept.reshape(2, 2, 4, rows, lanes)
            far = sent.reshape(2, 2, 4, rows, lanes).transpose(1, 0, 2, 3, 4)
            both = jnp.stack([near, far], axis=1)
            return both.transpose(0, 1, 3, 2, 4, 5).reshape(tp, width, lanes).astype(F32)

        def reduce_all(sent, kept):
            terms = lax.psum_scatter(
                absolute(sent, kept), "tensor", scatter_dimension=0, tiled=True
            )[0]
            return lax.psum_scatter(terms, "dp", scatter_dimension=0, tiled=True)

        sum_up = reduce_all(gu_s, gu_k)
        sum_down = reduce_all(gd_s, gd_k)
        terms = dw.reshape(2, 4, 3, rows, feats + pad).transpose(2, 1, 0, 3, 4)
        terms = terms.reshape(3, width, feats + pad).astype(F32)
        sum_qkv = lax.psum_scatter(terms, "dp", scatter_dimension=1, tiled=True)
        terms = jnp.stack([ftk, fts], axis=1).reshape(tp, groups, block, width).astype(F32)
        grad_first = lax.psum_scatter(terms, "tensor", scatter_dimension=0, tiled=True)[0]

    p_one, q_one = sums_one[:, 0], sums_one[:, 1]
    p_two, q_two = sums[:, 0], sums[:, 1]
    grad_mod = jnp.stack(
        [p_one, gain_one * q_one, sums[:, 3], p_two, gain_two * q_two, sums[:, 2]], axis=1
    )
    grad_mod = grad_mod.reshape(groups, dp, cols).transpose(1, 0, 2).reshape(dp, groups * cols)
    payload = jnp.concatenate(
        [
            grad_mod,
            upsum.reshape(dp, -1),
            jnp.sum(sums[:, 4], axis=0).reshape(dp, -1),
            jnp.sum((1.0 + mod[:, 1]) * q_one, axis=0).reshape(dp, -1),
            jnp.sum((1.0 + mod[:, 4]) * q_two, axis=0).reshape(dp, -1),
        ],
        axis=1,
    )
    lanes = payload.shape[1]
    payload = jnp.broadcast_to(payload[:, None, :], (dp, tp, lanes)).reshape(dp * tp, lanes)
    payload = lax.all_to_all(payload, ("dp", "tensor"), 0, 0, tiled=True)
    payload = jnp.sum(payload.reshape(dp, tp, lanes), axis=1)
    mods = payload[:, : groups * cols].reshape(dp * groups, cols)
    grad_adaw = jnp.dot(condition.T, mods, precision=lax.Precision.HIGHEST)
    grad_adab = jnp.sum(mods, axis=0)
    vectors = jnp.sum(payload[:, groups * cols :], axis=0)
    at, small = 0, []
    for count in (up_bias.shape[0], down_bias.shape[0], norm1_gain.shape[0], norm2_gain.shape[0]):
        small.append(vectors[at : at + count])
        at += count

    normed, inverse = (
        a.reshape(groups, block, -1)
        for a in norm_rows(tokens.astype(F32).reshape(groups * block, width))
    )
    scaled = grad_first * (gain_one * (1.0 + mod[:, 1]))[:, None, :]
    mean = jnp.mean(scaled, axis=-1, keepdims=True)
    along = jnp.mean(scaled * normed, axis=-1, keepdims=True)
    grad_input = grad_after + inverse * (scaled - mean - normed * along)

    return (
        out,
        grad_input.astype(BF),
        sum_qkv[:, :, :feats],
        sum_down[:, fh:].T,
        sum_up,
        small[0],
        sum_down[:, :fh].T,
        small[1],
        small[2],
        small[3],
        grad_adaw,
        grad_adab,
    )


def solution(mesh):
    in_specs = (
        P("dp", "tensor", None),
        P("dp"),
        P("dp"),
        P("dp", "tensor", None),
        P(None, "dp", "tensor"),
        P("tensor", "dp"),
        P("dp", "tensor"),
        P("dp"),
        P("tensor", "dp"),
        P("dp"),
        P("dp"),
        P("dp"),
        P(None, "dp"),
        P("dp"),
    )
    out_specs = (
        P("dp", "tensor", None),
        P("dp", "tensor", None),
        P(None, "dp", "tensor"),
        P("tensor", "dp"),
        P("dp", "tensor"),
        P("dp"),
        P("tensor", "dp"),
        P("dp"),
        P("dp"),
        P("dp"),
        P(None, "dp"),
        P("dp"),
    )
    return jax.shard_map(shards, mesh=mesh, in_specs=in_specs, out_specs=out_specs, check_vma=False)
```

```python
import functools
import math

import jax
import jax.numpy as jnp
import numpy as np
from jax import lax
from jax.experimental import pallas as pl
from jax.experimental.pallas import tpu as pltpu
from jax.sharding import PartitionSpec as P

HEAD = 64
EPS = 1e-05
MASKED = -1e30
BF = jnp.bfloat16
F32 = jnp.float32
VMEM_MAX = 60 * 1024 * 1024
NBLK = 8
NT = (((1,), (1,)), ((), ()))


def spec(block, index_map):
    return pl.BlockSpec(block, index_map)


def whole(shape):
    return pl.BlockSpec(shape, lambda *_: (0,) * len(shape))


ANY = pl.BlockSpec(memory_space=pl.ANY)


def params():
    return pltpu.CompilerParams(vmem_limit_bytes=VMEM_MAX)


def cost(flops, moved, trans=0):
    return pl.CostEstimate(flops=flops, bytes_accessed=moved, transcendentals=trans)


def norm_rows(rows):
    centered = rows - jnp.mean(rows, axis=1, keepdims=True)
    variance = jnp.mean(centered * centered, axis=1, keepdims=True)
    inverse = lax.rsqrt(variance + EPS)
    return centered * inverse, inverse


def qkv_kernel(tab, tok, mod, gain, cos, sin, w0, w1, first, q, k, v, kt, vt, w, sem):
    heads, block = q.shape[1], q.shape[2]
    step = pl.program_id(0) * pl.num_programs(1) + pl.program_id(1)
    rows = w0.shape[2]

    @pl.when(step == 0)
    def _():
        copies = []
        for p, ref in enumerate((w0, w1)):
            for j in range(4):
                row = pl.multiple_of(tab[p * 4 + j] * rows, 16)
                copies.append(
                    pltpu.make_async_copy(
                        ref.at[j], w.at[:, pl.ds(row, rows), :], sem.at[p * 4 + j]
                    )
                )
        for copy in copies:
            copy.start()
        for copy in copies:
            copy.wait()

    normed, _ = norm_rows(tok[0].astype(F32))
    factor = gain[...] * (1.0 + mod[0, 1:2, :])
    x = (normed * factor + mod[0, 0:1, :]).astype(BF)
    first[0] = x
    wide = w.shape[2]
    low = lax.rem(lax.broadcasted_iota(jnp.int32, (block, wide), 1), HEAD) < HEAD // 2

    def rotate(vec):
        turned = jnp.where(
            low, pltpu.roll(vec, wide - HEAD // 2, 1), pltpu.roll(vec, HEAD // 2, 1)
        )
        return vec * cos[...] + turned * sin[...]

    def store_heads(ref, vec):
        for h in range(heads):
            shifted = vec if h == 0 else pltpu.roll(vec, wide - h * HEAD, 1)
            ref[0, h] = shifted[:, :HEAD].astype(BF)

    query = rotate(jnp.dot(x, w[0], preferred_element_type=F32))
    store_heads(q, query * (HEAD**-0.5))
    key = rotate(jnp.dot(x, w[1], preferred_element_type=F32))
    store_heads(k, key)
    kt[0] = key.T[: heads * HEAD].astype(BF)
    value = jnp.dot(x, w[2], preferred_element_type=F32)
    store_heads(v, value)
    vt[0] = value.T[: heads * HEAD].astype(BF)


def qkv_call(tab, tok_all, mod, gain, cos, sin, w0, w1):
    groups, seq, width = tok_all.shape
    block = seq // 4
    wide = w0.shape[3]
    heads = (wide // HEAD) * 3 // 4
    feats = heads * HEAD
    grid_spec = pltpu.PrefetchScalarGridSpec(
        num_scalar_prefetch=1,
        grid=(groups, 4),
        in_specs=[
            spec((1, block, width), lambda g, j, _: (g, j, 0)),
            spec((1, 6, width), lambda g, j, _: (g, 0, 0)),
            whole((1, width)),
            spec((block, wide), lambda g, j, _: (j, 0)),
            spec((block, wide), lambda g, j, _: (j, 0)),
            ANY,
            ANY,
        ],
        out_specs=[
            spec((1, block, width), lambda g, j, _: (g, j, 0)),
            spec((1, heads, block, HEAD), lambda g, j, _: (g, 0, j, 0)),
            spec((1, heads, block, HEAD), lambda g, j, _: (g, 0, j, 0)),
            spec((1, heads, block, HEAD), lambda g, j, _: (g, 0, j, 0)),
            spec((1, feats, block), lambda g, j, _: (g, 0, j)),
            spec((1, feats, block), lambda g, j, _: (g, 0, j)),
            whole((3, width, wide)),
        ],
        scratch_shapes=[pltpu.SemaphoreType.DMA((8,))],
    )
    head_shape = jax.ShapeDtypeStruct((groups, heads, seq, HEAD), BF)
    turned = jax.ShapeDtypeStruct((groups, feats, seq), BF)
    return pl.pallas_call(
        qkv_kernel,
        grid_spec=grid_spec,
        out_shape=[
            jax.ShapeDtypeStruct((groups, seq, width), BF),
            head_shape,
            head_shape,
            head_shape,
            turned,
            turned,
            jax.ShapeDtypeStruct((3, width, wide), BF),
        ],
        compiler_params=params(),
        cost_estimate=cost(2 * groups * seq * width * wide * 3, 16 * 2**20),
        name="qkv",
    )(tab, tok_all, mod, gain, cos, sin, w0, w1)


def attend_kernel(lens, q, k, vt, mixed, probs, *, group):
    heads, seq = k.shape[1], k.shape[2]
    block = q.shape[2]
    live = lax.broadcasted_iota(jnp.int32, (seq, block), 0) < lens[group]
    for h in range(heads):
        scores = lax.dot_general(k[0, h], q[0, h], NT, preferred_element_type=F32)
        scores = jnp.where(live, scores, MASKED)
        largest = jnp.max(scores, axis=0, keepdims=True)
        weights = jnp.exp(scores - largest)
        total = jnp.sum(weights, axis=0, keepdims=True)
        low = (weights * (1.0 / total)).astype(BF)
        probs[h] = low
        here = slice(h * HEAD, (h + 1) * HEAD)
        mixed[0, here, :] = jnp.dot(vt[0, here, :], low, preferred_element_type=F32).astype(BF)


def attend_call(group, lens, q, k, vt):
    _, heads, seq, _ = q.shape
    block = seq // 4
    feats = heads * HEAD
    grid_spec = pltpu.PrefetchScalarGridSpec(
        num_scalar_prefetch=1,
        grid=(4,),
        in_specs=[
            spec((1, heads, block, HEAD), lambda j, _: (group, 0, j, 0)),
            spec((1, heads, seq, HEAD), lambda j, _: (group, 0, 0, 0)),
            spec((1, feats, seq), lambda j, _: (group, 0, 0)),
        ],
        out_specs=[
            spec((1, feats, block), lambda j, _: (j, 0, 0)),
            spec((heads, seq, block), lambda j, _: (0, 0, j)),
        ],
    )
    return pl.pallas_call(
        functools.partial(attend_kernel, group=group),
        grid_spec=grid_spec,
        out_shape=[
            jax.ShapeDtypeStruct((4, feats, block), BF),
            jax.ShapeDtypeStruct((heads, seq, seq), BF),
        ],
        compiler_params=params(),
        cost_estimate=cost(16 * heads * seq * seq * HEAD, 10 * 2**20, heads * seq * seq),
        name="attend",
    )(lens, q, k, vt)


def attend_back_kernel(q, kt, v, probs, gm, cos, sin, out, dk, dv):
    heads, block = q.shape[1], q.shape[2]
    half = HEAD // 2
    j = pl.program_id(0)

    @pl.when(j == 0)
    def _():
        dk[...] = jnp.zeros_like(dk)
        dv[...] = jnp.zeros_like(dv)

    columns = pl.ds(pl.multiple_of(j * block, 128), block)
    cos_here, sin_here = cos[:, columns], sin[:, columns]

    def store_turned(plane, h, vec, c, s, where):
        low, high = vec[:half], vec[half:]
        base = h * HEAD
        out[plane, base : base + half, where] = (low * c + high * s).astype(BF)
        out[plane, base + half : base + HEAD, where] = (high * c - low * s).astype(BF)

    for h in range(heads):
        here = slice(h * HEAD, (h + 1) * HEAD)
        grad = gm[0, here, :]
        low = probs[h]
        dp = jnp.dot(v[0, h], grad, preferred_element_type=F32)
        soft = low.astype(F32)
        prod = soft * dp
        inner = jnp.sum(prod, axis=0, keepdims=True)
        ds = (prod - soft * inner).astype(BF)
        dv[h] += lax.dot_general(low, grad, NT, preferred_element_type=F32)
        dk[h] += jnp.dot(ds, q[0, h], preferred_element_type=F32)
        dq = jnp.dot(kt[0, here, :], ds, preferred_element_type=F32)
        store_turned(0, h, dq * (HEAD**-0.5), cos_here, sin_here, columns)

    @pl.when(j == pl.num_programs(0) - 1)
    def _():
        for h in range(heads):
            store_turned(1, h, dk[h].T, cos[...], sin[...], slice(None))
            out[2, h * HEAD : (h + 1) * HEAD, :] = dv[h].T.astype(BF)


def attend_back_call(group, q, kt, v, probs, gm, cos, sin):
    _, heads, seq, _ = q.shape
    block = seq // 4
    feats = heads * HEAD
    half = HEAD // 2
    return pl.pallas_call(
        attend_back_kernel,
        grid=(4,),
        in_specs=[
            spec((1, heads, block, HEAD), lambda j: (group, 0, j, 0)),
            spec((1, feats, seq), lambda j: (group, 0, 0)),
            spec((1, heads, seq, HEAD), lambda j: (group, 0, 0, 0)),
            spec((heads, seq, block), lambda j: (0, 0, j)),
            spec((1, feats, block), lambda j: (j, 0, 0)),
            whole((half, seq)),
            whole((half, seq)),
        ],
        out_specs=whole((3, feats, seq)),
        out_shape=jax.ShapeDtypeStruct((3, feats, seq), BF),
        scratch_shapes=[
            pltpu.VMEM((heads, seq, HEAD), F32),
            pltpu.VMEM((heads, seq, HEAD), F32),
        ],
        compiler_params=params(),
        cost_estimate=cost(32 * heads * seq * seq * HEAD, 10 * 2**20),
        name="attend_back",
    )(q, kt, v, probs, gm, cos, sin)


def qkv_back_kernel(tab, gt0, gt1, first, tok, w, fts, ftk, sums, dw, acc):
    i = pl.program_id(0)
    feats, block = gt0.shape[1], gt0.shape[2]
    wide, width = w.shape[2], w.shape[1]
    rows = dw.shape[2]
    g = lax.rem(i, 2)

    @pl.when(i == 0)
    def _():
        acc[...] = jnp.zeros_like(acc)
        sums[...] = jnp.zeros_like(sums)

    total = None
    for j in range(3):
        part = jnp.where(g == 0, gt0[j], gt1[j])
        tall = part.astype(F32)
        if wide > feats:
            tall = jnp.concatenate([tall, jnp.zeros((wide - feats, block), F32)], axis=0)
        term = lax.dot_general(tall.T.astype(BF), w[j], NT, preferred_element_type=F32)
        total = term if total is None else total + term
        acc[j, :feats] += jnp.dot(part, first[0], preferred_element_type=F32)
    normed, _ = norm_rows(tok[0].astype(F32))
    sums[g, 0:1, :] += jnp.sum(total, axis=0, keepdims=True)
    sums[g, 1:2, :] += jnp.sum(total * normed, axis=0, keepdims=True)
    low = total.astype(BF)

    @pl.when(i < 4)
    def _():
        fts[0, 0] = low

    @pl.when(i >= 4)
    def _():
        ftk[0, 0] = low

    @pl.when(i == pl.num_programs(0) - 1)
    def _():
        for j in range(3):
            flat = acc[j].T.astype(BF)
            for b in range(NBLK):
                dw[tab[b], j] = flat[b * rows : (b + 1) * rows]


def qkv_back_call(tab, gt0, gt1, first, tok_all, w):
    _, feats, seq = gt0.shape
    groups = first.shape[0]
    block = seq // 4
    width = first.shape[2]
    wide = w.shape[2]
    rows = width // NBLK

    def piece(i, tab):
        return lax.bitwise_xor(tab[NBLK], lax.rem(i, 4) // 2 * 2 + (1 - i // 4))

    grid_spec = pltpu.PrefetchScalarGridSpec(
        num_scalar_prefetch=1,
        grid=(8,),
        in_specs=[
            spec((3, feats, block), lambda i, tab: (0, 0, piece(i, tab))),
            spec((3, feats, block), lambda i, tab: (0, 0, piece(i, tab))),
            spec((1, block, width), lambda i, tab: (lax.rem(i, 2), piece(i, tab), 0)),
            spec((1, block, width), lambda i, tab: (lax.rem(i, 2), piece(i, tab), 0)),
            whole((3, width, wide)),
        ],
        out_specs=[
            spec(
                (1, 1, block, width),
                lambda i, tab: (jnp.minimum(i, 3) // 2, lax.rem(jnp.minimum(i, 3), 2), 0, 0),
            ),
            spec(
                (1, 1, block, width),
                lambda i, tab: (
                    jnp.maximum(i - 4, 0) // 2,
                    lax.rem(jnp.maximum(i - 4, 0), 2),
                    0,
                    0,
                ),
            ),
            whole((groups, 2, width)),
            whole((NBLK, 3, rows, wide)),
        ],
        scratch_shapes=[pltpu.VMEM((3, wide, width), F32)],
    )
    terms = jax.ShapeDtypeStruct((2, groups, block, width), BF)
    return pl.pallas_call(
        qkv_back_kernel,
        grid_spec=grid_spec,
        out_shape=[
            terms,
            terms,
            jax.ShapeDtypeStruct((groups, 2, width), F32),
            jax.ShapeDtypeStruct((NBLK, 3, rows, wide), BF),
        ],
        compiler_params=params(),
        cost_estimate=cost(4 * groups * seq * width * wide * 3, 16 * 2**20),
        name="qkv_back",
    )(tab, gt0, gt1, first, tok_all, w)


def mlp_kernel(tab, tok, cot, mixed0, mixed1, mod, gain, upb, downb, *rest):
    up_pieces, down_pieces = rest[:8], rest[8:16]
    (
        out,
        gafter,
        gmixed0,
        gmixed1,
        sums,
        upsum,
        gu_s,
        gu_k,
        gd_s,
        gd_k,
        wu,
        wd,
        gu,
        gd,
        after,
        normed,
        inverse,
        second,
        second_t,
        gbr,
        gbr_t,
        att,
        branch,
        gsec,
        act,
        gh,
        sem_u,
        sem_w,
        sem_g,
        sem_d,
    ) = rest[16:]
    mixed, gmixed = (mixed0, mixed1), (gmixed0, gmixed1)
    groups, block, width = tok.shape
    feats = mixed0.shape[1]
    rows = up_pieces[0].shape[1]
    fh = upb.shape[1]
    total_rows = groups * block
    t_part, t_row, t_slot, t_dst = 3, 7, 39, 47

    def loads(sources, target, sem):
        copies = []
        for p in range(8):
            for j in range(4):
                row = pl.multiple_of(tab[t_row + p * 4 + j] * rows, 16)
                copies.append(
                    pltpu.make_async_copy(
                        sources[p].at[j],
                        target.at[tab[t_slot + p], pl.ds(row, rows), :],
                        sem.at[p * 4 + j],
                    )
                )
        return copies

    down_loads = loads(down_pieces, wd, sem_w)
    up_loads = loads(up_pieces, wu, sem_u)
    for load in down_loads + up_loads:
        load.start()
    for load in down_loads:
        load.wait()

    for g in range(groups):
        here = slice(g * block, (g + 1) * block)
        total = jnp.zeros((block, width), F32)
        for k in range(4):
            rows_mixed = mixed[g][tab[t_part + k]].T
            total += lax.dot_general(
                rows_mixed, wd[k, :, fh : fh + feats], NT, preferred_element_type=F32
            )
        att[here, :] = total
        rows_after = tok[g].astype(F32) + mod[g, 2:3, :] * total
        after[here, :] = rows_after
        n, inv = norm_rows(rows_after)
        normed[here, :] = n
        inverse[here, :] = jnp.broadcast_to(inv, (block, 128))
        x = n * (gain[...] * (1.0 + mod[g, 4:5, :])) + mod[g, 3:4, :]
        second[here, :] = x.astype(BF)
        position = tab[2] + lax.broadcasted_iota(jnp.int32, (block, width), 0)
        grad_y = jnp.where(position < tab[g], cot[g].astype(F32), 0.0)
        gb = (mod[g, 5:6, :] * grad_y).astype(BF)
        gbr[here, :] = gb
        sums[g, 4:5, :] = jnp.sum(gb.astype(F32), axis=0, keepdims=True)
        branch[here, :] = jnp.broadcast_to(downb[...], (block, width))
        gsec[here, :] = jnp.zeros((block, width), F32)
    second_t[...] = second[...].T
    gbr_t[...] = gbr[...].T
    for load in up_loads:
        load.wait()

    c1, c3 = math.sqrt(2.0 / math.pi), 0.044715

    def store_grads(k, src, sent, kept, sem):
        for b in range(NBLK):
            there = tab[t_dst + k * NBLK + b]
            piece = src.at[k, pl.ds(b * rows, rows), :]

            @pl.when(k < 2)
            def _():
                pltpu.make_async_copy(piece, kept.at[there], sem.at[k, b]).start()

            @pl.when(k >= 2)
            def _():
                pltpu.make_async_copy(piece, sent.at[there], sem.at[k, b]).start()

    def slot(k, _):
        part = tab[t_part + k]
        bias = upb[pl.ds(part, 1), :]

        hidden = jnp.dot(second[...], wu[k], preferred_element_type=F32) + bias
        square = hidden * hidden
        th = jnp.tanh(c1 * hidden * (1.0 + c3 * square))
        up = 0.5 * (1.0 + th)
        act[...] = (hidden * up).astype(BF)
        slope = up + (0.5 * c1) * hidden * (1.0 - th * th) * (1.0 + (3.0 * c3) * square)
        ga = jnp.dot(gbr[...], wd[k, :, :fh], preferred_element_type=F32)
        grad = (ga * slope).astype(BF)
        gh[...] = grad
        upsum[pl.ds(part, 1), :] = jnp.sum(grad.astype(F32), axis=0, keepdims=True)
        branch[...] += lax.dot_general(
            act[...], wd[k, :, :fh], NT, preferred_element_type=F32
        )
        gsec[...] += lax.dot_general(gh[...], wu[k], NT, preferred_element_type=F32)
        gu[k] = jnp.dot(second_t[...], gh[...], preferred_element_type=F32).astype(BF)
        gd[k, :, :fh] = jnp.dot(gbr_t[...], act[...], preferred_element_type=F32).astype(BF)
        store_grads(k, gu, gu_s, gu_k, sem_g)
        return 0

    lax.fori_loop(0, 4, slot, 0)

    for g in range(groups):
        here = slice(g * block, (g + 1) * block)
        position = tab[2] + lax.broadcasted_iota(jnp.int32, (block, width), 0)
        grad_y = jnp.where(position < tab[g], cot[g].astype(F32), 0.0)
        out[g] = (after[here, :] + mod[g, 5:6, :] * branch[here, :]).astype(BF)
        sums[g, 2:3, :] = jnp.sum(grad_y * branch[here, :], axis=0, keepdims=True)
        n = normed[here, :]
        gs = gsec[here, :]
        sums[g, 0:1, :] = jnp.sum(gs, axis=0, keepdims=True)
        sums[g, 1:2, :] = jnp.sum(gs * n, axis=0, keepdims=True)
        scaled = gs * (gain[...] * (1.0 + mod[g, 4:5, :]))
        mean = jnp.mean(scaled, axis=1, keepdims=True)
        along = jnp.mean(scaled * n, axis=1, keepdims=True)
        grad = grad_y + inverse[here, 0:1] * (scaled - mean - n * along)
        gafter[g] = grad
        sums[g, 3:4, :] = jnp.sum(grad * att[here, :], axis=0, keepdims=True)
        low = (mod[g, 2:3, :] * grad).astype(BF)
        gbr[here, :] = low
        for k in range(4):
            gmixed[g][tab[t_part + k]] = (
                jnp.dot(low, wd[k, :, fh : fh + feats], preferred_element_type=F32)
                .astype(BF)
                .T
            )
    gbr_t[...] = gbr[...].T

    def last(k, _):
        part = tab[t_part + k]
        total = jnp.zeros((width, feats), F32)
        for g in range(groups):
            total += lax.dot_general(
                gbr_t[:, g * block : (g + 1) * block],
                mixed[g][part],
                NT,
                preferred_element_type=F32,
            )
        gd[k, :, fh : fh + feats] = total.astype(BF)
        store_grads(k, gd, gd_s, gd_k, sem_d)
        return 0

    lax.fori_loop(0, 4, last, 0)
    for k in range(4):
        for b in range(NBLK):
            pltpu.make_async_copy(
                gu.at[k, pl.ds(b * rows, rows), :], gu_s.at[0], sem_g.at[k, b]
            ).wait()
            pltpu.make_async_copy(
                gd.at[k, pl.ds(b * rows, rows), :], gd_s.at[0], sem_d.at[k, b]
            ).wait()


def mlp_call(tab, tok, cot, mixed0, mixed1, mod, gain, upb, downb, up_pieces, down_pieces):
    groups, block, width = tok.shape
    feats = mixed0.shape[1]
    fh = upb.shape[1]
    rows = width // NBLK
    total = groups * block
    vm = pl.BlockSpec(memory_space=pltpu.VMEM)
    sm = pl.BlockSpec(memory_space=pltpu.SMEM)
    up = jax.ShapeDtypeStruct((16, rows, fh), BF)
    down = jax.ShapeDtypeStruct((16, rows, fh + feats), BF)
    turned = jax.ShapeDtypeStruct((4, feats, block), BF)
    return pl.pallas_call(
        mlp_kernel,
        in_specs=[sm] + [vm] * 8 + [ANY] * 16,
        out_specs=[vm] * 6 + [ANY] * 4,
        out_shape=[
            jax.ShapeDtypeStruct((groups, block, width), BF),
            jax.ShapeDtypeStruct((groups, block, width), F32),
            turned,
            turned,
            jax.ShapeDtypeStruct((groups, 8, width), F32),
            jax.ShapeDtypeStruct((4, fh), F32),
            up,
            up,
            down,
            down,
        ],
        scratch_shapes=[
            pltpu.VMEM((4, width, fh), BF),
            pltpu.VMEM((4, width, fh + feats), BF),
            pltpu.VMEM((4, width, fh), BF),
            pltpu.VMEM((4, width, fh + feats), BF),
            pltpu.VMEM((total, width), F32),
            pltpu.VMEM((total, width), F32),
            pltpu.VMEM((total, 128), F32),
            pltpu.VMEM((total, width), BF),
            pltpu.VMEM((width, total), BF),
            pltpu.VMEM((total, width), BF),
            pltpu.VMEM((width, total), BF),
            pltpu.VMEM((total, width), F32),
            pltpu.VMEM((total, width), F32),
            pltpu.VMEM((total, width), F32),
            pltpu.VMEM((total, fh), BF),
            pltpu.VMEM((total, fh), BF),
            pltpu.SemaphoreType.DMA((32,)),
            pltpu.SemaphoreType.DMA((32,)),
            pltpu.SemaphoreType.DMA((4, NBLK)),
            pltpu.SemaphoreType.DMA((4, NBLK)),
        ],
        compiler_params=params(),
        cost_estimate=cost(12 * total * width * fh * 4, 28 * 2**20, total * fh * 4),
        name="mlp",
    )(tab, tok, cot, mixed0, mixed1, mod, gain, upb, downb, *up_pieces, *down_pieces)


def norm_back_kernel(t0, t1, t2, tok, after, mod, gain, out):
    normed, inverse = norm_rows(tok[0].astype(F32))
    grad = t0[0, 0].astype(F32) + t1[0, 0].astype(F32) + t2[0].astype(F32)
    scaled = grad * (gain[...] * (1.0 + mod[0, 1:2, :]))
    mean = jnp.mean(scaled, axis=1, keepdims=True)
    along = jnp.mean(scaled * normed, axis=1, keepdims=True)
    out[0] = (after[0] + inverse * (scaled - mean - normed * along)).astype(BF)


def norm_back_call(t0, t1, t2, tok, after, mod, gain):
    groups, block, width = tok.shape
    row = spec((1, block, width), lambda g: (g, 0, 0))
    near = spec((1, 1, block, width), lambda g: (0, g, 0, 0))
    return pl.pallas_call(
        norm_back_kernel,
        grid=(groups,),
        in_specs=[near, near, row, row, row, spec((1, 6, width), lambda g: (g, 0, 0)), whole((1, width))],
        out_specs=row,
        out_shape=jax.ShapeDtypeStruct((groups, block, width), BF),
        compiler_params=params(),
        cost_estimate=cost(40 * groups * block * width, 12 * groups * block * width),
        name="norm_back",
    )(t0, t1, t2, tok, after, mod, gain)


AT = 640


def small_kernel(got, cond_t, adaw, adab, upb, downb, gain_one, gain_two):
    dp = got.shape[0]
    cols = adaw.shape[1]
    total = jnp.sum(got[...], axis=1)
    mods = jnp.concatenate([total[:, 0, :], total[:, 1, :]], axis=0)
    product = jnp.dot(
        cond_t[...], mods, precision=lax.Precision.HIGHEST, preferred_element_type=F32
    )
    adaw[...] = product[:, :cols]
    flat = jnp.sum(total, axis=0)
    adab[...] = flat[0:1, :cols] + flat[1:2, :cols]
    upb[...] = flat[2:3, : upb.shape[1]]
    for row, ref in enumerate((downb, gain_one, gain_two)):
        ref[...] = flat[row : row + 1, AT : AT + ref.shape[1]]


def small_call(got, cond_t, cols, up_count, count):
    shapes = [(cond_t.shape[0], cols), (1, cols), (1, up_count)] + [(1, count)] * 3
    vm = pl.BlockSpec(memory_space=pltpu.VMEM)
    return pl.pallas_call(
        small_kernel,
        in_specs=[vm, vm],
        out_specs=[vm] * 6,
        out_shape=[jax.ShapeDtypeStruct(shape, F32) for shape in shapes],
        compiler_params=params(),
        cost_estimate=cost(2**20, 2**20),
        name="small",
    )(got, cond_t)


def time_embedding(time_steps, width_total):
    half_width = width_total // 2
    frequency = jnp.exp(-math.log(10000.0) * jnp.arange(half_width, dtype=F32) / half_width)
    angles = time_steps.astype(F32)[:, None] * frequency[None, :]
    return jnp.concatenate([jnp.cos(angles), jnp.sin(angles)], axis=-1)


def rotary_halves(length_total):
    half = HEAD // 2
    inverse = jnp.exp(-math.log(10000.0) * 2.0 * jnp.arange(half, dtype=F32) / HEAD)
    angles = jnp.arange(length_total, dtype=F32)[:, None] * inverse[None, :]
    return jnp.cos(angles), jnp.sin(angles)


def device_index(z, y, x, c):
    return ((z * 2 + y) * 2 + x) * 2 + c


def permutation(move):
    pairs = []
    for z in range(4):
        for y in range(2):
            for x in range(2):
                for c in range(2):
                    pairs.append((device_index(z, y, x, c), device_index(*move(z, y, x, c))))
    return pairs


CORE = permutation(lambda z, y, x, c: (z, y, x, 1 - c))
FLIP_X = permutation(lambda z, y, x, c: (z, y, 1 - x, c))
FLIP_Y = permutation(lambda z, y, x, c: (z, 1 - y, x, c))
FIRST = permutation(lambda z, y, x, c: (z, 1 - y, x, c) if c == 0 else (z, y, 1 - x, c))
SECOND = permutation(lambda z, y, x, c: (z, y, 1 - x, c) if c == 0 else (z, 1 - y, x, c))
ALONG_Z = [permutation(lambda z, y, x, c, s=s: ((z + s) % 4, y, x, c)) for s in range(4)]


def send(array, pairs):
    return lax.ppermute(array, ("dp", "tensor"), pairs)


def start_z(shard):
    return [shard] + [send(shard, ALONG_Z[s]) for s in (1, 2, 3)]


def gather_z(shard):
    return jnp.stack(start_z(shard))


def after_all(value, *others):
    flat, tree = jax.tree.flatten(value)
    tied = lax.optimization_barrier((tuple(flat), others))[0]
    return jax.tree.unflatten(tree, tied)


def add_low(*terms):
    return functools.reduce(jnp.add, [term.astype(F32) for term in terms]).astype(BF)


class Reduce:
    def __init__(self, sent, kept):
        shape = (2, 2, 4) + sent.shape[1:]
        self.kept = kept.reshape(shape)
        self.got = send(sent, CORE).reshape(shape)

    def one(self):
        self.half = add_low(self.kept[1], self.got[1])
        return self.half

    def two(self):
        self.got_two = send(self.half, SECOND)
        self.quarter = add_low(self.kept[0, 1], self.got[0, 1], self.got_two[1])
        return self.quarter

    def three(self):
        got_three = send(self.quarter, FIRST)
        self.parts = [
            add_low(self.kept[0, 0, s], self.got[0, 0, s], self.got_two[0, s], got_three[s])
            for s in range(4)
        ]
        return self.parts

    def last(self, *others):
        got = [send(self.parts[s], ALONG_Z[s]) for s in (1, 2, 3)]
        if others:
            got = after_all(got, *others)
        return functools.reduce(jnp.add, [g.astype(F32) for g in [self.parts[0]] + got])


def tables(z, y, x, c):
    far_core = np.array([0, 0, 0, 0, 1, 1, 1, 1])
    kind = np.array([0, 1, 2, 3] * 2)
    core = jnp.bitwise_xor(c, far_core)
    rel_x = jnp.where(kind == 0, 0, jnp.where(kind == 3, 1, jnp.where(kind == 1, core, 1 - core)))
    rel_y = jnp.where(kind == 0, 0, jnp.where(kind == 3, 1, jnp.where(kind == 1, 1 - core, core)))
    slots = far_core * 2 + rel_x
    back = np.arange(4)
    from_z = jnp.remainder(z - back, 4)
    weight_rows = (from_z[None, :] * 2 + jnp.bitwise_xor(y, rel_y)[:, None]).reshape(32)
    slot = np.arange(4)
    parts = jnp.bitwise_xor(x, slot % 2) * 2 + jnp.bitwise_xor(c, slot // 2)
    block = np.arange(NBLK)
    to_z = jnp.remainder(block // 2 - z, 4)
    to_y = jnp.bitwise_xor(block % 2, y)
    slot_core = jnp.bitwise_xor(c, slot // 2)[:, None]
    to_x = (slot % 2)[:, None]
    major = jnp.where(slot_core == 0, to_x, to_y[None, :])
    minor = jnp.where(slot_core == 0, to_y[None, :], to_x)
    targets = (major * 8 + minor * 4 + to_z[None, :]).reshape(4 * NBLK)
    qkv_rows = jnp.concatenate(
        [from_z * 2 + y, from_z * 2 + (1 - y)]
    )
    qkv_targets = to_y * 4 + to_z
    return parts, weight_rows, slots, targets, qkv_rows, qkv_targets


def shards(
    tokens,
    lengths,
    times,
    cotangent,
    w_qkv,
    w_out,
    w_up,
    up_bias,
    w_down,
    down_bias,
    norm1_gain,
    norm2_gain,
    ada_weight,
    ada_bias,
):
    groups, block, width = tokens.shape
    dp, tp = lax.axis_size("dp"), lax.axis_size("tensor")
    seq = block * tp
    t = lax.axis_index("tensor")
    d = lax.axis_index("dp")
    fast = dp == 8 and tp == 4
    feats = w_qkv.shape[2]
    fh = w_up.shape[1]
    rows = width // NBLK
    zero = jnp.zeros((), jnp.int32)
    z, y, x, c = (d // 2, d % 2, t // 2, t % 2) if fast else (zero, zero, zero, zero)
    here = t if fast else zero
    parts, weight_rows, slots, targets, qkv_rows, qkv_targets = tables(z, y, x, c)

    all_times = lax.all_to_all(
        jnp.broadcast_to(times[None, :], (dp, groups)), "dp", 0, 0, tiled=True
    ).reshape(-1)
    pad = (-feats) % 128
    qkv_shard = jnp.pad(w_qkv, ((0, 0), (0, 0), (0, pad)))
    if fast:
        near = gather_z(qkv_shard)
        qkv_pieces = (near, send(near, FLIP_Y))
    else:
        full = lax.all_gather(qkv_shard, "dp", axis=1, tiled=True)
        full = full.reshape(3, NBLK, rows, feats + pad).transpose(1, 0, 2, 3)
        order = [[(-j) % 4 * 2 + p for j in range(4)] for p in range(2)]
        qkv_pieces = tuple(jnp.stack([full[b] for b in order[p]]) for p in range(2))
    tok_all = lax.all_gather(tokens, "tensor", axis=1, tiled=True)

    condition = time_embedding(all_times, ada_weight.shape[0])
    part = jnp.dot(
        condition, ada_weight.astype(F32), precision=lax.Precision.HIGHEST
    ) + ada_bias.astype(F32)
    cols = part.shape[1]
    vectors = jnp.concatenate([up_bias, down_bias, norm1_gain, norm2_gain]).astype(F32)
    sent_mod = jnp.concatenate(
        [
            part.reshape(dp, groups * cols),
            jnp.broadcast_to(vectors[None, :], (dp, vectors.shape[0])),
        ],
        axis=1,
    )
    payload = lax.all_to_all(sent_mod, "dp", 0, 0, tiled=True)
    mod = (
        payload[:, : groups * cols]
        .reshape(dp, groups, cols)
        .transpose(1, 0, 2)
        .reshape(groups, 6, width)
    )
    at = groups * cols
    small = []
    for count in (up_bias.shape[0], down_bias.shape[0], norm1_gain.shape[0], norm2_gain.shape[0]):
        small.append(payload[:, at : at + count].reshape(-1))
        at += count
    upb_all = small[0].reshape(tp, fh)
    downb_all, gain_one, gain_two = (v.reshape(1, width) for v in small[1:])

    up_shard = w_up
    down_shard = jnp.concatenate([w_down.T, w_out.T], axis=1)
    if fast:
        up_shard, down_shard = after_all((up_shard, down_shard), qkv_pieces[1], payload)
        up_parts = start_z(up_shard)
        down_parts = start_z(down_shard)
    else:

        def gather_pieces(shard):
            full = lax.all_gather(shard, "dp", axis=0, tiled=True)
            full = lax.all_gather(full, "tensor", axis=0, tiled=False)
            full = full.reshape(tp, NBLK, rows, full.shape[2])
            return [
                jnp.stack([full[rel_x * 2 + far, b] for b in order[rel_y]])
                for far in range(2)
                for rel_x, rel_y in ((0, 0), (far, 1 - far), (1 - far, far), (1, 1))
            ]

    cos, sin = rotary_halves(seq)
    heads_wide = (feats + pad) // HEAD
    cos_wide = jnp.tile(jnp.concatenate([cos, cos], axis=1), (1, heads_wide))
    sin_wide = jnp.tile(jnp.concatenate([-sin, sin], axis=1), (1, heads_wide))
    first_all, q, k, v, kt, vt, w_all = qkv_call(
        qkv_rows.astype(jnp.int32), tok_all, mod, gain_one, cos_wide, sin_wide, *qkv_pieces
    )
    vt_later = vt
    if fast:
        up_near = jnp.stack(after_all(up_parts, vt))
        vt = after_all(vt, up_near)
        up_one, up_two = send(up_near, FIRST), send(up_near, SECOND)
    mixed0, probs0 = attend_call(0, lengths, q, k, vt)
    mixed0_all = lax.all_to_all(mixed0, "tensor", 0, 0, tiled=True)
    if fast:
        down_near = jnp.stack(after_all(down_parts, mixed0))
        up_near, up_one, up_two = after_all((up_near, up_one, up_two), mixed0)
        vt_later = after_all(vt, down_near, up_one, up_two)
        up_both = send(up_one, SECOND)
        own = (up_near, up_one, up_two, up_both)
        down_one, down_two = send(down_near, FIRST), send(down_near, SECOND)
    mixed1, probs1 = attend_call(1, lengths, q, k, vt_later)
    if fast:
        down_near, down_one, down_two = after_all((down_near, down_one, down_two), mixed1)
    mixed1_all = lax.all_to_all(after_all(mixed1, mixed0_all), "tensor", 0, 0, tiled=True)
    if fast:
        down_both = send(down_one, SECOND)
        up_pieces = own + tuple(send(piece, CORE) for piece in own)
        own = (down_near, down_one, down_two, down_both)
        down_pieces = own + tuple(send(piece, CORE) for piece in own)
    else:
        up_pieces, down_pieces = gather_pieces(up_shard), gather_pieces(down_shard)

    tab = jnp.concatenate(
        [
            lengths,
            (t * block).reshape(1),
            parts,
            weight_rows,
            slots,
            targets,
        ]
    ).astype(jnp.int32)
    out, grad_after, gm0, gm1, sums, upsum, gu_s, gu_k, gd_s, gd_k = mlp_call(
        tab,
        tokens,
        cotangent,
        mixed0_all,
        mixed1_all,
        mod,
        gain_two,
        upb_all,
        downb_all,
        up_pieces,
        down_pieces,
    )
    gm0 = lax.all_to_all(gm0, "tensor", 0, 0, tiled=True)
    gm1 = lax.all_to_all(after_all(gm1, gm0), "tensor", 0, 0, tiled=True)
    if fast:
        up_sum = Reduce(gu_s, gu_k)
        down_sum = Reduce(after_all(gd_s, up_sum.got), gd_k)
        up_sum.got = after_all(up_sum.got, gm0)
        gm0 = after_all(gm0, up_sum.one())
    grad_t0 = attend_back_call(0, q, kt, v, probs0, gm0, cos.T, sin.T)
    if fast:
        gm1 = after_all(gm1, grad_t0, up_sum.two(), down_sum.one())
    grad_t1 = attend_back_call(1, q, kt, v, probs1, gm1, cos.T, sin.T)
    if fast:
        grad_t1 = after_all(grad_t1, down_sum.two(), *up_sum.three())
    fts, ftk, sums_one, dw = qkv_back_call(
        jnp.concatenate([qkv_targets, here.reshape(1)]).astype(jnp.int32),
        grad_t0,
        grad_t1,
        first_all,
        tok_all,
        w_all,
    )

    if fast:
        sum_up = up_sum.last()
        got = send(fts, CORE)
        far = send(add_low(ftk[1], got[1]), FLIP_X)
        grad_in = norm_back_call(ftk, got, far, tokens, grad_after, mod, gain_one)
        got_dw = send(dw[4:], FLIP_Y)
        dw_parts = [add_low(dw[s], got_dw[s]) for s in range(4)]
        last_parts = down_sum.three()
        sum_down = down_sum.last(grad_in)
        sum_qkv = functools.reduce(
            jnp.add,
            [dw_parts[0].astype(F32)]
            + [send(dw_parts[s], ALONG_Z[s]).astype(F32) for s in (1, 2, 3)],
        )
        ready = last_parts[0][:8, :128].astype(F32)
    else:

        def absolute(sent, kept):
            lanes = sent.shape[2]
            near = kept.reshape(2, 2, 4, rows, lanes)
            far = sent.reshape(2, 2, 4, rows, lanes).transpose(1, 0, 2, 3, 4)
            both = jnp.stack([near, far], axis=1)
            return both.transpose(0, 1, 3, 2, 4, 5).reshape(tp, width, lanes).astype(F32)

        def reduce_all(sent, kept):
            terms = lax.psum_scatter(
                absolute(sent, kept), "tensor", scatter_dimension=0, tiled=True
            )[0]
            return lax.psum_scatter(terms, "dp", scatter_dimension=0, tiled=True)

        sum_up = reduce_all(gu_s, gu_k)
        sum_down = reduce_all(gd_s, gd_k)
        terms = dw.reshape(2, 4, 3, rows, feats + pad).transpose(2, 1, 0, 3, 4)
        terms = terms.reshape(3, width, feats + pad).astype(F32)
        sum_qkv = lax.psum_scatter(terms, "dp", scatter_dimension=1, tiled=True)
        terms = jnp.stack([ftk, fts], axis=1).reshape(tp, groups, block, width).astype(F32)
        grad_first = lax.psum_scatter(terms, "tensor", scatter_dimension=0, tiled=True)[0]
        nought = jnp.zeros_like(grad_first)
        grad_in = norm_back_call(
            grad_first[None], nought[None], nought, tokens, grad_after, mod, gain_one
        )
        ready = sum_up

    q_one, q_two = sums_one[:, 1], sums[:, 1]
    grad_mod = jnp.stack(
        [sums_one[:, 0], gain_one * q_one, sums[:, 3], sums[:, 0], gain_two * q_two, sums[:, 2]],
        axis=1,
    )
    grad_mod = grad_mod.reshape(groups, dp, cols).transpose(1, 0, 2)
    up_count, count = up_bias.shape[0], down_bias.shape[0]
    firsts = jnp.concatenate(
        [
            jnp.pad(grad_mod, ((0, 0), (0, 0), (0, AT - cols))),
            jnp.pad(upsum.reshape(dp, 1, up_count), ((0, 0), (0, 0), (0, AT - up_count))),
        ],
        axis=1,
    )
    seconds = jnp.stack(
        [
            jnp.sum(sums[:, 4], axis=0),
            jnp.sum((1.0 + mod[:, 1]) * q_one, axis=0),
            jnp.sum((1.0 + mod[:, 4]) * q_two, axis=0),
        ]
    )
    seconds = seconds.reshape(3, dp, count).transpose(1, 0, 2)
    seconds = jnp.pad(seconds, ((0, 0), (0, 0), (0, width - AT - count)))
    payload = jnp.concatenate([firsts, seconds], axis=2)
    payload = jnp.broadcast_to(payload[:, None], (dp, tp, 3, width)).reshape(dp * tp, 3, width)
    payload = after_all(payload, ready)
    payload = lax.all_to_all(payload, ("dp", "tensor"), 0, 0, tiled=True)
    cond_t = condition.reshape(dp, groups, -1).transpose(2, 1, 0).reshape(-1, dp * groups)
    grad_adaw, grad_adab, g_up, g_down, g_one, g_two = small_call(
        payload.reshape(dp, tp, 3, width), cond_t, cols, up_count, count
    )

    return (
        out,
        grad_in,
        sum_qkv[:, :, :feats],
        sum_down[:, fh:].T,
        sum_up,
        g_up[0],
        sum_down[:, :fh].T,
        g_down[0],
        g_one[0],
        g_two[0],
        grad_adaw,
        grad_adab[0],
    )


def solution(mesh):
    in_specs = (
        P("dp", "tensor", None),
        P("dp"),
        P("dp"),
        P("dp", "tensor", None),
        P(None, "dp", "tensor"),
        P("tensor", "dp"),
        P("dp", "tensor"),
        P("dp"),
        P("tensor", "dp"),
        P("dp"),
        P("dp"),
        P("dp"),
        P(None, "dp"),
        P("dp"),
    )
    out_specs = (
        P("dp", "tensor", None),
        P("dp", "tensor", None),
        P(None, "dp", "tensor"),
        P("tensor", "dp"),
        P("dp", "tensor"),
        P("dp"),
        P("tensor", "dp"),
        P("dp"),
        P("dp"),
        P("dp"),
        P(None, "dp"),
        P("dp"),
    )
    return jax.shard_map(shards, mesh=mesh, in_specs=in_specs, out_specs=out_specs, check_vma=False)
```

```python
import functools
import math

import jax
import jax.numpy as jnp
import numpy as np
from jax import lax
from jax.experimental import pallas as pl
from jax.experimental.pallas import tpu as pltpu
from jax.sharding import PartitionSpec as P

HEAD = 64
EPS = 1e-05
MASKED = -1e30
BF = jnp.bfloat16
F32 = jnp.float32
VMEM_MAX = 60 * 1024 * 1024
NBLK = 8
NT = (((1,), (1,)), ((), ()))


def spec(block, index_map):
    return pl.BlockSpec(block, index_map)


def whole(shape):
    return pl.BlockSpec(shape, lambda *_: (0,) * len(shape))


ANY = pl.BlockSpec(memory_space=pl.ANY)


def params():
    return pltpu.CompilerParams(vmem_limit_bytes=VMEM_MAX)


def cost(flops, moved, trans=0):
    return pl.CostEstimate(flops=flops, bytes_accessed=moved, transcendentals=trans)


def norm_rows(rows):
    centered = rows - jnp.mean(rows, axis=1, keepdims=True)
    variance = jnp.mean(centered * centered, axis=1, keepdims=True)
    inverse = lax.rsqrt(variance + EPS)
    return centered * inverse, inverse


def qkv_kernel(tab, tok, mod, gain, cos, sin, w0, w1, first, q, k, v, kt, vt, w, sem):
    heads, block = q.shape[1], q.shape[2]
    step = pl.program_id(0) * pl.num_programs(1) + pl.program_id(1)
    rows = w0.shape[2]

    @pl.when(step == 0)
    def _():
        copies = []
        for p, ref in enumerate((w0, w1)):
            for j in range(4):
                row = pl.multiple_of(tab[p * 4 + j] * rows, 16)
                copies.append(
                    pltpu.make_async_copy(
                        ref.at[j], w.at[:, pl.ds(row, rows), :], sem.at[p * 4 + j]
                    )
                )
        for copy in copies:
            copy.start()
        for copy in copies:
            copy.wait()

    normed, _ = norm_rows(tok[0].astype(F32))
    factor = gain[...] * (1.0 + mod[0, 1:2, :])
    x = (normed * factor + mod[0, 0:1, :]).astype(BF)
    first[0] = x
    wide = w.shape[2]
    low = lax.rem(lax.broadcasted_iota(jnp.int32, (block, wide), 1), HEAD) < HEAD // 2

    def rotate(vec):
        turned = jnp.where(
            low, pltpu.roll(vec, wide - HEAD // 2, 1), pltpu.roll(vec, HEAD // 2, 1)
        )
        return vec * cos[...] + turned * sin[...]

    def store_heads(ref, vec):
        for h in range(heads):
            shifted = vec if h == 0 else pltpu.roll(vec, wide - h * HEAD, 1)
            ref[0, h] = shifted[:, :HEAD].astype(BF)

    query = rotate(jnp.dot(x, w[0], preferred_element_type=F32))
    store_heads(q, query * (HEAD**-0.5))
    key = rotate(jnp.dot(x, w[1], preferred_element_type=F32))
    store_heads(k, key)
    kt[0] = key.T[: heads * HEAD].astype(BF)
    value = jnp.dot(x, w[2], preferred_element_type=F32)
    store_heads(v, value)
    vt[0] = value.T[: heads * HEAD].astype(BF)


def qkv_call(tab, tok_all, mod, gain, cos, sin, w0, w1):
    groups, seq, width = tok_all.shape
    block = seq // 4
    wide = w0.shape[3]
    heads = (wide // HEAD) * 3 // 4
    feats = heads * HEAD
    grid_spec = pltpu.PrefetchScalarGridSpec(
        num_scalar_prefetch=1,
        grid=(groups, 4),
        in_specs=[
            spec((1, block, width), lambda g, j, _: (g, j, 0)),
            spec((1, 6, width), lambda g, j, _: (g, 0, 0)),
            whole((1, width)),
            spec((block, wide), lambda g, j, _: (j, 0)),
            spec((block, wide), lambda g, j, _: (j, 0)),
            ANY,
            ANY,
        ],
        out_specs=[
            spec((1, block, width), lambda g, j, _: (g, j, 0)),
            spec((1, heads, block, HEAD), lambda g, j, _: (g, 0, j, 0)),
            spec((1, heads, block, HEAD), lambda g, j, _: (g, 0, j, 0)),
            spec((1, heads, block, HEAD), lambda g, j, _: (g, 0, j, 0)),
            spec((1, feats, block), lambda g, j, _: (g, 0, j)),
            spec((1, feats, block), lambda g, j, _: (g, 0, j)),
            whole((3, width, wide)),
        ],
        scratch_shapes=[pltpu.SemaphoreType.DMA((8,))],
    )
    head_shape = jax.ShapeDtypeStruct((groups, heads, seq, HEAD), BF)
    turned = jax.ShapeDtypeStruct((groups, feats, seq), BF)
    return pl.pallas_call(
        qkv_kernel,
        grid_spec=grid_spec,
        out_shape=[
            jax.ShapeDtypeStruct((groups, seq, width), BF),
            head_shape,
            head_shape,
            head_shape,
            turned,
            turned,
            jax.ShapeDtypeStruct((3, width, wide), BF),
        ],
        compiler_params=params(),
        cost_estimate=cost(2 * groups * seq * width * wide * 3, 16 * 2**20),
        name="qkv",
    )(tab, tok_all, mod, gain, cos, sin, w0, w1)


def attend_kernel(tab, q, k, vt, mix0, mix1, mix2, mix3, probs, *, group):
    heads, seq = k.shape[1], k.shape[2]
    block = q.shape[2]
    live = lax.broadcasted_iota(jnp.int32, (seq, block), 0) < tab[group]
    parts = []
    for h in range(heads):
        scores = lax.dot_general(k[0, h], q[0, h], NT, preferred_element_type=F32)
        scores = jnp.where(live, scores, MASKED)
        largest = jnp.max(scores, axis=0, keepdims=True)
        weights = jnp.exp(scores - largest)
        total = jnp.sum(weights, axis=0, keepdims=True)
        low = (weights * (1.0 / total)).astype(BF)
        probs[h] = low
        here = slice(h * HEAD, (h + 1) * HEAD)
        parts.append(jnp.dot(vt[0, here, :], low, preferred_element_type=F32).astype(BF))
    for r, ref in enumerate((mix0, mix1, mix2, mix3)):

        @pl.when(turn(pl.program_id(0)) == r)
        def _():
            for h in range(heads):
                ref[h * HEAD : (h + 1) * HEAD, :] = parts[h]


def turn(step):
    return lax.rem(step + 1, 4)


def attend_call(group, tab, q, k, vt):
    _, heads, seq, _ = q.shape
    block = seq // 4
    feats = heads * HEAD

    def piece(i, tab):
        return lax.bitwise_xor(tab[2], turn(i))

    grid_spec = pltpu.PrefetchScalarGridSpec(
        num_scalar_prefetch=1,
        grid=(4,),
        in_specs=[
            spec((1, heads, block, HEAD), lambda i, tab: (group, 0, piece(i, tab), 0)),
            spec((1, heads, seq, HEAD), lambda i, tab: (group, 0, 0, 0)),
            spec((1, feats, seq), lambda i, tab: (group, 0, 0)),
        ],
        out_specs=[
            *[whole((feats, block))] * 4,
            spec((heads, seq, block), lambda i, tab: (0, 0, piece(i, tab))),
        ],
    )
    return pl.pallas_call(
        functools.partial(attend_kernel, group=group),
        grid_spec=grid_spec,
        out_shape=[
            *[jax.ShapeDtypeStruct((feats, block), BF)] * 4,
            jax.ShapeDtypeStruct((heads, seq, seq), BF),
        ],
        compiler_params=params(),
        cost_estimate=cost(16 * heads * seq * seq * HEAD, 10 * 2**20, heads * seq * seq),
        name="attend",
    )(tab, q, k, vt)


def attend_back_kernel(tab, q, kt, v, probs, gm0, gm1, gm2, gm3, cos, sin, out, dk, dv, gm):
    heads, block = q.shape[1], q.shape[2]
    half = HEAD // 2
    step = pl.program_id(0)
    j = lax.bitwise_xor(tab[0], step)

    @pl.when(step == 0)
    def _():
        dk[...] = jnp.zeros_like(dk)
        dv[...] = jnp.zeros_like(dv)
        for r, ref in enumerate((gm0, gm1, gm2, gm3)):
            gm[r] = ref[...]

    columns = pl.ds(pl.multiple_of(j * block, 128), block)
    cos_here, sin_here = cos[:, columns], sin[:, columns]

    def store_turned(plane, h, vec, c, s, where):
        low, high = vec[:half], vec[half:]
        base = h * HEAD
        out[plane, base : base + half, where] = (low * c + high * s).astype(BF)
        out[plane, base + half : base + HEAD, where] = (high * c - low * s).astype(BF)

    for h in range(heads):
        here = slice(h * HEAD, (h + 1) * HEAD)
        grad = gm[step, here, :]
        low = probs[h]
        dp = jnp.dot(v[0, h], grad, preferred_element_type=F32)
        soft = low.astype(F32)
        prod = soft * dp
        inner = jnp.sum(prod, axis=0, keepdims=True)
        ds = (prod - soft * inner).astype(BF)
        dv[h] += lax.dot_general(low, grad, NT, preferred_element_type=F32)
        dk[h] += jnp.dot(ds, q[0, h], preferred_element_type=F32)
        dq = jnp.dot(kt[0, here, :], ds, preferred_element_type=F32)
        store_turned(0, h, dq * (HEAD**-0.5), cos_here, sin_here, columns)

    @pl.when(step == pl.num_programs(0) - 1)
    def _():
        for h in range(heads):
            store_turned(1, h, dk[h].T, cos[...], sin[...], slice(None))
            out[2, h * HEAD : (h + 1) * HEAD, :] = dv[h].T.astype(BF)


def attend_back_call(group, tab, q, kt, v, probs, gm, cos, sin):
    _, heads, seq, _ = q.shape
    block = seq // 4
    feats = heads * HEAD
    half = HEAD // 2

    def piece(i, tab):
        return lax.bitwise_xor(tab[0], i)

    grid_spec = pltpu.PrefetchScalarGridSpec(
        num_scalar_prefetch=1,
        grid=(4,),
        in_specs=[
            spec((1, heads, block, HEAD), lambda i, tab: (group, 0, piece(i, tab), 0)),
            spec((1, feats, seq), lambda i, tab: (group, 0, 0)),
            spec((1, heads, seq, HEAD), lambda i, tab: (group, 0, 0, 0)),
            spec((heads, seq, block), lambda i, tab: (0, 0, piece(i, tab))),
            *[spec((feats, block), lambda i, tab: (0, group))] * 4,
            whole((half, seq)),
            whole((half, seq)),
        ],
        out_specs=whole((3, feats, seq)),
        scratch_shapes=[
            pltpu.VMEM((heads, seq, HEAD), F32),
            pltpu.VMEM((heads, seq, HEAD), F32),
            pltpu.VMEM((4, feats, block), BF),
        ],
    )
    return pl.pallas_call(
        attend_back_kernel,
        grid_spec=grid_spec,
        out_shape=jax.ShapeDtypeStruct((3, feats, seq), BF),
        compiler_params=params(),
        cost_estimate=cost(32 * heads * seq * seq * HEAD, 10 * 2**20),
        name="attend_back",
    )(tab, q, kt, v, probs, *gm, cos, sin)


def qkv_back_kernel(tab, gt0, gt1, first, tok, w, fts, ftk, sums, dws, dwk, acc):
    i = pl.program_id(0)
    feats, block = gt0.shape[1], gt0.shape[2]
    wide, width = w.shape[2], w.shape[1]
    rows = dws.shape[2]
    g = lax.rem(i, 2)

    @pl.when(i == 0)
    def _():
        acc[...] = jnp.zeros_like(acc)
        sums[...] = jnp.zeros_like(sums)

    total = None
    for j in range(3):
        part = jnp.where(g == 0, gt0[j], gt1[j])
        tall = part.astype(F32)
        if wide > feats:
            tall = jnp.concatenate([tall, jnp.zeros((wide - feats, block), F32)], axis=0)
        term = lax.dot_general(tall.T.astype(BF), w[j], NT, preferred_element_type=F32)
        total = term if total is None else total + term
        acc[j, :feats] += jnp.dot(part, first[0], preferred_element_type=F32)
    normed, _ = norm_rows(tok[0].astype(F32))
    sums[g, 0:1, :] += jnp.sum(total, axis=0, keepdims=True)
    sums[g, 1:2, :] += jnp.sum(total * normed, axis=0, keepdims=True)
    low = total.astype(BF)

    @pl.when(i < 4)
    def _():
        fts[0, 0] = low

    @pl.when(i >= 4)
    def _():
        ftk[0, 0] = low

    @pl.when(i == pl.num_programs(0) - 1)
    def _():
        for j in range(3):
            flat = acc[j].T.astype(BF)
            for b in range(NBLK):
                part = flat[b * rows : (b + 1) * rows]
                there = tab[b]

                @pl.when(there < NBLK // 2)
                def _():
                    dwk[there, j] = part

                @pl.when(there >= NBLK // 2)
                def _():
                    dws[there - NBLK // 2, j] = part


def qkv_back_call(tab, gt0, gt1, first, tok_all, w):
    _, feats, seq = gt0.shape
    groups = first.shape[0]
    block = seq // 4
    width = first.shape[2]
    wide = w.shape[2]
    rows = width // NBLK

    def piece(i, tab):
        return lax.bitwise_xor(tab[NBLK], lax.rem(i, 4) // 2 * 2 + (1 - i // 4))

    grid_spec = pltpu.PrefetchScalarGridSpec(
        num_scalar_prefetch=1,
        grid=(8,),
        in_specs=[
            spec((3, feats, block), lambda i, tab: (0, 0, piece(i, tab))),
            spec((3, feats, block), lambda i, tab: (0, 0, piece(i, tab))),
            spec((1, block, width), lambda i, tab: (lax.rem(i, 2), piece(i, tab), 0)),
            spec((1, block, width), lambda i, tab: (lax.rem(i, 2), piece(i, tab), 0)),
            whole((3, width, wide)),
        ],
        out_specs=[
            spec(
                (1, 1, block, width),
                lambda i, tab: (jnp.minimum(i, 3) // 2, lax.rem(jnp.minimum(i, 3), 2), 0, 0),
            ),
            spec(
                (1, 1, block, width),
                lambda i, tab: (
                    jnp.maximum(i - 4, 0) // 2,
                    lax.rem(jnp.maximum(i - 4, 0), 2),
                    0,
                    0,
                ),
            ),
            whole((groups, 2, width)),
            whole((NBLK // 2, 3, rows, wide)),
            whole((NBLK // 2, 3, rows, wide)),
        ],
        scratch_shapes=[pltpu.VMEM((3, wide, width), F32)],
    )
    terms = jax.ShapeDtypeStruct((2, groups, block, width), BF)
    return pl.pallas_call(
        qkv_back_kernel,
        grid_spec=grid_spec,
        out_shape=[
            terms,
            terms,
            jax.ShapeDtypeStruct((groups, 2, width), F32),
            jax.ShapeDtypeStruct((NBLK // 2, 3, rows, wide), BF),
            jax.ShapeDtypeStruct((NBLK // 2, 3, rows, wide), BF),
        ],
        compiler_params=params(),
        cost_estimate=cost(4 * groups * seq * width * wide * 3, 16 * 2**20),
        name="qkv_back",
    )(tab, gt0, gt1, first, tok_all, w)


MIXED = (0, 2, 1, 3)
T_PART, T_ROW, T_SLOT = 3, 7, 39


def start_weights(tab, pieces, lanes, target, sem):
    rows = pieces[0].shape[1]
    for p in range(8):
        slot = tab[T_SLOT + p]
        for j in range(4):
            row = pl.multiple_of(tab[T_ROW + p * 4 + j] * rows, 16)
            pltpu.make_async_copy(
                pieces[p].at[j, :, lanes], target.at[slot, pl.ds(row, rows), :], sem.at[slot]
            ).start()


def wait_weights(target, k, sem):
    pltpu.make_async_copy(target.at[k], target.at[k], sem.at[k]).wait()


def live_cotangent(tab, cot, g):
    _, block, width = cot.shape
    position = tab[2] + lax.broadcasted_iota(jnp.int32, (block, width), 0)
    return jnp.where(position < tab[g], cot[g].astype(F32), 0.0)


def mlp_in_kernel(tab, tok, cot, mod, gain, upb, *rest):
    mixed, pieces, rest = (rest[:4], rest[4:8]), rest[8:16], rest[16:]
    after, att, second_t, gbr, gbr_t, sums, act, slope, w, wo, second, sem, sem_o = rest
    groups, block, width = tok.shape
    feats = mixed[0][0].shape[0]
    fh = upb.shape[1]
    k = pl.program_id(0)

    @pl.when(k == 0)
    def _():
        start_weights(tab, pieces, slice(fh, None), wo, sem_o)
        start_weights(tab, pieces, slice(0, fh), w, sem)
        for g in range(groups):
            here = slice(g * block, (g + 1) * block)
            gb = (mod[g, 5:6, :] * live_cotangent(tab, cot, g)).astype(BF)
            gbr[here, :] = gb
            sums[g : g + 1, :] = jnp.sum(gb.astype(F32), axis=0, keepdims=True)
        gbr_t[...] = gbr[...].T
        for r in range(4):
            wait_weights(wo, r, sem_o)
        for g in range(groups):
            here = slice(g * block, (g + 1) * block)
            total = jnp.zeros((block, width), F32)
            for r in range(4):
                total += lax.dot_general(
                    mixed[g][MIXED[r]][...].T,
                    wo[r, :, :feats],
                    NT,
                    preferred_element_type=F32,
                )
            att[g] = total
            rows_after = tok[g].astype(F32) + mod[g, 2:3, :] * total
            after[g] = rows_after
            n, _ = norm_rows(rows_after)
            x = n * (gain[...] * (1.0 + mod[g, 4:5, :])) + mod[g, 3:4, :]
            second[here, :] = x.astype(BF)
        second_t[...] = second[...].T

    c1, c3 = math.sqrt(2.0 / math.pi), 0.044715
    wait_weights(w, k, sem)
    bias = upb[pl.ds(tab[T_PART + k], 1), :]
    hidden = jnp.dot(second[...], w[k], preferred_element_type=F32) + bias
    square = hidden * hidden
    th = jnp.tanh(c1 * hidden * (1.0 + c3 * square))
    up = 0.5 * (1.0 + th)
    act[0] = (hidden * up).astype(BF)
    slope[0] = (
        up + (0.5 * c1) * hidden * (1.0 - th * th) * (1.0 + (3.0 * c3) * square)
    ).astype(BF)


def mlp_out_kernel(tab, mod, downb, gbr, act, slope, *rest):
    pieces, late, rest = rest[:8], rest[8:10], rest[10:]
    out, sums, upsum, gh, w, branch, cot, after, sem, sem_late = rest
    groups, block, width = cot.shape
    k = pl.program_id(0)

    @pl.when(k == 0)
    def _():
        start_weights(tab, pieces, slice(None), w, sem)
        start_late(late, (cot, after), sem_late)
        branch[...] = jnp.broadcast_to(downb[...], branch.shape)

    wait_weights(w, k, sem)
    ga = jnp.dot(gbr[...], w[k], preferred_element_type=F32)
    grad = (ga * slope[0].astype(F32)).astype(BF)
    gh[0] = grad
    upsum[pl.ds(tab[T_PART + k], 1), :] = jnp.sum(grad.astype(F32), axis=0, keepdims=True)
    branch[...] += lax.dot_general(act[0], w[k], NT, preferred_element_type=F32)

    @pl.when(k == 3)
    def _():
        wait_late(late, (cot, after), sem_late)
        for g in range(groups):
            here = slice(g * block, (g + 1) * block)
            out[g] = (after[g] + mod[g, 5:6, :] * branch[here, :]).astype(BF)
            sums[g : g + 1, :] = jnp.sum(
                live_cotangent(tab, cot, g) * branch[here, :], axis=0, keepdims=True
            )


def start_late(sources, targets, sem):
    for i, (source, target) in enumerate(zip(sources, targets)):
        pltpu.make_async_copy(source, target, sem.at[i]).start()


def wait_late(sources, targets, sem):
    for i, (source, target) in enumerate(zip(sources, targets)):
        pltpu.make_async_copy(source, target, sem.at[i]).wait()


def mlp_back_kernel(tab, mod, gain, gh, *rest):
    pieces, late, rest = rest[:8], rest[8:11], rest[11:]
    gmixed, rest = rest[:4], rest[4:]
    sums, gafter, gat_t, w, wo, gsec, gat, cot, after, att, sem, sem_o, sem_late = rest
    groups, block, width = cot.shape
    feats = gmixed[0].shape[0]
    fh = gh.shape[2]
    k = pl.program_id(0)

    @pl.when(k == 0)
    def _():
        start_weights(tab, pieces, slice(0, fh), w, sem)
        start_weights(tab, pieces, slice(fh, None), wo, sem_o)
        start_late(late, (cot, after, att), sem_late)
        gsec[...] = jnp.zeros_like(gsec)

    wait_weights(w, k, sem)
    gsec[...] += lax.dot_general(gh[0], w[k], NT, preferred_element_type=F32)

    @pl.when(k == 3)
    def _():
        wait_late(late, (cot, after, att), sem_late)
        for r in range(4):
            wait_weights(wo, r, sem_o)
        for g in range(groups):
            here = slice(g * block, (g + 1) * block)
            n, inverse = norm_rows(after[g])
            gs = gsec[here, :]
            sums[g, 0:1, :] = jnp.sum(gs, axis=0, keepdims=True)
            sums[g, 1:2, :] = jnp.sum(gs * n, axis=0, keepdims=True)
            scaled = gs * (gain[...] * (1.0 + mod[g, 4:5, :]))
            mean = jnp.mean(scaled, axis=1, keepdims=True)
            along = jnp.mean(scaled * n, axis=1, keepdims=True)
            grad = live_cotangent(tab, cot, g) + inverse * (scaled - mean - n * along)
            gafter[g] = grad
            sums[g, 2:3, :] = jnp.sum(grad * att[g], axis=0, keepdims=True)
            low = (mod[g, 2:3, :] * grad).astype(BF)
            gat[here, :] = low
            for r in range(4):
                gmixed[MIXED[r]][:, here] = (
                    jnp.dot(low, wo[r, :, :feats], preferred_element_type=F32)
                    .astype(BF)
                    .T
                )
        gat_t[...] = gat[...].T


def steps_call(
    kernel, name, tab, arrays, stepped, pieces, late, outs, stepped_outs, scratch, sems, flops
):
    sm = pl.BlockSpec(memory_space=pltpu.SMEM)

    def slot_spec(shape):
        return spec((1,) + shape[1:], lambda k: (k, 0, 0))

    return pl.pallas_call(
        kernel,
        grid=(4,),
        in_specs=[sm]
        + [whole(a.shape) for a in arrays]
        + [slot_spec(a.shape) for a in stepped]
        + [ANY] * (len(pieces) + len(late)),
        out_specs=[whole(a.shape) for a in outs] + [slot_spec(a.shape) for a in stepped_outs],
        out_shape=list(outs) + list(stepped_outs),
        scratch_shapes=scratch
        + [pltpu.VMEM(a.shape, a.dtype) for a in late]
        + [pltpu.SemaphoreType.DMA((4,))] * sems,
        compiler_params=params(),
        cost_estimate=cost(flops, 16 * 2**20),
        name=name,
    )(tab, *arrays, *stepped, *pieces, *late)


def struct(shape, dtype):
    return jax.ShapeDtypeStruct(shape, dtype)


def mlp_in_call(tab, tok, cot, mod, gain, upb, mixed, pieces):
    groups, block, width = tok.shape
    total, fh = groups * block, upb.shape[1]
    rows = struct((groups, block, width), F32)
    tall = struct((width, total), BF)
    wide = struct((4, total, fh), BF)

    return steps_call(
        mlp_in_kernel,
        "mlp_in",
        tab,
        [tok, cot, mod, gain, upb, *mixed[0], *mixed[1]],
        [],
        pieces,
        [],
        [rows, rows, tall, struct((total, width), BF), tall, struct((groups, width), F32)],
        [wide, wide],
        [
            pltpu.VMEM((4, width, fh), BF),
            pltpu.VMEM((4, width, pieces[0].shape[2] - fh), BF),
            pltpu.VMEM((total, width), BF),
        ],
        2,
        10 * total * width * fh,
    )


def mlp_out_call(tab, cot, mod, downb, after, gbr, act, slope, pieces):
    groups, block, width = cot.shape
    total, fh = groups * block, act.shape[2]
    return steps_call(
        mlp_out_kernel,
        "mlp_out",
        tab,
        [mod, downb, gbr],
        [act, slope],
        pieces,
        [cot, after],
        [
            struct((groups, block, width), BF),
            struct((groups, width), F32),
            struct((4, fh), F32),
        ],
        [struct((4, total, fh), BF)],
        [pltpu.VMEM((4, width, fh), BF), pltpu.VMEM((total, width), F32)],
        2,
        16 * total * width * fh,
    )


def mlp_back_call(tab, cot, mod, gain, after, att, gh, pieces, feats):
    groups, block, width = cot.shape
    total, fh = groups * block, gh.shape[2]
    return steps_call(
        mlp_back_kernel,
        "mlp_back",
        tab,
        [mod, gain],
        [gh],
        pieces,
        [cot, after, att],
        [
            *[struct((feats, groups * block), BF)] * 4,
            struct((groups, 3, width), F32),
            struct((groups, block, width), F32),
            struct((width, total), BF),
        ],
        [],
        [
            pltpu.VMEM((4, width, fh), BF),
            pltpu.VMEM((4, width, pieces[0].shape[2] - fh), BF),
            pltpu.VMEM((total, width), F32),
            pltpu.VMEM((total, width), BF),
        ],
        3,
        10 * total * width * fh,
    )


def store_grads(tab, k, src, sent, kept0, kept1, sem):
    rows = src.shape[1] // NBLK
    for b in range(NBLK):
        there = tab[k * NBLK + b]
        piece = src.at[k, pl.ds(b * rows, rows), :]

        @pl.when(k >= 2)
        def _():
            pltpu.make_async_copy(piece, sent.at[there], sem.at[k, b]).start()

        @pl.when((k < 2) & (there < 8))
        def _():
            pltpu.make_async_copy(piece, kept0.at[there], sem.at[k, b]).start()

        @pl.when((k < 2) & (there >= 8))
        def _():
            pltpu.make_async_copy(piece, kept1.at[there - 8], sem.at[k, b]).start()


def wait_grads(src, sent, sem):
    rows = src.shape[1] // NBLK
    for k in range(4):
        for b in range(NBLK):
            pltpu.make_async_copy(
                src.at[k, pl.ds(b * rows, rows), :], sent.at[0], sem.at[k, b]
            ).wait()


def down_grad_kernel(tab, gbr_t, act, sent, kept0, kept1, acc, sem):
    k = pl.program_id(0)
    acc[k] = jnp.dot(gbr_t[...], act[0], preferred_element_type=F32).astype(BF)
    store_grads(tab, k, acc, sent, kept0, kept1, sem)

    @pl.when(k == 3)
    def _():
        wait_grads(acc, sent, sem)


def up_grad_kernel(tab, second_t, gat_t, gh, *rest):
    mixed, (sent, kept0, kept1, acc, sem) = (rest[:4], rest[4:8]), rest[8:]
    k = pl.program_id(0)
    fh = gh.shape[2]
    feats, block = mixed[0][0].shape
    acc[k, :, :fh] = jnp.dot(second_t[...], gh[0], preferred_element_type=F32).astype(BF)
    if acc.shape[2] > fh + feats:
        acc[k, :, fh + feats :] = jnp.zeros((acc.shape[1], acc.shape[2] - fh - feats), BF)
    for r in range(4):

        @pl.when(k == r)
        def _():
            total = None
            for g in range(2):
                term = lax.dot_general(
                    gat_t[:, g * block : (g + 1) * block],
                    mixed[g][MIXED[r]][...],
                    NT,
                    preferred_element_type=F32,
                )
                total = term if total is None else total + term
            acc[k, :, fh : fh + feats] = total.astype(BF)

    store_grads(tab, k, acc, sent, kept0, kept1, sem)

    @pl.when(k == 3)
    def _():
        wait_grads(acc, sent, sem)


def grad_call(kernel, name, tab, fixed, moving, others, lanes):
    width, total = fixed[0].shape
    fh = moving.shape[2]
    rows = width // NBLK
    grid_spec = pltpu.PrefetchScalarGridSpec(
        num_scalar_prefetch=1,
        grid=(4,),
        in_specs=[whole(a.shape) for a in fixed]
        + [spec((1, total, fh), lambda k, _: (k, 0, 0))]
        + [whole(a.shape) for a in others],
        out_specs=[ANY, ANY, ANY],
        scratch_shapes=[
            pltpu.VMEM((4, width, lanes), BF),
            pltpu.SemaphoreType.DMA((4, NBLK)),
        ],
    )
    return pl.pallas_call(
        kernel,
        grid_spec=grid_spec,
        out_shape=[struct((16, rows, lanes), BF)] + [struct((8, rows, lanes), BF)] * 2,
        compiler_params=params(),
        cost_estimate=cost(8 * width * total * lanes, 14 * 2**20),
        name=name,
    )(tab, *fixed, moving, *others)


def norm_back_kernel(t0, t1, t2, tok, after, mod, gain, out):
    normed, inverse = norm_rows(tok[0].astype(F32))
    grad = t0[0, 0].astype(F32) + t1[0, 0].astype(F32) + t2[0].astype(F32)
    scaled = grad * (gain[...] * (1.0 + mod[0, 1:2, :]))
    mean = jnp.mean(scaled, axis=1, keepdims=True)
    along = jnp.mean(scaled * normed, axis=1, keepdims=True)
    out[0] = (after[0] + inverse * (scaled - mean - normed * along)).astype(BF)


def norm_back_call(t0, t1, t2, tok, after, mod, gain):
    groups, block, width = tok.shape
    row = spec((1, block, width), lambda g: (g, 0, 0))
    near = spec((1, 1, block, width), lambda g: (0, g, 0, 0))
    return pl.pallas_call(
        norm_back_kernel,
        grid=(groups,),
        in_specs=[near, near, row, row, row, spec((1, 6, width), lambda g: (g, 0, 0)), whole((1, width))],
        out_specs=row,
        out_shape=jax.ShapeDtypeStruct((groups, block, width), BF),
        compiler_params=params(),
        cost_estimate=cost(40 * groups * block * width, 12 * groups * block * width),
        name="norm_back",
    )(t0, t1, t2, tok, after, mod, gain)


AT = 640


def pack_kernel(one, two, gate_two, upsum, down_bias, mod, gain_one, gain_two, out):
    dp, tp, _, width = out.shape
    groups = one.shape[0]
    lane = lax.broadcasted_iota(jnp.int32, (1, width), 1)

    def window(rows, start, count, at=0):
        row, offset = divmod(start, width)
        first = min(count, width - offset)
        got = rows[row]
        shift = (at - offset) % width
        got = pltpu.roll(got, shift, 1) if shift else got
        if first < count:
            shift = (at + first) % width
            rest = rows[row + 1]
            rest = pltpu.roll(rest, shift, 1) if shift else rest
            got = jnp.where(lane < at + first, got, rest)
        return got

    mods, count_mod = [], 6 * width // dp
    for g in range(groups):
        mods.append(
            [
                one[g, 0:1, :],
                gain_one[...] * one[g, 1:2, :],
                two[g, 2:3, :],
                two[g, 0:1, :],
                gain_two[...] * two[g, 1:2, :],
                gate_two[g : g + 1, :],
            ]
        )
    zero = jnp.zeros((1, width), F32)
    vectors = [zero, zero, zero]
    for g in range(groups):
        vectors[0] += down_bias[g : g + 1, :]
        vectors[1] += (1.0 + mod[g, 1:2, :]) * one[g, 1:2, :]
        vectors[2] += (1.0 + mod[g, 4:5, :]) * two[g, 1:2, :]
    rows_up = [upsum[r : r + 1, :] for r in range(upsum.shape[0])]
    count_up, count = upsum.shape[0] * width // dp, width // dp
    for d in range(dp):
        firsts = [window(mods[g], d * count_mod, count_mod) for g in range(groups)]
        firsts.append(window(rows_up, d * count_up, count_up))
        for r in range(3):
            row = jnp.where(lane < AT, firsts[r], window([vectors[r]], d * count, count, AT))
            for t in range(tp):
                out[d, t, r : r + 1, :] = row


def pack_call(dp, tp, one, two, gate_two, upsum, down_bias, mod, gain_one, gain_two):
    vm = pl.BlockSpec(memory_space=pltpu.VMEM)
    return pl.pallas_call(
        pack_kernel,
        in_specs=[vm] * 8,
        out_specs=vm,
        out_shape=struct((dp, tp, 3, one.shape[2]), F32),
        compiler_params=params(),
        cost_estimate=cost(2**20, 2**20),
        name="pack",
    )(one, two, gate_two, upsum, down_bias, mod, gain_one, gain_two)


def small_kernel(got, cond_t, adaw, adab, upb, downb, gain_one, gain_two):
    dp = got.shape[0]
    cols = adaw.shape[0]
    total = jnp.sum(got[...], axis=1)
    mods = jnp.concatenate([total[:, 0, :], total[:, 1, :]], axis=0)
    product = lax.dot_general(
        mods,
        cond_t[...],
        (((0,), (1,)), ((), ())),
        precision=lax.Precision.HIGHEST,
        preferred_element_type=F32,
    )
    adaw[...] = product[:cols]
    flat = jnp.sum(total, axis=0)
    adab[...] = flat[0:1, :cols] + flat[1:2, :cols]
    upb[...] = flat[2:3, : upb.shape[1]]
    for row, ref in enumerate((downb, gain_one, gain_two)):
        ref[...] = flat[row : row + 1, AT : AT + ref.shape[1]]


def small_call(got, cond_t, cols, up_count, count):
    shapes = [(cols, cond_t.shape[0]), (1, cols), (1, up_count)] + [(1, count)] * 3
    vm = pl.BlockSpec(memory_space=pltpu.VMEM)
    return pl.pallas_call(
        small_kernel,
        in_specs=[vm, vm],
        out_specs=[vm] * 6,
        out_shape=[jax.ShapeDtypeStruct(shape, F32) for shape in shapes],
        compiler_params=params(),
        cost_estimate=cost(2**20, 2**20),
        name="small",
    )(got, cond_t)


def time_embedding(time_steps, width_total):
    half_width = width_total // 2
    frequency = jnp.exp(-math.log(10000.0) * jnp.arange(half_width, dtype=F32) / half_width)
    angles = time_steps.astype(F32)[:, None] * frequency[None, :]
    return jnp.concatenate([jnp.cos(angles), jnp.sin(angles)], axis=-1)


def rotary_halves(length_total):
    half = HEAD // 2
    inverse = jnp.exp(-math.log(10000.0) * 2.0 * jnp.arange(half, dtype=F32) / HEAD)
    angles = jnp.arange(length_total, dtype=F32)[:, None] * inverse[None, :]
    return jnp.cos(angles), jnp.sin(angles)


def device_index(z, y, x, c):
    return ((z * 2 + y) * 2 + x) * 2 + c


def permutation(move):
    pairs = []
    for z in range(4):
        for y in range(2):
            for x in range(2):
                for c in range(2):
                    pairs.append((device_index(z, y, x, c), device_index(*move(z, y, x, c))))
    return pairs


CORE = permutation(lambda z, y, x, c: (z, y, x, 1 - c))
FLIP_X = permutation(lambda z, y, x, c: (z, y, 1 - x, c))
FLIP_BOTH = permutation(lambda z, y, x, c: (z, y, 1 - x, 1 - c))
FLIP_Y = permutation(lambda z, y, x, c: (z, 1 - y, x, c))
FIRST = permutation(lambda z, y, x, c: (z, 1 - y, x, c) if c == 0 else (z, y, 1 - x, c))
SECOND = permutation(lambda z, y, x, c: (z, y, 1 - x, c) if c == 0 else (z, 1 - y, x, c))
ALONG_Z = [permutation(lambda z, y, x, c, s=s: ((z + s) % 4, y, x, c)) for s in range(4)]


def send(array, pairs):
    return lax.ppermute(array, ("dp", "tensor"), pairs)


def start_z(shard):
    return [shard] + [send(shard, ALONG_Z[s]) for s in (1, 2, 3)]


def gather_z(shard):
    return jnp.stack(start_z(shard))


def after_all(value, *others):
    flat, tree = jax.tree.flatten(value)
    tied = lax.optimization_barrier((tuple(flat), others))[0]
    return jax.tree.unflatten(tree, tied)


def add_low(*terms):
    return functools.reduce(jnp.add, [term.astype(F32) for term in terms]).astype(BF)


def exchange(arrays, fast):
    if fast:
        perms = (None, CORE, FLIP_X, FLIP_BOTH)
        return [arrays[0]] + [send(arrays[r], perms[r]) for r in (1, 2, 3)]
    return list(lax.all_to_all(jnp.stack(arrays), "tensor", 0, 0, tiled=True))


class Reduce:
    def __init__(self, sent, kept0, kept1):
        shape = (2, 4) + sent.shape[1:]
        self.kept = kept0.reshape(shape), kept1.reshape(shape)
        self.got = send(sent, CORE).reshape((2,) + shape)

    def one(self, *others):
        got = after_all(self.got, *others) if others else self.got
        self.got = got
        self.half = add_low(self.kept[1], got[1])
        return self.half

    def two(self, *others):
        self.got_two = after_all(send(self.half, SECOND), *others)
        self.quarter = add_low(self.kept[0][1], self.got[0, 1], self.got_two[1])
        return self.quarter

    def three(self, *others):
        self.got_three = after_all(send(self.quarter, FIRST), *others)
        self.parts = [
            add_low(self.kept[0][0, s], self.got[0, 0, s], self.got_two[0, s], self.got_three[s])
            for s in range(4)
        ]
        return self.parts

    def start_last(self):
        return [send(self.parts[s], ALONG_Z[s]) for s in (1, 2, 3)]

    def end_last(self, got):
        return functools.reduce(jnp.add, [g.astype(F32) for g in [self.parts[0]] + list(got)])


def tables(z, y, x, c):
    far_core = np.array([0, 0, 0, 0, 1, 1, 1, 1])
    kind = np.array([0, 1, 2, 3] * 2)
    core = jnp.bitwise_xor(c, far_core)
    rel_x = jnp.where(kind == 0, 0, jnp.where(kind == 3, 1, jnp.where(kind == 1, core, 1 - core)))
    rel_y = jnp.where(kind == 0, 0, jnp.where(kind == 3, 1, jnp.where(kind == 1, 1 - core, core)))
    slots = far_core * 2 + rel_x
    back = np.arange(4)
    from_z = jnp.remainder(z - back, 4)
    weight_rows = (from_z[None, :] * 2 + jnp.bitwise_xor(y, rel_y)[:, None]).reshape(32)
    slot = np.arange(4)
    parts = jnp.bitwise_xor(x, slot % 2) * 2 + jnp.bitwise_xor(c, slot // 2)
    block = np.arange(NBLK)
    to_z = jnp.remainder(block // 2 - z, 4)
    to_y = jnp.bitwise_xor(block % 2, y)
    slot_core = jnp.bitwise_xor(c, slot // 2)[:, None]
    to_x = (slot % 2)[:, None]
    major = jnp.where(slot_core == 0, to_x, to_y[None, :])
    minor = jnp.where(slot_core == 0, to_y[None, :], to_x)
    targets = (major * 8 + minor * 4 + to_z[None, :]).reshape(4 * NBLK)
    qkv_rows = jnp.concatenate(
        [from_z * 2 + y, from_z * 2 + (1 - y)]
    )
    qkv_targets = to_y * 4 + to_z
    return parts, weight_rows, slots, targets, qkv_rows, qkv_targets


def shards(
    tokens,
    lengths,
    times,
    cotangent,
    w_qkv,
    w_out,
    w_up,
    up_bias,
    w_down,
    down_bias,
    norm1_gain,
    norm2_gain,
    ada_weight,
    ada_bias,
):
    groups, block, width = tokens.shape
    dp, tp = lax.axis_size("dp"), lax.axis_size("tensor")
    seq = block * tp
    t = lax.axis_index("tensor")
    d = lax.axis_index("dp")
    fast = dp == 8 and tp == 4
    feats = w_qkv.shape[2]
    fh = w_up.shape[1]
    rows = width // NBLK
    zero = jnp.zeros((), jnp.int32)
    z, y, x, c = (d // 2, d % 2, t // 2, t % 2) if fast else (zero, zero, zero, zero)
    here = t if fast else zero
    parts, weight_rows, slots, targets, qkv_rows, qkv_targets = tables(z, y, x, c)

    all_times = lax.all_to_all(
        jnp.broadcast_to(times[None, :], (dp, groups)), "dp", 0, 0, tiled=True
    ).reshape(-1)
    pad = (-feats) % 128
    qkv_shard = jnp.pad(w_qkv, ((0, 0), (0, 0), (0, pad)))
    if fast:
        near = gather_z(qkv_shard)
        qkv_pieces = (near, send(near, FLIP_Y))
    else:
        full = lax.all_gather(qkv_shard, "dp", axis=1, tiled=True)
        full = full.reshape(3, NBLK, rows, feats + pad).transpose(1, 0, 2, 3)
        order = [[(-j) % 4 * 2 + p for j in range(4)] for p in range(2)]
        qkv_pieces = tuple(jnp.stack([full[b] for b in order[p]]) for p in range(2))
    tok_all = lax.all_gather(tokens, "tensor", axis=1, tiled=True)

    condition = time_embedding(all_times, ada_weight.shape[0])
    part = jnp.dot(
        condition, ada_weight.astype(F32), precision=lax.Precision.HIGHEST
    ) + ada_bias.astype(F32)
    cols = part.shape[1]
    vectors = jnp.concatenate([up_bias, down_bias, norm1_gain, norm2_gain]).astype(F32)
    sent_mod = jnp.concatenate(
        [
            part.reshape(dp, groups * cols),
            jnp.broadcast_to(vectors[None, :], (dp, vectors.shape[0])),
        ],
        axis=1,
    )
    payload = lax.all_to_all(sent_mod, "dp", 0, 0, tiled=True)
    mod = (
        payload[:, : groups * cols]
        .reshape(dp, groups, cols)
        .transpose(1, 0, 2)
        .reshape(groups, 6, width)
    )
    at = groups * cols
    small = []
    for count in (up_bias.shape[0], down_bias.shape[0], norm1_gain.shape[0], norm2_gain.shape[0]):
        small.append(payload[:, at : at + count].reshape(-1))
        at += count
    upb_all = small[0].reshape(tp, fh)
    downb_all, gain_one, gain_two = (v.reshape(1, width) for v in small[1:])

    up_shard = jnp.pad(
        jnp.concatenate([w_up, w_out.T], axis=1), ((0, 0), (0, (-fh - feats) % 128))
    )
    down_shard = w_down.T
    if fast:
        up_shard, down_shard = after_all((up_shard, down_shard), qkv_pieces[1], payload)
        up_parts = start_z(up_shard)
        down_parts = start_z(down_shard)
    else:

        def gather_pieces(shard):
            full = lax.all_gather(shard, "dp", axis=0, tiled=True)
            full = lax.all_gather(full, "tensor", axis=0, tiled=False)
            full = full.reshape(tp, NBLK, rows, full.shape[2])
            return [
                jnp.stack([full[rel_x * 2 + far, b] for b in order[rel_y]])
                for far in range(2)
                for rel_x, rel_y in ((0, 0), (far, 1 - far), (1 - far, far), (1, 1))
            ]

    cos, sin = rotary_halves(seq)
    heads_wide = (feats + pad) // HEAD
    cos_wide = jnp.tile(jnp.concatenate([cos, cos], axis=1), (1, heads_wide))
    sin_wide = jnp.tile(jnp.concatenate([-sin, sin], axis=1), (1, heads_wide))
    first_all, q, k, v, kt, vt, w_all = qkv_call(
        qkv_rows.astype(jnp.int32), tok_all, mod, gain_one, cos_wide, sin_wide, *qkv_pieces
    )
    vt_later = vt
    if fast:
        up_near = jnp.stack(after_all(up_parts, vt))
        vt = after_all(vt, up_near)
        up_one, up_two = send(up_near, FIRST), send(up_near, SECOND)
    small_tab = jnp.concatenate([lengths, here.reshape(1)]).astype(jnp.int32)
    *mixed0, probs0 = attend_call(0, small_tab, q, k, vt)
    if fast:
        mixed0, up_near, up_one, up_two, down_parts = after_all(
            (mixed0, up_near, up_one, up_two, down_parts), probs0
        )
        vt_later = after_all(vt, up_one, up_two)
        mixed0_all = exchange(mixed0, fast)
        up_both = send(up_one, SECOND)
        up_far = [send(piece, CORE) for piece in (up_near, up_one, up_two)]
    *mixed1, probs1 = attend_call(1, small_tab, q, k, vt_later)
    if fast:
        mixed1, up_both = after_all((mixed1, up_both), probs1, *mixed0_all)
        mixed1 = after_all(mixed1, up_both)
        up_far.append(send(up_both, CORE))
        up_pieces = [up_near, up_one, up_two, up_both] + up_far
    else:
        up_pieces, down_pieces = gather_pieces(up_shard), gather_pieces(down_shard)
        mixed0_all = exchange(mixed0, fast)
    mixed1_all = exchange(mixed1, fast)

    tab = jnp.concatenate([lengths, (t * block).reshape(1), parts, weight_rows, slots]).astype(
        jnp.int32
    )
    if fast:
        down_parts, up_pieces = after_all((down_parts, up_pieces), *mixed1_all)
        down_near = jnp.stack(down_parts)
        up_pieces = after_all(up_pieces, down_near)
        down_one, down_two = send(down_near, FIRST), send(down_near, SECOND)
    after, att, second_t, gbr, gbr_t, sum_down_bias, act, slope = mlp_in_call(
        tab, tokens, cotangent, mod, gain_two, upb_all, (mixed0_all, mixed1_all), up_pieces
    )
    targets = targets.astype(jnp.int32)
    if fast:
        down_one, down_two, act = after_all((down_one, down_two, act), after)
        act = after_all(act, down_one, down_two)
        down_both = send(down_one, SECOND)
        down_far = [send(piece, CORE) for piece in (down_near, down_one, down_two)]
    gd_s, *gd_k = grad_call(down_grad_kernel, "down_grad", targets, [gbr_t], act, [], fh)
    if fast:
        gd_s, down_both, down_far = after_all((gd_s, down_both, down_far), *gd_k)
        gd_s = after_all(gd_s, down_both, *down_far)
        down_sum = Reduce(gd_s, *gd_k)
        down_far.append(send(down_both, CORE))
        down_pieces = [down_near, down_one, down_two, down_both] + down_far
    out, sum_gate_two, upsum, gh = mlp_out_call(
        tab, cotangent, mod, downb_all, after, gbr, act, slope, down_pieces
    )
    if fast:
        gh = after_all(gh, down_sum.one(gh))
    *gms, sums_two, grad_after, gat_t = mlp_back_call(
        tab, cotangent, mod, gain_two, after, att, gh, up_pieces, feats
    )
    if fast:
        gms, gh, quarter = after_all((gms, gh, down_sum.two(grad_after)), down_sum.got_two)
    gm = exchange(gms, fast)
    if fast:
        gh = after_all(gh, quarter)
    gu_s, *gu_k = grad_call(
        up_grad_kernel,
        "up_grad",
        targets,
        [second_t, gat_t],
        gh,
        [*mixed0_all, *mixed1_all],
        up_pieces[0].shape[2],
    )
    here_tab = here.reshape(1).astype(jnp.int32)
    if fast:
        down_sum.three(*gu_k)
        gu_s = after_all(gu_s, down_sum.got_three, *gm)
        up_sum = Reduce(gu_s, *gu_k)
        down_got = down_sum.start_last()
        gm = after_all(gm, up_sum.one(*down_sum.parts))
    grad_t0 = attend_back_call(0, here_tab, q, kt, v, probs0, gm, cos.T, sin.T)
    if fast:
        down_got = after_all(down_got, grad_t0)
        gm = after_all(gm, up_sum.two(grad_t0, *down_got))
    grad_t1 = attend_back_call(1, here_tab, q, kt, v, probs1, gm, cos.T, sin.T)
    if fast:
        grad_t1 = after_all(grad_t1, *up_sum.three(grad_t1))
    fts, ftk, sums_one, dws, dwk = qkv_back_call(
        jnp.concatenate([qkv_targets, here.reshape(1)]).astype(jnp.int32),
        grad_t0,
        grad_t1,
        first_all,
        tok_all,
        w_all,
    )

    if fast:
        up_got = up_sum.start_last()
        fts, dws, sums_one, sums_two = after_all((fts, dws, sums_one, sums_two), *up_got)
        got, got_dw = send(fts, CORE), send(dws, FLIP_Y)
        far = send(add_low(ftk[1], got[1]), FLIP_X)
    else:

        def absolute(sent, kept):
            lanes = sent.shape[2]
            near = kept.reshape(2, 2, 4, rows, lanes)
            far = sent.reshape(2, 2, 4, rows, lanes).transpose(1, 0, 2, 3, 4)
            both = jnp.stack([near, far], axis=1)
            return both.transpose(0, 1, 3, 2, 4, 5).reshape(tp, width, lanes).astype(F32)

        def reduce_all(sent, kept):
            terms = lax.psum_scatter(
                absolute(sent, kept), "tensor", scatter_dimension=0, tiled=True
            )[0]
            return lax.psum_scatter(terms, "dp", scatter_dimension=0, tiled=True)

        sum_up = reduce_all(gu_s, jnp.concatenate(gu_k))
        sum_down = reduce_all(gd_s, jnp.concatenate(gd_k))
        terms = jnp.stack([dwk, dws]).transpose(2, 1, 0, 3, 4)
        terms = terms.reshape(3, width, feats + pad).astype(F32)
        sum_qkv = lax.psum_scatter(terms, "dp", scatter_dimension=1, tiled=True)
        terms = jnp.stack([ftk, fts], axis=1).reshape(tp, groups, block, width).astype(F32)
        grad_first = lax.psum_scatter(terms, "tensor", scatter_dimension=0, tiled=True)[0]
        nought = jnp.zeros_like(grad_first)
        grad_in = norm_back_call(
            grad_first[None], nought[None], nought, tokens, grad_after, mod, gain_one
        )

    up_count, count = up_bias.shape[0], down_bias.shape[0]
    payload = pack_call(
        dp,
        tp,
        sums_one,
        sums_two,
        sum_gate_two,
        upsum,
        sum_down_bias,
        mod,
        gain_one,
        gain_two,
    ).reshape(dp * tp, 3, width)
    payload = lax.all_to_all(payload, ("dp", "tensor"), 0, 0, tiled=True)
    cond_t = condition.reshape(dp, groups, -1).transpose(2, 1, 0).reshape(-1, dp * groups)
    grad_adaw, grad_adab, g_up, g_down, g_one, g_two = small_call(
        payload.reshape(dp, tp, 3, width), cond_t, cols, up_count, count
    )
    if fast:
        got_dw = after_all(got_dw, grad_adaw)
        dw_parts = [add_low(dwk[s], got_dw[s]) for s in range(4)]
        dw_got = [send(dw_parts[s], ALONG_Z[s]) for s in (1, 2, 3)]
        far, up_got = after_all((far, up_got), *dw_parts)
        grad_in = norm_back_call(ftk, got, far, tokens, grad_after, mod, gain_one)
        dw_got = after_all(dw_got, grad_in)
        sum_up = up_sum.end_last(up_got)
        sum_down = down_sum.end_last(down_got)
        sum_qkv = functools.reduce(jnp.add, [g.astype(F32) for g in [dw_parts[0]] + dw_got])

    return (
        out,
        grad_in,
        sum_qkv[:, :, :feats],
        sum_up[:, fh : fh + feats].T,
        sum_up[:, :fh],
        g_up[0],
        sum_down.T,
        g_down[0],
        g_one[0],
        g_two[0],
        grad_adaw.T,
        grad_adab[0],
    )


def solution(mesh):
    in_specs = (
        P("dp", "tensor", None),
        P("dp"),
        P("dp"),
        P("dp", "tensor", None),
        P(None, "dp", "tensor"),
        P("tensor", "dp"),
        P("dp", "tensor"),
        P("dp"),
        P("tensor", "dp"),
        P("dp"),
        P("dp"),
        P("dp"),
        P(None, "dp"),
        P("dp"),
    )
    out_specs = (
        P("dp", "tensor", None),
        P("dp", "tensor", None),
        P(None, "dp", "tensor"),
        P("tensor", "dp"),
        P("dp", "tensor"),
        P("dp"),
        P("tensor", "dp"),
        P("dp"),
        P("dp"),
        P("dp"),
        P(None, "dp"),
        P("dp"),
    )
    return jax.shard_map(shards, mesh=mesh, in_specs=in_specs, out_specs=out_specs, check_vma=False)
```

```python
import functools
import math

import jax
import jax.numpy as jnp
import numpy as np
from jax import lax
from jax.experimental import pallas as pl
from jax.experimental.pallas import tpu as pltpu
from jax.sharding import PartitionSpec as P

HEAD = 64
EPS = 1e-05
MASKED = -1e30
BF = jnp.bfloat16
F32 = jnp.float32
VMEM_MAX = 60 * 1024 * 1024
NBLK = 8
NT = (((1,), (1,)), ((), ()))


def spec(block, index_map):
    return pl.BlockSpec(block, index_map)


def whole(shape):
    return pl.BlockSpec(shape, lambda *_: (0,) * len(shape))


ANY = pl.BlockSpec(memory_space=pl.ANY)


def params():
    return pltpu.CompilerParams(vmem_limit_bytes=VMEM_MAX)


def cost(flops, moved, trans=0):
    return pl.CostEstimate(flops=flops, bytes_accessed=moved, transcendentals=trans)


def norm_rows(rows):
    centered = rows - jnp.mean(rows, axis=1, keepdims=True)
    variance = jnp.mean(centered * centered, axis=1, keepdims=True)
    inverse = lax.rsqrt(variance + EPS)
    return centered * inverse, inverse


def first_rows(tok, shift, scale, gain):
    normed, _ = norm_rows(tok.astype(F32))
    return (normed * (gain * (1.0 + scale)) + shift).astype(BF), normed


def qkv_kernel(tab, tok, mod, gain, cos, sin, w0, w1, q, k, v, kt, vt, w, sem):
    groups, heads, block = q.shape[:3]
    rows, wide = w0.shape[2], w.shape[2]

    @pl.when(pl.program_id(0) == 0)
    def _():
        copies = []
        for p, ref in enumerate((w0, w1)):
            for j in range(4):
                row = pl.multiple_of(tab[p * 4 + j] * rows, 16)
                copies.append(
                    pltpu.make_async_copy(
                        ref.at[j], w.at[:, pl.ds(row, rows), :], sem.at[p * 4 + j]
                    )
                )
        for copy in copies:
            copy.start()
        for copy in copies:
            copy.wait()

    low = lax.rem(lax.broadcasted_iota(jnp.int32, (block, wide), 1), HEAD) < HEAD // 2
    cos_wide = jnp.concatenate([cos[...]] * (wide // 128), axis=1)
    sin_wide = jnp.concatenate([sin[...]] * (wide // 128), axis=1)

    def rotate(vec):
        turned = jnp.where(
            low, pltpu.roll(vec, wide - HEAD // 2, 1), pltpu.roll(vec, HEAD // 2, 1)
        )
        return vec * cos_wide + turned * sin_wide

    for g in range(groups):

        def store_heads(ref, vec):
            for h in range(heads):
                shifted = vec if h == 0 else pltpu.roll(vec, wide - h * HEAD, 1)
                ref[g, h] = shifted[:, :HEAD].astype(BF)

        x, _ = first_rows(tok[g], mod[g, 0:1, :], mod[g, 1:2, :], gain[...])
        query = rotate(jnp.dot(x, w[0], preferred_element_type=F32))
        store_heads(q, query * (HEAD**-0.5))
        key = rotate(jnp.dot(x, w[1], preferred_element_type=F32))
        store_heads(k, key)
        kt[g] = key.T[: heads * HEAD].astype(BF)
        value = jnp.dot(x, w[2], preferred_element_type=F32)
        store_heads(v, value)
        vt[g] = value.T[: heads * HEAD].astype(BF)


def qkv_call(tab, tok_all, mod, gain, cos, sin, w0, w1):
    groups, seq, width = tok_all.shape
    block = seq // 4
    wide = w0.shape[3]
    heads = (wide // HEAD) * 3 // 4
    feats = heads * HEAD
    by_head = spec((groups, heads, block, HEAD), lambda j, _: (0, 0, j, 0))
    by_feat = spec((groups, feats, block), lambda j, _: (0, 0, j))
    grid_spec = pltpu.PrefetchScalarGridSpec(
        num_scalar_prefetch=1,
        grid=(4,),
        in_specs=[
            spec((groups, block, width), lambda j, _: (0, j, 0)),
            whole((groups, 6, width)),
            whole((1, width)),
            spec((block, 128), lambda j, _: (j, 0)),
            spec((block, 128), lambda j, _: (j, 0)),
            ANY,
            ANY,
        ],
        out_specs=[by_head, by_head, by_head, by_feat, by_feat, whole((3, width, wide))],
        scratch_shapes=[pltpu.SemaphoreType.DMA((8,))],
    )
    head_shape = jax.ShapeDtypeStruct((groups, heads, seq, HEAD), BF)
    turned = jax.ShapeDtypeStruct((groups, feats, seq), BF)
    return pl.pallas_call(
        qkv_kernel,
        grid_spec=grid_spec,
        out_shape=[
            head_shape,
            head_shape,
            head_shape,
            turned,
            turned,
            jax.ShapeDtypeStruct((3, width, wide), BF),
        ],
        compiler_params=params(),
        cost_estimate=cost(2 * groups * seq * width * wide * 3, 16 * 2**20),
        name="qkv",
    )(tab, tok_all, mod, gain, cos, sin, w0, w1)


CHUNK = 128
LEAST = 256


def unrolled(count, step, carried):
    for i in range(count):
        carried = step(i, carried)
    return carried


def eights(rows, op):
    return op(rows.reshape(rows.shape[0] // 8, 8, rows.shape[1]), axis=0)


def attend_kernel(tab, q, k, vt, mix0, mix1, mix2, mix3, probs, inverse, raw, mixed, *, group):
    heads = k.shape[1]
    block = q.shape[2]
    length = tab[group]
    chunks = k.shape[2] // CHUNK
    position = lax.broadcasted_iota(jnp.int32, (CHUNK, block), 0)

    def head(h, _):
        query = q[0, h]

        def score(c, largest):
            rows = slice(c * CHUNK, (c + 1) * CHUNK)
            scores = lax.dot_general(k[0, h, rows, :], query, NT, preferred_element_type=F32)
            if (c + 1) * CHUNK > LEAST:
                scores = jnp.where(position < length - c * CHUNK, scores, MASKED)
            raw[rows, :] = scores
            return jnp.maximum(largest, eights(scores, jnp.max))

        largest = unrolled(chunks, score, jnp.full((8, block), MASKED, F32))
        largest = jnp.max(largest, axis=0, keepdims=True)
        here = pl.ds(pl.multiple_of(h * HEAD, HEAD), HEAD)

        def weigh(c, carried):
            total, out = carried
            rows = slice(c * CHUNK, (c + 1) * CHUNK)
            weights = jnp.exp(raw[rows, :] - largest)
            low = weights.astype(BF)
            probs[h, rows, :] = low
            out = out + jnp.dot(vt[0, here, rows], low, preferred_element_type=F32)
            return total + eights(weights, jnp.sum), out

        total, out = unrolled(
            chunks, weigh, (jnp.zeros((8, block), F32), jnp.zeros((HEAD, block), F32))
        )
        scale = 1.0 / jnp.sum(total, axis=0, keepdims=True)
        inverse[h] = scale
        mixed[here, :] = (out * scale).astype(BF)
        return 0

    unrolled(heads, head, 0)
    for r, ref in enumerate((mix0, mix1, mix2, mix3)):

        @pl.when(turn(pl.program_id(0)) == r)
        def _():
            ref[...] = mixed[...]


def turn(step):
    return lax.rem(step + 1, 4)


def attend_call(group, tab, q, k, vt):
    _, heads, seq, _ = q.shape
    block = seq // 4
    feats = heads * HEAD

    def piece(i, tab):
        return lax.bitwise_xor(tab[2], turn(i))

    grid_spec = pltpu.PrefetchScalarGridSpec(
        num_scalar_prefetch=1,
        grid=(4,),
        in_specs=[
            spec((1, heads, block, HEAD), lambda i, tab: (group, 0, piece(i, tab), 0)),
            spec((1, heads, seq, HEAD), lambda i, tab: (group, 0, 0, 0)),
            spec((1, feats, seq), lambda i, tab: (group, 0, 0)),
        ],
        out_specs=[
            *[whole((feats, block))] * 4,
            spec((heads, seq, block), lambda i, tab: (0, 0, piece(i, tab))),
            spec((heads, 1, block), lambda i, tab: (0, 0, piece(i, tab))),
        ],
        scratch_shapes=[pltpu.VMEM((seq, block), F32), pltpu.VMEM((feats, block), BF)],
    )
    return pl.pallas_call(
        functools.partial(attend_kernel, group=group),
        grid_spec=grid_spec,
        out_shape=[
            *[jax.ShapeDtypeStruct((feats, block), BF)] * 4,
            jax.ShapeDtypeStruct((heads, seq, seq), BF),
            jax.ShapeDtypeStruct((heads, 1, seq), F32),
        ],
        compiler_params=params(),
        cost_estimate=cost(16 * heads * seq * seq * HEAD, 10 * 2**20, heads * seq * seq),
        name="attend",
    )(tab, q, k, vt)


def attend_back_kernel(
    tab, q, kt, v, probs, inverse, gm0, gm1, gm2, gm3, cos, sin, out, dk, dv, gm
):
    heads, block = q.shape[1], q.shape[2]
    half = HEAD // 2
    step = pl.program_id(0)
    j = lax.bitwise_xor(tab[2], step)

    @pl.when(step == 0)
    def _():
        dk[...] = jnp.zeros_like(dk)
        dv[...] = jnp.zeros_like(dv)
        for r, ref in enumerate((gm0, gm1, gm2, gm3)):
            gm[r] = ref[...]

    columns = pl.ds(pl.multiple_of(j * block, 128), block)
    cos_here, sin_here = cos[:, columns], sin[:, columns]

    def store_turned(plane, h, vec, c, s, where):
        low, high = vec[:half], vec[half:]
        base = pl.multiple_of(h * HEAD, HEAD)
        out[plane, pl.ds(base, half), where] = (low * c + high * s).astype(BF)
        out[plane, pl.ds(base + half, half), where] = (high * c - low * s).astype(BF)

    def head(h, _):
        here = pl.ds(pl.multiple_of(h * HEAD, HEAD), HEAD)
        scale = inverse[h]
        grad = (gm[step, here, :].astype(F32) * scale).astype(BF)
        query = q[0, h]

        low = probs[h]
        dp = jnp.dot(v[0, h], grad, preferred_element_type=F32)
        soft = low.astype(F32)
        prod = soft * dp
        inner = jnp.sum(prod, axis=0, keepdims=True) * scale
        ds = (prod - soft * inner).astype(BF)
        dv[h] += lax.dot_general(low, grad, NT, preferred_element_type=F32)
        dk[h] += jnp.dot(ds, query, preferred_element_type=F32)
        dq = jnp.dot(kt[0, here, :], ds, preferred_element_type=F32)
        store_turned(0, h, dq * (HEAD**-0.5), cos_here, sin_here, columns)
        return 0

    unrolled(heads, head, 0)

    @pl.when(step == pl.num_programs(0) - 1)
    def _():
        def turn_keys(h, _):
            store_turned(1, h, dk[h].T, cos[...], sin[...], slice(None))
            out[2, pl.ds(pl.multiple_of(h * HEAD, HEAD), HEAD), :] = dv[h].T.astype(BF)
            return 0

        unrolled(heads, turn_keys, 0)


def attend_back_call(group, tab, q, kt, v, probs, inverse, gm, cos, sin):
    _, heads, seq, _ = q.shape
    block = seq // 4
    feats = heads * HEAD
    half = HEAD // 2

    def piece(i, tab):
        return lax.bitwise_xor(tab[2], i)

    grid_spec = pltpu.PrefetchScalarGridSpec(
        num_scalar_prefetch=1,
        grid=(4,),
        in_specs=[
            spec((1, heads, block, HEAD), lambda i, tab: (group, 0, piece(i, tab), 0)),
            spec((1, feats, seq), lambda i, tab: (group, 0, 0)),
            spec((1, heads, seq, HEAD), lambda i, tab: (group, 0, 0, 0)),
            spec((heads, seq, block), lambda i, tab: (0, 0, piece(i, tab))),
            spec((heads, 1, block), lambda i, tab: (0, 0, piece(i, tab))),
            *[spec((feats, block), lambda i, tab: (0, group))] * 4,
            whole((half, seq)),
            whole((half, seq)),
        ],
        out_specs=whole((3, feats, seq)),
        scratch_shapes=[
            pltpu.VMEM((heads, seq, HEAD), F32),
            pltpu.VMEM((heads, seq, HEAD), F32),
            pltpu.VMEM((4, feats, block), BF),
        ],
    )
    return pl.pallas_call(
        attend_back_kernel,
        grid_spec=grid_spec,
        out_shape=jax.ShapeDtypeStruct((3, feats, seq), BF),
        compiler_params=params(),
        cost_estimate=cost(32 * heads * seq * seq * HEAD, 10 * 2**20),
        name="attend_back",
    )(tab, q, kt, v, probs, inverse, *gm, cos, sin)


def qkv_back_kernel(tab, gt0, gt1, tok, w, mod, gain, fts, ftk, sums, dws, dwk, acc):
    i = pl.program_id(0)
    feats, block = gt0.shape[1], gt0.shape[2]
    wide, width = w.shape[2], w.shape[1]
    rows = dws.shape[2]

    @pl.when(i == 0)
    def _():
        acc[...] = jnp.zeros_like(acc)
        sums[...] = jnp.zeros_like(sums)

    for g, gt in enumerate((gt0, gt1)):
        first, normed = first_rows(tok[g], mod[g, 0:1, :], mod[g, 1:2, :], gain[...])
        total = None
        for j in range(3):
            part = gt[j]
            tall = part.astype(F32)
            if wide > feats:
                tall = jnp.concatenate([tall, jnp.zeros((wide - feats, block), F32)], axis=0)
            term = lax.dot_general(tall.T.astype(BF), w[j], NT, preferred_element_type=F32)
            total = term if total is None else total + term
            acc[j, :feats] += jnp.dot(part, first, preferred_element_type=F32)
        sums[g, 0:1, :] += jnp.sum(total, axis=0, keepdims=True)
        sums[g, 1:2, :] += jnp.sum(total * normed, axis=0, keepdims=True)
        low = total.astype(BF)

        @pl.when(i < 2)
        def _():
            fts[0, g] = low

        @pl.when(i >= 2)
        def _():
            ftk[0, g] = low

    @pl.when(i == pl.num_programs(0) - 1)
    def _():
        for j in range(3):
            flat = acc[j].T.astype(BF)
            for b in range(NBLK):
                part = flat[b * rows : (b + 1) * rows]
                there = tab[b]

                @pl.when(there < NBLK // 2)
                def _():
                    dwk[there, j] = part

                @pl.when(there >= NBLK // 2)
                def _():
                    dws[there - NBLK // 2, j] = part


def qkv_back_call(tab, gt0, gt1, tok_all, w, mod, gain):
    _, feats, seq = gt0.shape
    groups = tok_all.shape[0]
    block = seq // 4
    width = tok_all.shape[2]
    wide = w.shape[2]
    rows = width // NBLK

    def piece(i, tab):
        return lax.bitwise_xor(tab[NBLK], lax.rem(i, 2) * 2 + (1 - i // 2))

    by_feat = spec((3, feats, block), lambda i, tab: (0, 0, piece(i, tab)))
    grid_spec = pltpu.PrefetchScalarGridSpec(
        num_scalar_prefetch=1,
        grid=(4,),
        in_specs=[
            by_feat,
            by_feat,
            spec((groups, block, width), lambda i, tab: (0, piece(i, tab), 0)),
            whole((3, width, wide)),
            whole((groups, 6, width)),
            whole((1, width)),
        ],
        out_specs=[
            spec((1, groups, block, width), lambda i, tab: (jnp.minimum(i, 1), 0, 0, 0)),
            spec((1, groups, block, width), lambda i, tab: (jnp.maximum(i - 2, 0), 0, 0, 0)),
            whole((groups, 2, width)),
            whole((NBLK // 2, 3, rows, wide)),
            whole((NBLK // 2, 3, rows, wide)),
        ],
        scratch_shapes=[pltpu.VMEM((3, wide, width), F32)],
    )
    terms = jax.ShapeDtypeStruct((2, groups, block, width), BF)
    share = jax.ShapeDtypeStruct((NBLK // 2, 3, rows, wide), BF)
    return pl.pallas_call(
        qkv_back_kernel,
        grid_spec=grid_spec,
        out_shape=[terms, terms, jax.ShapeDtypeStruct((groups, 2, width), F32), share, share],
        compiler_params=params(),
        cost_estimate=cost(4 * groups * seq * width * wide * 3, 16 * 2**20),
        name="qkv_back",
    )(tab, gt0, gt1, tok_all, w, mod, gain)


MIXED = (0, 2, 1, 3)
T_PART, T_ROW, T_SLOT = 3, 7, 39


def start_weights(tab, pieces, lanes, target, sem):
    rows = pieces[0].shape[1]
    for p in range(8):
        slot = tab[T_SLOT + p]
        for j in range(4):
            row = pl.multiple_of(tab[T_ROW + p * 4 + j] * rows, 16)
            pltpu.make_async_copy(
                pieces[p].at[j, :, lanes], target.at[slot, pl.ds(row, rows), :], sem.at[slot]
            ).start()


def wait_weights(target, k, sem):
    pltpu.make_async_copy(target.at[k], target.at[k], sem.at[k]).wait()


def live_cotangent(tab, cot, g):
    _, block, width = cot.shape
    position = tab[2] + lax.broadcasted_iota(jnp.int32, (block, width), 0)
    return jnp.where(position < tab[g], cot[g].astype(F32), 0.0)


def mlp_in_kernel(tab, tok, cot, mod, gain, upb, *rest):
    mixed, pieces, rest = (rest[:4], rest[4:8]), rest[8:16], rest[16:]
    after, att, second_t, gbr, gbr_t, sums, act, slope, w, wo, second, sem, sem_o = rest
    groups, block, width = tok.shape
    feats = mixed[0][0].shape[0]
    fh = upb.shape[1]
    k = pl.program_id(0)

    @pl.when(k == 0)
    def _():
        start_weights(tab, pieces, slice(fh, None), wo, sem_o)
        start_weights(tab, pieces, slice(0, fh), w, sem)
        for g in range(groups):
            here = slice(g * block, (g + 1) * block)
            gb = (mod[g, 5:6, :] * live_cotangent(tab, cot, g)).astype(BF)
            gbr[here, :] = gb
            sums[g : g + 1, :] = jnp.sum(gb.astype(F32), axis=0, keepdims=True)
        gbr_t[...] = gbr[...].T
        for r in range(4):
            wait_weights(wo, r, sem_o)
        for g in range(groups):
            here = slice(g * block, (g + 1) * block)
            total = jnp.zeros((block, width), F32)
            for r in range(4):
                total += lax.dot_general(
                    mixed[g][MIXED[r]][...].T,
                    wo[r, :, :feats],
                    NT,
                    preferred_element_type=F32,
                )
            att[g] = total
            rows_after = tok[g].astype(F32) + mod[g, 2:3, :] * total
            after[g] = rows_after
            n, _ = norm_rows(rows_after)
            x = n * (gain[...] * (1.0 + mod[g, 4:5, :])) + mod[g, 3:4, :]
            second[here, :] = x.astype(BF)
        second_t[...] = second[...].T

    c1, c3 = math.sqrt(2.0 / math.pi), 0.044715
    wait_weights(w, k, sem)
    bias = upb[pl.ds(tab[T_PART + k], 1), :]
    hidden = jnp.dot(second[...], w[k], preferred_element_type=F32) + bias
    square = hidden * hidden
    th = jnp.tanh(c1 * hidden * (1.0 + c3 * square))
    up = 0.5 * (1.0 + th)
    act[0] = (hidden * up).astype(BF)
    slope[0] = (
        up + (0.5 * c1) * hidden * (1.0 - th * th) * (1.0 + (3.0 * c3) * square)
    ).astype(BF)


def mlp_out_kernel(tab, mod, downb, gbr, act, slope, *rest):
    pieces, late, rest = rest[:8], rest[8:10], rest[10:]
    out, sums, upsum, gh, w, branch, cot, after, sem, sem_late = rest
    groups, block, width = cot.shape
    k = pl.program_id(0)

    @pl.when(k == 0)
    def _():
        start_weights(tab, pieces, slice(None), w, sem)
        start_late(late, (cot, after), sem_late)
        branch[...] = jnp.broadcast_to(downb[...], branch.shape)

    wait_weights(w, k, sem)
    ga = jnp.dot(gbr[...], w[k], preferred_element_type=F32)
    grad = (ga * slope[0].astype(F32)).astype(BF)
    gh[0] = grad
    upsum[pl.ds(tab[T_PART + k], 1), :] = jnp.sum(grad.astype(F32), axis=0, keepdims=True)
    branch[...] += lax.dot_general(act[0], w[k], NT, preferred_element_type=F32)

    @pl.when(k == 3)
    def _():
        wait_late(late, (cot, after), sem_late)
        for g in range(groups):
            here = slice(g * block, (g + 1) * block)
            out[g] = (after[g] + mod[g, 5:6, :] * branch[here, :]).astype(BF)
            sums[g : g + 1, :] = jnp.sum(
                live_cotangent(tab, cot, g) * branch[here, :], axis=0, keepdims=True
            )


def start_late(sources, targets, sem):
    for i, (source, target) in enumerate(zip(sources, targets)):
        pltpu.make_async_copy(source, target, sem.at[i]).start()


def wait_late(sources, targets, sem):
    for i, (source, target) in enumerate(zip(sources, targets)):
        pltpu.make_async_copy(source, target, sem.at[i]).wait()


def mlp_back_kernel(tab, mod, gain, gh, *rest):
    pieces, late, rest = rest[:8], rest[8:11], rest[11:]
    gmixed, rest = rest[:4], rest[4:]
    sums, gafter, gat_t, w, wo, gsec, gat, cot, after, att, sem, sem_o, sem_late = rest
    groups, block, width = cot.shape
    feats = gmixed[0].shape[0]
    fh = gh.shape[2]
    k = pl.program_id(0)

    @pl.when(k == 0)
    def _():
        start_weights(tab, pieces, slice(0, fh), w, sem)
        start_weights(tab, pieces, slice(fh, None), wo, sem_o)
        start_late(late, (cot, after, att), sem_late)
        gsec[...] = jnp.zeros_like(gsec)

    wait_weights(w, k, sem)
    gsec[...] += lax.dot_general(gh[0], w[k], NT, preferred_element_type=F32)

    @pl.when(k == 3)
    def _():
        wait_late(late, (cot, after, att), sem_late)
        for r in range(4):
            wait_weights(wo, r, sem_o)
        for g in range(groups):
            here = slice(g * block, (g + 1) * block)
            n, inverse = norm_rows(after[g])
            gs = gsec[here, :]
            sums[g, 0:1, :] = jnp.sum(gs, axis=0, keepdims=True)
            sums[g, 1:2, :] = jnp.sum(gs * n, axis=0, keepdims=True)
            scaled = gs * (gain[...] * (1.0 + mod[g, 4:5, :]))
            mean = jnp.mean(scaled, axis=1, keepdims=True)
            along = jnp.mean(scaled * n, axis=1, keepdims=True)
            grad = live_cotangent(tab, cot, g) + inverse * (scaled - mean - n * along)
            gafter[g] = grad
            sums[g, 2:3, :] = jnp.sum(grad * att[g], axis=0, keepdims=True)
            low = (mod[g, 2:3, :] * grad).astype(BF)
            gat[here, :] = low
            for r in range(4):
                gmixed[MIXED[r]][:, here] = (
                    jnp.dot(low, wo[r, :, :feats], preferred_element_type=F32)
                    .astype(BF)
                    .T
                )
        gat_t[...] = gat[...].T


def steps_call(
    kernel, name, tab, arrays, stepped, pieces, late, outs, stepped_outs, scratch, sems, flops
):
    sm = pl.BlockSpec(memory_space=pltpu.SMEM)

    def slot_spec(shape):
        return spec((1,) + shape[1:], lambda k: (k, 0, 0))

    return pl.pallas_call(
        kernel,
        grid=(4,),
        in_specs=[sm]
        + [whole(a.shape) for a in arrays]
        + [slot_spec(a.shape) for a in stepped]
        + [ANY] * (len(pieces) + len(late)),
        out_specs=[whole(a.shape) for a in outs] + [slot_spec(a.shape) for a in stepped_outs],
        out_shape=list(outs) + list(stepped_outs),
        scratch_shapes=scratch
        + [pltpu.VMEM(a.shape, a.dtype) for a in late]
        + [pltpu.SemaphoreType.DMA((4,))] * sems,
        compiler_params=params(),
        cost_estimate=cost(flops, 16 * 2**20),
        name=name,
    )(tab, *arrays, *stepped, *pieces, *late)


def struct(shape, dtype):
    return jax.ShapeDtypeStruct(shape, dtype)


def mlp_in_call(tab, tok, cot, mod, gain, upb, mixed, pieces):
    groups, block, width = tok.shape
    total, fh = groups * block, upb.shape[1]
    rows = struct((groups, block, width), F32)
    tall = struct((width, total), BF)
    wide = struct((4, total, fh), BF)

    return steps_call(
        mlp_in_kernel,
        "mlp_in",
        tab,
        [tok, cot, mod, gain, upb, *mixed[0], *mixed[1]],
        [],
        pieces,
        [],
        [rows, rows, tall, struct((total, width), BF), tall, struct((groups, width), F32)],
        [wide, wide],
        [
            pltpu.VMEM((4, width, fh), BF),
            pltpu.VMEM((4, width, pieces[0].shape[2] - fh), BF),
            pltpu.VMEM((total, width), BF),
        ],
        2,
        10 * total * width * fh,
    )


def mlp_out_call(tab, cot, mod, downb, after, gbr, act, slope, pieces):
    groups, block, width = cot.shape
    total, fh = groups * block, act.shape[2]
    return steps_call(
        mlp_out_kernel,
        "mlp_out",
        tab,
        [mod, downb, gbr],
        [act, slope],
        pieces,
        [cot, after],
        [
            struct((groups, block, width), BF),
            struct((groups, width), F32),
            struct((4, fh), F32),
        ],
        [struct((4, total, fh), BF)],
        [pltpu.VMEM((4, width, fh), BF), pltpu.VMEM((total, width), F32)],
        2,
        16 * total * width * fh,
    )


def mlp_back_call(tab, cot, mod, gain, after, att, gh, pieces, feats):
    groups, block, width = cot.shape
    total, fh = groups * block, gh.shape[2]
    return steps_call(
        mlp_back_kernel,
        "mlp_back",
        tab,
        [mod, gain],
        [gh],
        pieces,
        [cot, after, att],
        [
            *[struct((feats, groups * block), BF)] * 4,
            struct((groups, 3, width), F32),
            struct((groups, block, width), F32),
            struct((width, total), BF),
        ],
        [],
        [
            pltpu.VMEM((4, width, fh), BF),
            pltpu.VMEM((4, width, pieces[0].shape[2] - fh), BF),
            pltpu.VMEM((total, width), F32),
            pltpu.VMEM((total, width), BF),
        ],
        3,
        10 * total * width * fh,
    )


def store_grads(tab, k, src, sent, kept0, kept1, sem):
    rows = src.shape[1] // NBLK
    for b in range(NBLK):
        there = tab[k * NBLK + b]
        piece = src.at[k, pl.ds(b * rows, rows), :]

        @pl.when(k >= 2)
        def _():
            pltpu.make_async_copy(piece, sent.at[there], sem.at[k, b]).start()

        @pl.when((k < 2) & (there < 8))
        def _():
            pltpu.make_async_copy(piece, kept0.at[there], sem.at[k, b]).start()

        @pl.when((k < 2) & (there >= 8))
        def _():
            pltpu.make_async_copy(piece, kept1.at[there - 8], sem.at[k, b]).start()


def wait_grads(src, sent, sem):
    rows = src.shape[1] // NBLK
    for k in range(4):
        for b in range(NBLK):
            pltpu.make_async_copy(
                src.at[k, pl.ds(b * rows, rows), :], sent.at[0], sem.at[k, b]
            ).wait()


def down_grad_kernel(tab, gbr_t, act, sent, kept0, kept1, acc, sem):
    k = pl.program_id(0)
    acc[k] = jnp.dot(gbr_t[...], act[0], preferred_element_type=F32).astype(BF)
    store_grads(tab, k, acc, sent, kept0, kept1, sem)

    @pl.when(k == 3)
    def _():
        wait_grads(acc, sent, sem)


def up_grad_kernel(tab, second_t, gat_t, gh, *rest):
    mixed, (sent, kept0, kept1, acc, sem) = (rest[:4], rest[4:8]), rest[8:]
    k = pl.program_id(0)
    fh = gh.shape[2]
    feats, block = mixed[0][0].shape
    acc[k, :, :fh] = jnp.dot(second_t[...], gh[0], preferred_element_type=F32).astype(BF)
    if acc.shape[2] > fh + feats:
        acc[k, :, fh + feats :] = jnp.zeros((acc.shape[1], acc.shape[2] - fh - feats), BF)
    for r in range(4):

        @pl.when(k == r)
        def _():
            total = None
            for g in range(2):
                term = lax.dot_general(
                    gat_t[:, g * block : (g + 1) * block],
                    mixed[g][MIXED[r]][...],
                    NT,
                    preferred_element_type=F32,
                )
                total = term if total is None else total + term
            acc[k, :, fh : fh + feats] = total.astype(BF)

    store_grads(tab, k, acc, sent, kept0, kept1, sem)

    @pl.when(k == 3)
    def _():
        wait_grads(acc, sent, sem)


def grad_call(kernel, name, tab, fixed, moving, others, lanes):
    width, total = fixed[0].shape
    fh = moving.shape[2]
    rows = width // NBLK
    grid_spec = pltpu.PrefetchScalarGridSpec(
        num_scalar_prefetch=1,
        grid=(4,),
        in_specs=[whole(a.shape) for a in fixed]
        + [spec((1, total, fh), lambda k, _: (k, 0, 0))]
        + [whole(a.shape) for a in others],
        out_specs=[ANY, ANY, ANY],
        scratch_shapes=[
            pltpu.VMEM((4, width, lanes), BF),
            pltpu.SemaphoreType.DMA((4, NBLK)),
        ],
    )
    return pl.pallas_call(
        kernel,
        grid_spec=grid_spec,
        out_shape=[struct((16, rows, lanes), BF)] + [struct((8, rows, lanes), BF)] * 2,
        compiler_params=params(),
        cost_estimate=cost(8 * width * total * lanes, 14 * 2**20),
        name=name,
    )(tab, *fixed, moving, *others)


def norm_back_kernel(t0, t1, t2, tok, after, mod, gain, out):
    normed, inverse = norm_rows(tok[0].astype(F32))
    grad = t0[0, 0].astype(F32) + t1[0, 0].astype(F32) + t2[0].astype(F32)
    scaled = grad * (gain[...] * (1.0 + mod[0, 1:2, :]))
    mean = jnp.mean(scaled, axis=1, keepdims=True)
    along = jnp.mean(scaled * normed, axis=1, keepdims=True)
    out[0] = (after[0] + inverse * (scaled - mean - normed * along)).astype(BF)


def norm_back_call(t0, t1, t2, tok, after, mod, gain):
    groups, block, width = tok.shape
    row = spec((1, block, width), lambda g: (g, 0, 0))
    near = spec((1, 1, block, width), lambda g: (0, g, 0, 0))
    return pl.pallas_call(
        norm_back_kernel,
        grid=(groups,),
        in_specs=[near, near, row, row, row, spec((1, 6, width), lambda g: (g, 0, 0)), whole((1, width))],
        out_specs=row,
        out_shape=jax.ShapeDtypeStruct((groups, block, width), BF),
        compiler_params=params(),
        cost_estimate=cost(40 * groups * block * width, 12 * groups * block * width),
        name="norm_back",
    )(t0, t1, t2, tok, after, mod, gain)


AT = 640


def pack_kernel(one, two, gate_two, upsum, down_bias, mod, gain_one, gain_two, out):
    dp, tp, _, width = out.shape
    groups = one.shape[0]
    lane = lax.broadcasted_iota(jnp.int32, (1, width), 1)

    def window(rows, start, count, at=0):
        row, offset = divmod(start, width)
        first = min(count, width - offset)
        got = rows[row]
        shift = (at - offset) % width
        got = pltpu.roll(got, shift, 1) if shift else got
        if first < count:
            shift = (at + first) % width
            rest = rows[row + 1]
            rest = pltpu.roll(rest, shift, 1) if shift else rest
            got = jnp.where(lane < at + first, got, rest)
        return got

    mods, count_mod = [], 6 * width // dp
    for g in range(groups):
        mods.append(
            [
                one[g, 0:1, :],
                gain_one[...] * one[g, 1:2, :],
                two[g, 2:3, :],
                two[g, 0:1, :],
                gain_two[...] * two[g, 1:2, :],
                gate_two[g : g + 1, :],
            ]
        )
    zero = jnp.zeros((1, width), F32)
    vectors = [zero, zero, zero]
    for g in range(groups):
        vectors[0] += down_bias[g : g + 1, :]
        vectors[1] += (1.0 + mod[g, 1:2, :]) * one[g, 1:2, :]
        vectors[2] += (1.0 + mod[g, 4:5, :]) * two[g, 1:2, :]
    rows_up = [upsum[r : r + 1, :] for r in range(upsum.shape[0])]
    count_up, count = upsum.shape[0] * width // dp, width // dp
    for d in range(dp):
        firsts = [window(mods[g], d * count_mod, count_mod) for g in range(groups)]
        firsts.append(window(rows_up, d * count_up, count_up))
        for r in range(3):
            row = jnp.where(lane < AT, firsts[r], window([vectors[r]], d * count, count, AT))
            for t in range(tp):
                out[d, t, r : r + 1, :] = row


def pack_call(dp, tp, one, two, gate_two, upsum, down_bias, mod, gain_one, gain_two):
    vm = pl.BlockSpec(memory_space=pltpu.VMEM)
    return pl.pallas_call(
        pack_kernel,
        in_specs=[vm] * 8,
        out_specs=vm,
        out_shape=struct((dp, tp, 3, one.shape[2]), F32),
        compiler_params=params(),
        cost_estimate=cost(1024, 1024),
        name="pack",
    )(one, two, gate_two, upsum, down_bias, mod, gain_one, gain_two)


def small_kernel(got, cond_t, adaw, adab, upb, downb, gain_one, gain_two):
    dp = got.shape[0]
    cols = adaw.shape[0]
    total = jnp.sum(got[...], axis=1)
    mods = jnp.concatenate([total[:, 0, :], total[:, 1, :]], axis=0)
    product = lax.dot_general(
        mods,
        cond_t[...],
        (((0,), (1,)), ((), ())),
        precision=lax.Precision.HIGHEST,
        preferred_element_type=F32,
    )
    adaw[...] = product[:cols]
    flat = jnp.sum(total, axis=0)
    adab[...] = (flat[0:1, :cols] + flat[1:2, :cols]).reshape(cols)
    upb[...] = flat[2:3, : upb.shape[0]].reshape(upb.shape[0])
    for row, ref in enumerate((downb, gain_one, gain_two)):
        ref[...] = flat[row : row + 1, AT : AT + ref.shape[0]].reshape(ref.shape[0])


def small_call(got, cond_t, cols, up_count, count):
    shapes = [(cols, cond_t.shape[0]), (cols,), (up_count,)] + [(count,)] * 3
    vm = pl.BlockSpec(memory_space=pltpu.VMEM)
    return pl.pallas_call(
        small_kernel,
        in_specs=[vm, vm],
        out_specs=[vm] * 6,
        out_shape=[jax.ShapeDtypeStruct(shape, F32) for shape in shapes],
        compiler_params=params(),
        cost_estimate=cost(1024, 1024),
        name="small",
    )(got, cond_t)


def time_embedding(time_steps, width_total):
    half_width = width_total // 2
    frequency = jnp.exp(-math.log(10000.0) * jnp.arange(half_width, dtype=F32) / half_width)
    angles = time_steps.astype(F32)[:, None] * frequency[None, :]
    return jnp.concatenate([jnp.cos(angles), jnp.sin(angles)], axis=-1)


def rotary_halves(length_total):
    half = HEAD // 2
    inverse = jnp.exp(-math.log(10000.0) * 2.0 * jnp.arange(half, dtype=F32) / HEAD)
    angles = jnp.arange(length_total, dtype=F32)[:, None] * inverse[None, :]
    return jnp.cos(angles), jnp.sin(angles)


def device_index(z, y, x, c):
    return ((z * 2 + y) * 2 + x) * 2 + c


def permutation(move):
    pairs = []
    for z in range(4):
        for y in range(2):
            for x in range(2):
                for c in range(2):
                    pairs.append((device_index(z, y, x, c), device_index(*move(z, y, x, c))))
    return pairs


CORE = permutation(lambda z, y, x, c: (z, y, x, 1 - c))
FLIP_X = permutation(lambda z, y, x, c: (z, y, 1 - x, c))
FLIP_BOTH = permutation(lambda z, y, x, c: (z, y, 1 - x, 1 - c))
FLIP_Y = permutation(lambda z, y, x, c: (z, 1 - y, x, c))
FIRST = permutation(lambda z, y, x, c: (z, 1 - y, x, c) if c == 0 else (z, y, 1 - x, c))
SECOND = permutation(lambda z, y, x, c: (z, y, 1 - x, c) if c == 0 else (z, 1 - y, x, c))
ALONG_Z = [permutation(lambda z, y, x, c, s=s: ((z + s) % 4, y, x, c)) for s in range(4)]


def send(array, pairs):
    return lax.ppermute(array, ("dp", "tensor"), pairs)


def start_z(shard):
    return [shard] + [send(shard, ALONG_Z[s]) for s in (1, 2, 3)]


def gather_z(shard):
    return jnp.stack(start_z(shard))


def after_all(value, *others):
    flat, tree = jax.tree.flatten(value)
    tied = lax.optimization_barrier((tuple(flat), others))[0]
    return jax.tree.unflatten(tree, tied)


def add_low(*terms):
    return functools.reduce(jnp.add, [term.astype(F32) for term in terms]).astype(BF)


def exchange(arrays, fast):
    if fast:
        perms = (None, CORE, FLIP_X, FLIP_BOTH)
        return [arrays[0]] + [send(arrays[r], perms[r]) for r in (1, 2, 3)]
    return list(lax.all_to_all(jnp.stack(arrays), "tensor", 0, 0, tiled=True))


class Reduce:
    def __init__(self, sent, kept0, kept1):
        shape = (2, 4) + sent.shape[1:]
        self.kept = kept0.reshape(shape), kept1.reshape(shape)
        self.got = send(sent, CORE).reshape((2,) + shape)

    def one(self, *others):
        got = after_all(self.got, *others) if others else self.got
        self.got = got
        self.half = add_low(self.kept[1], got[1])
        return self.half

    def two(self, *others):
        self.got_two = after_all(send(self.half, SECOND), *others)
        self.quarter = add_low(self.kept[0][1], self.got[0, 1], self.got_two[1])
        return self.quarter

    def start_three(self):
        self.got_three = send(self.quarter, FIRST)

    def three(self):
        self.parts = [
            add_low(self.kept[0][0, s], self.got[0, 0, s], self.got_two[0, s], self.got_three[s])
            for s in range(4)
        ]
        return self.parts

    def start_last(self):
        return [send(self.parts[s], ALONG_Z[s]) for s in (1, 2, 3)]

    def end_last(self, got):
        return functools.reduce(jnp.add, [g.astype(F32) for g in [self.parts[0]] + list(got)])


def tables(z, y, x, c):
    far_core = np.array([0, 0, 0, 0, 1, 1, 1, 1])
    kind = np.array([0, 1, 2, 3] * 2)
    core = jnp.bitwise_xor(c, far_core)
    rel_x = jnp.where(kind == 0, 0, jnp.where(kind == 3, 1, jnp.where(kind == 1, core, 1 - core)))
    rel_y = jnp.where(kind == 0, 0, jnp.where(kind == 3, 1, jnp.where(kind == 1, 1 - core, core)))
    slots = far_core * 2 + rel_x
    back = np.arange(4)
    from_z = jnp.remainder(z - back, 4)
    weight_rows = (from_z[None, :] * 2 + jnp.bitwise_xor(y, rel_y)[:, None]).reshape(32)
    slot = np.arange(4)
    parts = jnp.bitwise_xor(x, slot % 2) * 2 + jnp.bitwise_xor(c, slot // 2)
    block = np.arange(NBLK)
    to_z = jnp.remainder(block // 2 - z, 4)
    to_y = jnp.bitwise_xor(block % 2, y)
    slot_core = jnp.bitwise_xor(c, slot // 2)[:, None]
    to_x = (slot % 2)[:, None]
    major = jnp.where(slot_core == 0, to_x, to_y[None, :])
    minor = jnp.where(slot_core == 0, to_y[None, :], to_x)
    targets = (major * 8 + minor * 4 + to_z[None, :]).reshape(4 * NBLK)
    qkv_rows = jnp.concatenate(
        [from_z * 2 + y, from_z * 2 + (1 - y)]
    )
    qkv_targets = to_y * 4 + to_z
    return parts, weight_rows, slots, targets, qkv_rows, qkv_targets


def shards(
    tokens,
    lengths,
    times,
    cotangent,
    w_qkv,
    w_out,
    w_up,
    up_bias,
    w_down,
    down_bias,
    norm1_gain,
    norm2_gain,
    ada_weight,
    ada_bias,
):
    groups, block, width = tokens.shape
    dp, tp = lax.axis_size("dp"), lax.axis_size("tensor")
    seq = block * tp
    t = lax.axis_index("tensor")
    d = lax.axis_index("dp")
    fast = dp == 8 and tp == 4
    feats = w_qkv.shape[2]
    fh = w_up.shape[1]
    rows = width // NBLK
    zero = jnp.zeros((), jnp.int32)
    z, y, x, c = (d // 2, d % 2, t // 2, t % 2) if fast else (zero, zero, zero, zero)
    here = t if fast else zero

    all_times = lax.all_to_all(
        jnp.broadcast_to(times[None, :], (dp, groups)), "dp", 0, 0, tiled=True
    ).reshape(-1)
    pad = (-feats) % 128
    qkv_shard = jnp.pad(w_qkv, ((0, 0), (0, 0), (0, pad)))
    if fast:
        near = gather_z(qkv_shard)
        all_times = after_all(all_times, near)
        qkv_pieces = (near, send(near, FLIP_Y))
    else:
        full = lax.all_gather(qkv_shard, "dp", axis=1, tiled=True)
        full = full.reshape(3, NBLK, rows, feats + pad).transpose(1, 0, 2, 3)
        order = [[(-j) % 4 * 2 + p for j in range(4)] for p in range(2)]
        qkv_pieces = tuple(jnp.stack([full[b] for b in order[p]]) for p in range(2))
    tok_all = lax.all_gather(tokens, "tensor", axis=1, tiled=True)

    condition = time_embedding(all_times, ada_weight.shape[0])
    part = jnp.dot(
        condition, ada_weight.astype(F32), precision=lax.Precision.HIGHEST
    ) + ada_bias.astype(F32)
    cols = part.shape[1]
    vectors = jnp.concatenate([up_bias, down_bias, norm1_gain, norm2_gain]).astype(F32)
    sent_mod = jnp.concatenate(
        [
            part.reshape(dp, groups * cols),
            jnp.broadcast_to(vectors[None, :], (dp, vectors.shape[0])),
        ],
        axis=1,
    )
    payload = lax.all_to_all(sent_mod, "dp", 0, 0, tiled=True)
    lengths, z, y, x, c, t, here, late_condition = after_all(
        (lengths, z, y, x, c, t, here, condition), sent_mod
    )
    parts, weight_rows, slots, targets, qkv_rows, qkv_targets = tables(z, y, x, c)
    cos, sin = rotary_halves(seq)
    ready = (
        qkv_rows.astype(jnp.int32),
        jnp.concatenate([lengths, here.reshape(1)]).astype(jnp.int32),
        jnp.concatenate([lengths, (t * block).reshape(1), parts, weight_rows, slots]).astype(
            jnp.int32
        ),
        targets.astype(jnp.int32),
        jnp.concatenate([qkv_targets, here.reshape(1)]).astype(jnp.int32),
        late_condition.reshape(dp, groups, -1).transpose(2, 1, 0).reshape(-1, dp * groups),
        jnp.concatenate([cos, cos] * 2, axis=1),
        jnp.concatenate([-sin, sin] * 2, axis=1),
        cos.T,
        sin.T,
    )
    payload, ready, qkv_pieces = after_all((payload, ready, qkv_pieces))
    qkv_rows, small_tab, tab, targets, back_tab, cond_t, cos_wide, sin_wide, cos_t, sin_t = ready
    mod = (
        payload[:, : groups * cols]
        .reshape(dp, groups, cols)
        .transpose(1, 0, 2)
        .reshape(groups, 6, width)
    )
    at = groups * cols
    small = []
    for count in (up_bias.shape[0], down_bias.shape[0], norm1_gain.shape[0], norm2_gain.shape[0]):
        small.append(payload[:, at : at + count].reshape(-1))
        at += count
    upb_all = small[0].reshape(tp, fh)
    downb_all, gain_one, gain_two = (v.reshape(1, width) for v in small[1:])

    up_shard = jnp.pad(
        jnp.concatenate([w_up, w_out.T], axis=1), ((0, 0), (0, (-fh - feats) % 128))
    )
    down_shard = w_down.T
    if fast:
        up_shard, down_shard = after_all((up_shard, down_shard), qkv_pieces[1], payload)
        up_parts = start_z(up_shard)
        down_parts = start_z(down_shard)
    else:

        def gather_pieces(shard):
            full = lax.all_gather(shard, "dp", axis=0, tiled=True)
            full = lax.all_gather(full, "tensor", axis=0, tiled=False)
            full = full.reshape(tp, NBLK, rows, full.shape[2])
            return [
                jnp.stack([full[rel_x * 2 + far, b] for b in order[rel_y]])
                for far in range(2)
                for rel_x, rel_y in ((0, 0), (far, 1 - far), (1 - far, far), (1, 1))
            ]

    q, k, v, kt, vt, w_all = qkv_call(
        qkv_rows, tok_all, mod, gain_one, cos_wide, sin_wide, *qkv_pieces
    )
    vt_later = vt
    if fast:
        up_near = jnp.stack(after_all(up_parts, vt))
        vt = after_all(vt, up_near)
        up_one, up_two = send(up_near, FIRST), send(up_near, SECOND)
    *mixed0, probs0, scale0 = attend_call(0, small_tab, q, k, vt)
    if fast:
        mixed0, up_near, up_one, up_two, down_parts = after_all(
            (mixed0, up_near, up_one, up_two, down_parts), probs0
        )
        vt_later = after_all(vt, up_one, up_two)
        mixed0_all = exchange(mixed0, fast)
        up_both = send(up_one, SECOND)
        up_far = [send(piece, CORE) for piece in (up_near, up_one, up_two)]
    *mixed1, probs1, scale1 = attend_call(1, small_tab, q, k, vt_later)
    if fast:
        mixed1, up_both = after_all((mixed1, up_both), probs1, *mixed0_all)
        mixed1 = after_all(mixed1, up_both)
        up_far.append(send(up_both, CORE))
        up_pieces = [up_near, up_one, up_two, up_both] + up_far
    else:
        up_pieces, down_pieces = gather_pieces(up_shard), gather_pieces(down_shard)
        mixed0_all = exchange(mixed0, fast)
    mixed1_all = exchange(mixed1, fast)

    if fast:
        down_parts, up_pieces = after_all((down_parts, up_pieces), *mixed1_all)
        down_near = jnp.stack(down_parts)
        up_pieces = after_all(up_pieces, down_near)
        down_one, down_two = send(down_near, FIRST), send(down_near, SECOND)
    after, att, second_t, gbr, gbr_t, sum_down_bias, act, slope = mlp_in_call(
        tab, tokens, cotangent, mod, gain_two, upb_all, (mixed0_all, mixed1_all), up_pieces
    )
    if fast:
        down_one, down_two, act = after_all((down_one, down_two, act), after)
        act = after_all(act, down_one, down_two)
        down_both = send(down_one, SECOND)
        down_far = [send(piece, CORE) for piece in (down_near, down_one, down_two)]
    gd_s, *gd_k = grad_call(down_grad_kernel, "down_grad", targets, [gbr_t], act, [], fh)
    if fast:
        gd_s, down_both, down_far = after_all((gd_s, down_both, down_far), *gd_k)
        gd_s = after_all(gd_s, down_both, *down_far)
        down_far.append(send(down_both, CORE))
        down_sum = Reduce(after_all(gd_s, down_far[3]), *gd_k)
        down_pieces = [down_near, down_one, down_two, down_both] + down_far
    out, sum_gate_two, upsum, gh = mlp_out_call(
        tab, cotangent, mod, downb_all, after, gbr, act, slope, down_pieces
    )
    if fast:
        gh = after_all(gh, down_sum.one(gh))
    *gms, sums_two, grad_after, gat_t = mlp_back_call(
        tab, cotangent, mod, gain_two, after, att, gh, up_pieces, feats
    )
    if fast:
        gms, gh = after_all((gms, gh), grad_after)
    gm = exchange(gms, fast)
    gu_s, *gu_k = grad_call(
        up_grad_kernel,
        "up_grad",
        targets,
        [second_t, gat_t],
        gh,
        [*mixed0_all, *mixed1_all],
        up_pieces[0].shape[2],
    )
    if fast:
        down_sum.two(*gu_k)
        gu_s = after_all(gu_s, down_sum.got_two, *gm)
        up_sum = Reduce(gu_s, *gu_k)
        gm = after_all(gm, up_sum.one(*gu_k))
    grad_t0 = attend_back_call(0, small_tab, q, kt, v, probs0, scale0, gm, cos_t, sin_t)
    if fast:
        down_sum.quarter, quarter = after_all((down_sum.quarter, up_sum.two(grad_t0)), grad_t0)
        up_sum.quarter = quarter
        gm = after_all(gm, quarter, down_sum.quarter)
    grad_t1 = attend_back_call(1, small_tab, q, kt, v, probs1, scale1, gm, cos_t, sin_t)
    if fast:
        down_sum.start_three()
        up_sum.start_three()
        down_sum.got_three, up_sum.got_three = after_all(
            (down_sum.got_three, up_sum.got_three), grad_t1
        )
        down_parts = down_sum.three()
        down_got = down_sum.start_last()
        grad_t1 = after_all(grad_t1, *down_parts)
    fts, ftk, sums_one, dws, dwk = qkv_back_call(
        back_tab,
        grad_t0,
        grad_t1,
        tok_all,
        w_all,
        mod,
        gain_one,
    )

    if fast:
        fts, dws, up_sum.got_three, down_got = after_all((fts, dws, up_sum.got_three, down_got))
        up_sum.three()
        got, got_dw = send(fts, CORE), send(dws, FLIP_Y)
        got = after_all(got, *up_sum.parts)
        up_got = up_sum.start_last()
        far = add_low(ftk[1], got[1])
        sums_one, sums_two = after_all((sums_one, sums_two), far, up_got[0])
        far = send(far, FLIP_X)
    else:

        def absolute(sent, kept):
            lanes = sent.shape[2]
            near = kept.reshape(2, 2, 4, rows, lanes)
            far = sent.reshape(2, 2, 4, rows, lanes).transpose(1, 0, 2, 3, 4)
            both = jnp.stack([near, far], axis=1)
            return both.transpose(0, 1, 3, 2, 4, 5).reshape(tp, width, lanes).astype(F32)

        def reduce_all(sent, kept):
            terms = lax.psum_scatter(
                absolute(sent, kept), "tensor", scatter_dimension=0, tiled=True
            )[0]
            return lax.psum_scatter(terms, "dp", scatter_dimension=0, tiled=True)

        sum_up = reduce_all(gu_s, jnp.concatenate(gu_k))
        sum_down = reduce_all(gd_s, jnp.concatenate(gd_k))
        terms = jnp.stack([dwk, dws]).transpose(2, 1, 0, 3, 4)
        terms = terms.reshape(3, width, feats + pad).astype(F32)
        sum_qkv = lax.psum_scatter(terms, "dp", scatter_dimension=1, tiled=True)
        terms = jnp.stack([ftk, fts], axis=1).reshape(tp, groups, block, width).astype(F32)
        grad_first = lax.psum_scatter(terms, "tensor", scatter_dimension=0, tiled=True)[0]
        nought = jnp.zeros_like(grad_first)
        grad_in = norm_back_call(
            grad_first[None], nought[None], nought, tokens, grad_after, mod, gain_one
        )

    up_count, count = up_bias.shape[0], down_bias.shape[0]
    payload = pack_call(
        dp,
        tp,
        sums_one,
        sums_two,
        sum_gate_two,
        upsum,
        sum_down_bias,
        mod,
        gain_one,
        gain_two,
    ).reshape(dp * tp, 3, width)
    payload = lax.all_to_all(payload, ("dp", "tensor"), 0, 0, tiled=True)
    if fast:
        dw_parts = [add_low(dwk[s], got_dw[s]) for s in range(4)]
        dw_got = [send(dw_parts[s], ALONG_Z[s]) for s in (1, 2, 3)]
        far, up_got = after_all((far, up_got), *dw_parts)
        grad_in = norm_back_call(ftk, got, far, tokens, grad_after, mod, gain_one)
        payload = after_all(payload, grad_in)
    grad_adaw, grad_adab, g_up, g_down, g_one, g_two = small_call(
        payload.reshape(dp, tp, 3, width), cond_t, cols, up_count, count
    )
    if fast:
        dw_got = after_all(dw_got, grad_adaw)
        sum_up = up_sum.end_last(up_got)
        sum_down = down_sum.end_last(down_got)
        sum_qkv = functools.reduce(jnp.add, [g.astype(F32) for g in [dw_parts[0]] + dw_got])

    return (
        out,
        grad_in,
        sum_qkv[:, :, :feats],
        sum_up[:, fh : fh + feats].T,
        sum_up[:, :fh],
        g_up,
        sum_down.T,
        g_down,
        g_one,
        g_two,
        grad_adaw.T,
        grad_adab,
    )


def solution(mesh):
    in_specs = (
        P("dp", "tensor", None),
        P("dp"),
        P("dp"),
        P("dp", "tensor", None),
        P(None, "dp", "tensor"),
        P("tensor", "dp"),
        P("dp", "tensor"),
        P("dp"),
        P("tensor", "dp"),
        P("dp"),
        P("dp"),
        P("dp"),
        P(None, "dp"),
        P("dp"),
    )
    out_specs = (
        P("dp", "tensor", None),
        P("dp", "tensor", None),
        P(None, "dp", "tensor"),
        P("tensor", "dp"),
        P("dp", "tensor"),
        P("dp"),
        P("tensor", "dp"),
        P("dp"),
        P("dp"),
        P("dp"),
        P(None, "dp"),
        P("dp"),
    )
    return jax.shard_map(shards, mesh=mesh, in_specs=in_specs, out_specs=out_specs, check_vma=False)
```

```python
import functools
import math

import jax
import jax.numpy as jnp
import numpy as np
from jax import lax
from jax.experimental import pallas as pl
from jax.experimental.pallas import tpu as pltpu
from jax.sharding import PartitionSpec as P

HEAD = 64
EPS = 1e-05
MASKED = -1e30
BF = jnp.bfloat16
F32 = jnp.float32
VMEM_MAX = 60 * 1024 * 1024
NBLK = 8
NT = (((1,), (1,)), ((), ()))


def spec(block, index_map):
    return pl.BlockSpec(block, index_map)


def whole(shape):
    return pl.BlockSpec(shape, lambda *_: (0,) * len(shape))


ANY = pl.BlockSpec(memory_space=pl.ANY)


def params():
    return pltpu.CompilerParams(vmem_limit_bytes=VMEM_MAX)


def cost(flops, moved, trans=0):
    return pl.CostEstimate(flops=flops, bytes_accessed=moved, transcendentals=trans)


def norm_rows(rows):
    centered = rows - jnp.mean(rows, axis=1, keepdims=True)
    variance = jnp.mean(centered * centered, axis=1, keepdims=True)
    inverse = lax.rsqrt(variance + EPS)
    return centered * inverse, inverse


def first_rows(tok, shift, scale, gain):
    normed, _ = norm_rows(tok.astype(F32))
    return (normed * (gain * (1.0 + scale)) + shift).astype(BF), normed


def qkv_kernel(tab, tok, mod, gain, cos, sin, w0, w1, q, k, v, kt, vt, w, sem):
    groups, heads, block = q.shape[:3]
    rows, wide = w0.shape[2], w.shape[2]

    @pl.when(pl.program_id(0) == 0)
    def _():
        copies = []
        for p, ref in enumerate((w0, w1)):
            for j in range(4):
                row = pl.multiple_of(tab[p * 4 + j] * rows, 16)
                copies.append(
                    pltpu.make_async_copy(
                        ref.at[j], w.at[:, pl.ds(row, rows), :], sem.at[p * 4 + j]
                    )
                )
        for copy in copies:
            copy.start()
        for copy in copies:
            copy.wait()

    low = lax.rem(lax.broadcasted_iota(jnp.int32, (block, wide), 1), HEAD) < HEAD // 2
    cos_wide = jnp.concatenate([cos[...]] * (wide // 128), axis=1)
    sin_wide = jnp.concatenate([sin[...]] * (wide // 128), axis=1)

    def rotate(vec):
        turned = jnp.where(
            low, pltpu.roll(vec, wide - HEAD // 2, 1), pltpu.roll(vec, HEAD // 2, 1)
        )
        return vec * cos_wide + turned * sin_wide

    for g in range(groups):

        def store_heads(ref, vec):
            for h in range(heads):
                shifted = vec if h == 0 else pltpu.roll(vec, wide - h * HEAD, 1)
                ref[g, h] = shifted[:, :HEAD].astype(BF)

        x, _ = first_rows(tok[g], mod[g, 0:1, :], mod[g, 1:2, :], gain[...])
        query = rotate(jnp.dot(x, w[0], preferred_element_type=F32))
        store_heads(q, query * (HEAD**-0.5))
        key = rotate(jnp.dot(x, w[1], preferred_element_type=F32))
        store_heads(k, key)
        kt[g] = key.T[: heads * HEAD].astype(BF)
        value = jnp.dot(x, w[2], preferred_element_type=F32)
        store_heads(v, value)
        vt[g] = value.T[: heads * HEAD].astype(BF)


def qkv_call(tab, tok_all, mod, gain, cos, sin, w0, w1):
    groups, seq, width = tok_all.shape
    block = seq // 4
    wide = w0.shape[3]
    heads = (wide // HEAD) * 3 // 4
    feats = heads * HEAD
    by_head = spec((groups, heads, block, HEAD), lambda j, _: (0, 0, j, 0))
    by_feat = spec((groups, feats, block), lambda j, _: (0, 0, j))
    grid_spec = pltpu.PrefetchScalarGridSpec(
        num_scalar_prefetch=1,
        grid=(4,),
        in_specs=[
            spec((groups, block, width), lambda j, _: (0, j, 0)),
            whole((groups, 6, width)),
            whole((1, width)),
            spec((block, 128), lambda j, _: (j, 0)),
            spec((block, 128), lambda j, _: (j, 0)),
            ANY,
            ANY,
        ],
        out_specs=[by_head, by_head, by_head, by_feat, by_feat, whole((3, width, wide))],
        scratch_shapes=[pltpu.SemaphoreType.DMA((8,))],
    )
    head_shape = jax.ShapeDtypeStruct((groups, heads, seq, HEAD), BF)
    turned = jax.ShapeDtypeStruct((groups, feats, seq), BF)
    return pl.pallas_call(
        qkv_kernel,
        grid_spec=grid_spec,
        out_shape=[
            head_shape,
            head_shape,
            head_shape,
            turned,
            turned,
            jax.ShapeDtypeStruct((3, width, wide), BF),
        ],
        compiler_params=params(),
        cost_estimate=cost(2 * groups * seq * width * wide * 3, 16 * 2**20),
        name="qkv",
    )(tab, tok_all, mod, gain, cos, sin, w0, w1)


CHUNK = 128
LEAST = 256


def unrolled(count, step, carried):
    for i in range(count):
        carried = step(i, carried)
    return carried


def eights(rows, op):
    return op(rows.reshape(rows.shape[0] // 8, 8, rows.shape[1]), axis=0)


def attend_kernel(tab, q, k, vt, mix0, mix1, mix2, mix3, probs, inverse, raw, mixed, *, group):
    heads = k.shape[1]
    block = q.shape[2]
    length = tab[group]
    chunks = k.shape[2] // CHUNK
    position = lax.broadcasted_iota(jnp.int32, (CHUNK, block), 0)

    def head(h, _):
        query = q[0, h]

        def score(c, largest):
            rows = slice(c * CHUNK, (c + 1) * CHUNK)
            scores = lax.dot_general(k[0, h, rows, :], query, NT, preferred_element_type=F32)
            if (c + 1) * CHUNK > LEAST:
                scores = jnp.where(position < length - c * CHUNK, scores, MASKED)
            raw[rows, :] = scores
            return jnp.maximum(largest, eights(scores, jnp.max))

        largest = unrolled(chunks, score, jnp.full((8, block), MASKED, F32))
        largest = jnp.max(largest, axis=0, keepdims=True)
        here = pl.ds(pl.multiple_of(h * HEAD, HEAD), HEAD)

        def weigh(c, carried):
            total, out = carried
            rows = slice(c * CHUNK, (c + 1) * CHUNK)
            weights = jnp.exp(raw[rows, :] - largest)
            low = weights.astype(BF)
            probs[h, rows, :] = low
            out = out + jnp.dot(vt[0, here, rows], low, preferred_element_type=F32)
            return total + eights(weights, jnp.sum), out

        total, out = unrolled(
            chunks, weigh, (jnp.zeros((8, block), F32), jnp.zeros((HEAD, block), F32))
        )
        scale = 1.0 / jnp.sum(total, axis=0, keepdims=True)
        inverse[h] = scale
        mixed[here, :] = (out * scale).astype(BF)
        return 0

    unrolled(heads, head, 0)
    for r, ref in enumerate((mix0, mix1, mix2, mix3)):

        @pl.when(turn(pl.program_id(0)) == r)
        def _():
            ref[...] = mixed[...]


def turn(step):
    return lax.rem(step + 1, 4)


def attend_call(group, tab, q, k, vt):
    _, heads, seq, _ = q.shape
    block = seq // 4
    feats = heads * HEAD

    def piece(i, tab):
        return lax.bitwise_xor(tab[2], turn(i))

    grid_spec = pltpu.PrefetchScalarGridSpec(
        num_scalar_prefetch=1,
        grid=(4,),
        in_specs=[
            spec((1, heads, block, HEAD), lambda i, tab: (group, 0, piece(i, tab), 0)),
            spec((1, heads, seq, HEAD), lambda i, tab: (group, 0, 0, 0)),
            spec((1, feats, seq), lambda i, tab: (group, 0, 0)),
        ],
        out_specs=[
            *[whole((feats, block))] * 4,
            spec((heads, seq, block), lambda i, tab: (0, 0, piece(i, tab))),
            spec((heads, 1, block), lambda i, tab: (0, 0, piece(i, tab))),
        ],
        scratch_shapes=[pltpu.VMEM((seq, block), F32), pltpu.VMEM((feats, block), BF)],
    )
    return pl.pallas_call(
        functools.partial(attend_kernel, group=group),
        grid_spec=grid_spec,
        out_shape=[
            *[jax.ShapeDtypeStruct((feats, block), BF)] * 4,
            jax.ShapeDtypeStruct((heads, seq, seq), BF),
            jax.ShapeDtypeStruct((heads, 1, seq), F32),
        ],
        compiler_params=params(),
        cost_estimate=cost(16 * heads * seq * seq * HEAD, 10 * 2**20, heads * seq * seq),
        name="attend",
    )(tab, q, k, vt)


def attend_back_kernel(
    tab, q, kt, v, probs, inverse, gm0, gm1, gm2, gm3, cos, sin, out, dk, dv, gm
):
    heads, block = q.shape[1], q.shape[2]
    half = HEAD // 2
    step = pl.program_id(0)
    j = lax.bitwise_xor(tab[2], step)

    @pl.when(step == 0)
    def _():
        dk[...] = jnp.zeros_like(dk)
        dv[...] = jnp.zeros_like(dv)
        for r, ref in enumerate((gm0, gm1, gm2, gm3)):
            gm[r] = ref[...]

    columns = pl.ds(pl.multiple_of(j * block, 128), block)
    cos_here, sin_here = cos[:, columns], sin[:, columns]

    def store_turned(plane, h, vec, c, s, where):
        low, high = vec[:half], vec[half:]
        base = pl.multiple_of(h * HEAD, HEAD)
        out[plane, pl.ds(base, half), where] = (low * c + high * s).astype(BF)
        out[plane, pl.ds(base + half, half), where] = (high * c - low * s).astype(BF)

    def head(h, _):
        here = pl.ds(pl.multiple_of(h * HEAD, HEAD), HEAD)
        scale = inverse[h]
        grad = (gm[step, here, :].astype(F32) * scale).astype(BF)
        query = q[0, h]

        low = probs[h]
        dp = jnp.dot(v[0, h], grad, preferred_element_type=F32)
        soft = low.astype(F32)
        prod = soft * dp
        inner = jnp.sum(prod, axis=0, keepdims=True) * scale
        ds = (prod - soft * inner).astype(BF)
        dv[h] += lax.dot_general(low, grad, NT, preferred_element_type=F32)
        dk[h] += jnp.dot(ds, query, preferred_element_type=F32)
        dq = jnp.dot(kt[0, here, :], ds, preferred_element_type=F32)
        store_turned(0, h, dq * (HEAD**-0.5), cos_here, sin_here, columns)
        return 0

    unrolled(heads, head, 0)

    @pl.when(step == pl.num_programs(0) - 1)
    def _():
        def turn_keys(h, _):
            store_turned(1, h, dk[h].T, cos[...], sin[...], slice(None))
            out[2, pl.ds(pl.multiple_of(h * HEAD, HEAD), HEAD), :] = dv[h].T.astype(BF)
            return 0

        unrolled(heads, turn_keys, 0)


def attend_back_call(group, tab, q, kt, v, probs, inverse, gm, cos, sin):
    _, heads, seq, _ = q.shape
    block = seq // 4
    feats = heads * HEAD
    half = HEAD // 2

    def piece(i, tab):
        return lax.bitwise_xor(tab[2], i)

    grid_spec = pltpu.PrefetchScalarGridSpec(
        num_scalar_prefetch=1,
        grid=(4,),
        in_specs=[
            spec((1, heads, block, HEAD), lambda i, tab: (group, 0, piece(i, tab), 0)),
            spec((1, feats, seq), lambda i, tab: (group, 0, 0)),
            spec((1, heads, seq, HEAD), lambda i, tab: (group, 0, 0, 0)),
            spec((heads, seq, block), lambda i, tab: (0, 0, piece(i, tab))),
            spec((heads, 1, block), lambda i, tab: (0, 0, piece(i, tab))),
            *[spec((feats, block), lambda i, tab: (0, group))] * 4,
            whole((half, seq)),
            whole((half, seq)),
        ],
        out_specs=whole((3, feats, seq)),
        scratch_shapes=[
            pltpu.VMEM((heads, seq, HEAD), F32),
            pltpu.VMEM((heads, seq, HEAD), F32),
            pltpu.VMEM((4, feats, block), BF),
        ],
    )
    return pl.pallas_call(
        attend_back_kernel,
        grid_spec=grid_spec,
        out_shape=jax.ShapeDtypeStruct((3, feats, seq), BF),
        compiler_params=params(),
        cost_estimate=cost(32 * heads * seq * seq * HEAD, 10 * 2**20),
        name="attend_back",
    )(tab, q, kt, v, probs, inverse, *gm, cos, sin)


def qkv_back_kernel(tab, gt0, gt1, tok, w, mod, gain, fts, ftk, sums, dws, dwk, acc):
    i = pl.program_id(0)
    feats, block = gt0.shape[1], gt0.shape[2]
    wide, width = w.shape[2], w.shape[1]
    rows = dws.shape[2]

    @pl.when(i == 0)
    def _():
        acc[...] = jnp.zeros_like(acc)
        sums[...] = jnp.zeros_like(sums)

    for g, gt in enumerate((gt0, gt1)):
        first, normed = first_rows(tok[g], mod[g, 0:1, :], mod[g, 1:2, :], gain[...])
        total = None
        for j in range(3):
            part = gt[j]
            tall = part.astype(F32)
            if wide > feats:
                tall = jnp.concatenate([tall, jnp.zeros((wide - feats, block), F32)], axis=0)
            term = lax.dot_general(tall.T.astype(BF), w[j], NT, preferred_element_type=F32)
            total = term if total is None else total + term
            acc[j, :feats] += jnp.dot(part, first, preferred_element_type=F32)
        sums[g, 0:1, :] += jnp.sum(total, axis=0, keepdims=True)
        sums[g, 1:2, :] += jnp.sum(total * normed, axis=0, keepdims=True)
        low = total.astype(BF)

        @pl.when(i < 2)
        def _():
            fts[0, g] = low

        @pl.when(i >= 2)
        def _():
            ftk[0, g] = low

    @pl.when(i == pl.num_programs(0) - 1)
    def _():
        for j in range(3):
            flat = acc[j].T.astype(BF)
            for b in range(NBLK):
                part = flat[b * rows : (b + 1) * rows]
                there = tab[b]

                @pl.when(there < NBLK // 2)
                def _():
                    dwk[there, j] = part

                @pl.when(there >= NBLK // 2)
                def _():
                    dws[there - NBLK // 2, j] = part


def qkv_back_call(tab, gt0, gt1, tok_all, w, mod, gain):
    _, feats, seq = gt0.shape
    groups = tok_all.shape[0]
    block = seq // 4
    width = tok_all.shape[2]
    wide = w.shape[2]
    rows = width // NBLK

    def piece(i, tab):
        return lax.bitwise_xor(tab[NBLK], lax.rem(i, 2) * 2 + (1 - i // 2))

    by_feat = spec((3, feats, block), lambda i, tab: (0, 0, piece(i, tab)))
    grid_spec = pltpu.PrefetchScalarGridSpec(
        num_scalar_prefetch=1,
        grid=(4,),
        in_specs=[
            by_feat,
            by_feat,
            spec((groups, block, width), lambda i, tab: (0, piece(i, tab), 0)),
            whole((3, width, wide)),
            whole((groups, 6, width)),
            whole((1, width)),
        ],
        out_specs=[
            spec((1, groups, block, width), lambda i, tab: (jnp.minimum(i, 1), 0, 0, 0)),
            spec((1, groups, block, width), lambda i, tab: (jnp.maximum(i - 2, 0), 0, 0, 0)),
            whole((groups, 2, width)),
            whole((NBLK // 2, 3, rows, wide)),
            whole((NBLK // 2, 3, rows, wide)),
        ],
        scratch_shapes=[pltpu.VMEM((3, wide, width), F32)],
    )
    terms = jax.ShapeDtypeStruct((2, groups, block, width), BF)
    share = jax.ShapeDtypeStruct((NBLK // 2, 3, rows, wide), BF)
    return pl.pallas_call(
        qkv_back_kernel,
        grid_spec=grid_spec,
        out_shape=[terms, terms, jax.ShapeDtypeStruct((groups, 2, width), F32), share, share],
        compiler_params=params(),
        cost_estimate=cost(4 * groups * seq * width * wide * 3, 16 * 2**20),
        name="qkv_back",
    )(tab, gt0, gt1, tok_all, w, mod, gain)


MIXED = (0, 2, 1, 3)
T_PART, T_ROW, T_SLOT = 3, 7, 39


def start_weights(tab, pieces, lanes, target, sem):
    rows = pieces[0].shape[1]
    for p in range(8):
        slot = tab[T_SLOT + p]
        for j in range(4):
            row = pl.multiple_of(tab[T_ROW + p * 4 + j] * rows, 16)
            pltpu.make_async_copy(
                pieces[p].at[j, :, lanes], target.at[slot, pl.ds(row, rows), :], sem.at[slot]
            ).start()


def wait_weights(target, k, sem):
    pltpu.make_async_copy(target.at[k], target.at[k], sem.at[k]).wait()


def live_cotangent(tab, cot, g):
    _, block, width = cot.shape
    position = tab[2] + lax.broadcasted_iota(jnp.int32, (block, width), 0)
    return jnp.where(position < tab[g], cot[g].astype(F32), 0.0)


def mlp_in_kernel(tab, tok, cot, mod, gain, upb, *rest):
    mixed, pieces, rest = (rest[:4], rest[4:8]), rest[8:16], rest[16:]
    sent, rest = rest[:4], rest[4:]
    sums, act, slope, w, wo, second, after, att, second_t, gbr_t, sem, sem_o, sem_s = rest
    groups, block, width = tok.shape
    feats = mixed[0][0].shape[0]
    fh = upb.shape[1]
    k = pl.program_id(0)

    @pl.when(k == 0)
    def _():
        start_weights(tab, pieces, slice(fh, None), wo, sem_o)
        start_weights(tab, pieces, slice(0, fh), w, sem)
        for g in range(groups):
            here = slice(g * block, (g + 1) * block)
            gb = (mod[g, 5:6, :] * live_cotangent(tab, cot, g)).astype(BF)
            gbr_t[:, here] = gb.T
            sums[g : g + 1, :] = jnp.sum(gb.astype(F32), axis=0, keepdims=True)
        for r in range(4):
            wait_weights(wo, r, sem_o)
        for g in range(groups):
            here = slice(g * block, (g + 1) * block)
            total = jnp.zeros((block, width), F32)
            for r in range(4):
                total += lax.dot_general(
                    mixed[g][MIXED[r]][...].T,
                    wo[r, :, :feats],
                    NT,
                    preferred_element_type=F32,
                )
            att[g] = total.astype(BF)
            rows_after = tok[g].astype(F32) + mod[g, 2:3, :] * total
            after[g] = rows_after
            n, _ = norm_rows(rows_after)
            x = n * (gain[...] * (1.0 + mod[g, 4:5, :])) + mod[g, 3:4, :]
            second[here, :] = x.astype(BF)
        second_t[...] = second[...].T
        start_late((after, att, second_t, gbr_t), sent, sem_s)

    @pl.when(k == 3)
    def _():
        wait_late((after, att, second_t, gbr_t), sent, sem_s)

    c1, c3 = math.sqrt(2.0 / math.pi), 0.044715
    wait_weights(w, k, sem)
    bias = upb[pl.ds(tab[T_PART + k], 1), :]
    hidden = jnp.dot(second[...], w[k], preferred_element_type=F32) + bias
    square = hidden * hidden
    th = jnp.tanh(c1 * hidden * (1.0 + c3 * square))
    up = 0.5 * (1.0 + th)
    act[0] = (hidden * up).astype(BF)
    slope[0] = (
        up + (0.5 * c1) * hidden * (1.0 - th * th) * (1.0 + (3.0 * c3) * square)
    ).astype(BF)


def mlp_out_kernel(tab, mod, downb, cot, act, slope, *rest):
    pieces, late, rest = rest[:8], rest[8:9], rest[9:]
    out, sums, upsum, gh, w, branch, gbr, after, sem, sem_late = rest
    groups, block, width = cot.shape
    k = pl.program_id(0)

    @pl.when(k == 0)
    def _():
        start_weights(tab, pieces, slice(None), w, sem)
        start_late(late, (after,), sem_late)
        for g in range(groups):
            grad_branch = mod[g, 5:6, :] * live_cotangent(tab, cot, g)
            gbr[g * block : (g + 1) * block, :] = grad_branch.astype(BF)
        branch[...] = jnp.broadcast_to(downb[...], branch.shape)

    wait_weights(w, k, sem)
    ga = jnp.dot(gbr[...], w[k], preferred_element_type=F32)
    grad = (ga * slope[0].astype(F32)).astype(BF)
    gh[0] = grad
    upsum[pl.ds(tab[T_PART + k], 1), :] = jnp.sum(grad.astype(F32), axis=0, keepdims=True)
    branch[...] += lax.dot_general(act[0], w[k], NT, preferred_element_type=F32)

    @pl.when(k == 3)
    def _():
        wait_late(late, (after,), sem_late)
        for g in range(groups):
            here = slice(g * block, (g + 1) * block)
            out[g] = (after[g] + mod[g, 5:6, :] * branch[here, :]).astype(BF)
            sums[g : g + 1, :] = jnp.sum(
                live_cotangent(tab, cot, g) * branch[here, :], axis=0, keepdims=True
            )


def start_late(sources, targets, sem):
    for i, (source, target) in enumerate(zip(sources, targets)):
        pltpu.make_async_copy(source, target, sem.at[i]).start()


def wait_late(sources, targets, sem):
    for i, (source, target) in enumerate(zip(sources, targets)):
        pltpu.make_async_copy(source, target, sem.at[i]).wait()


def mlp_back_kernel(tab, mod, gain, gh, *rest):
    pieces, late, rest = rest[:8], rest[8:11], rest[11:]
    gmixed, rest = rest[:4], rest[4:]
    sums, gafter, gat_t, w, wo, gsec, gat, cot, after, att, sem, sem_o, sem_late = rest
    groups, block, width = cot.shape
    feats = gmixed[0].shape[0]
    fh = gh.shape[2]
    k = pl.program_id(0)

    @pl.when(k == 0)
    def _():
        start_weights(tab, pieces, slice(0, fh), w, sem)
        start_weights(tab, pieces, slice(fh, None), wo, sem_o)
        start_late(late, (cot, after, att), sem_late)
        gsec[...] = jnp.zeros_like(gsec)

    wait_weights(w, k, sem)
    gsec[...] += lax.dot_general(gh[0], w[k], NT, preferred_element_type=F32)

    @pl.when(k == 3)
    def _():
        wait_late(late, (cot, after, att), sem_late)
        for r in range(4):
            wait_weights(wo, r, sem_o)
        for g in range(groups):
            here = slice(g * block, (g + 1) * block)
            n, inverse = norm_rows(after[g])
            gs = gsec[here, :]
            sums[g, 0:1, :] = jnp.sum(gs, axis=0, keepdims=True)
            sums[g, 1:2, :] = jnp.sum(gs * n, axis=0, keepdims=True)
            scaled = gs * (gain[...] * (1.0 + mod[g, 4:5, :]))
            mean = jnp.mean(scaled, axis=1, keepdims=True)
            along = jnp.mean(scaled * n, axis=1, keepdims=True)
            grad = live_cotangent(tab, cot, g) + inverse * (scaled - mean - n * along)
            gafter[g] = grad
            sums[g, 2:3, :] = jnp.sum(grad * att[g].astype(F32), axis=0, keepdims=True)
            low = (mod[g, 2:3, :] * grad).astype(BF)
            gat[here, :] = low
            for r in range(4):
                gmixed[MIXED[r]][:, here] = (
                    jnp.dot(low, wo[r, :, :feats], preferred_element_type=F32)
                    .astype(BF)
                    .T
                )
        gat_t[...] = gat[...].T


def steps_call(
    kernel, name, tab, arrays, stepped, pieces, late, sent, outs, stepped_outs, scratch, sems, flops
):
    sm = pl.BlockSpec(memory_space=pltpu.SMEM)

    def slot_spec(shape):
        return spec((1,) + shape[1:], lambda k: (k, 0, 0))

    return pl.pallas_call(
        kernel,
        grid=(4,),
        in_specs=[sm]
        + [whole(a.shape) for a in arrays]
        + [slot_spec(a.shape) for a in stepped]
        + [ANY] * (len(pieces) + len(late)),
        out_specs=[ANY] * len(sent)
        + [whole(a.shape) for a in outs]
        + [slot_spec(a.shape) for a in stepped_outs],
        out_shape=list(sent) + list(outs) + list(stepped_outs),
        scratch_shapes=scratch
        + [pltpu.VMEM(a.shape, a.dtype) for a in [*late, *sent]]
        + [pltpu.SemaphoreType.DMA((4,))] * sems,
        compiler_params=params(),
        cost_estimate=cost(flops, 16 * 2**20),
        name=name,
    )(tab, *arrays, *stepped, *pieces, *late)


def struct(shape, dtype):
    return jax.ShapeDtypeStruct(shape, dtype)


def mlp_in_call(tab, tok, cot, mod, gain, upb, mixed, pieces):
    groups, block, width = tok.shape
    total, fh = groups * block, upb.shape[1]
    rows = struct((groups, block, width), F32)
    tall = struct((width, total), BF)
    wide = struct((4, total, fh), BF)

    return steps_call(
        mlp_in_kernel,
        "mlp_in",
        tab,
        [tok, cot, mod, gain, upb, *mixed[0], *mixed[1]],
        [],
        pieces,
        [],
        [rows, struct((groups, block, width), BF), tall, tall],
        [struct((groups, width), F32)],
        [wide, wide],
        [
            pltpu.VMEM((4, width, fh), BF),
            pltpu.VMEM((4, width, pieces[0].shape[2] - fh), BF),
            pltpu.VMEM((total, width), BF),
        ],
        3,
        10 * total * width * fh,
    )


def mlp_out_call(tab, cot, mod, downb, after, act, slope, pieces):
    groups, block, width = cot.shape
    total, fh = groups * block, act.shape[2]
    return steps_call(
        mlp_out_kernel,
        "mlp_out",
        tab,
        [mod, downb, cot],
        [act, slope],
        pieces,
        [after],
        [],
        [
            struct((groups, block, width), BF),
            struct((groups, width), F32),
            struct((4, fh), F32),
        ],
        [struct((4, total, fh), BF)],
        [
            pltpu.VMEM((4, width, fh), BF),
            pltpu.VMEM((total, width), F32),
            pltpu.VMEM((total, width), BF),
        ],
        2,
        16 * total * width * fh,
    )


def mlp_back_call(tab, cot, mod, gain, after, att, gh, pieces, feats):
    groups, block, width = cot.shape
    total, fh = groups * block, gh.shape[2]
    return steps_call(
        mlp_back_kernel,
        "mlp_back",
        tab,
        [mod, gain],
        [gh],
        pieces,
        [cot, after, att],
        [],
        [
            *[struct((feats, groups * block), BF)] * 4,
            struct((groups, 3, width), F32),
            struct((groups, block, width), F32),
            struct((width, total), BF),
        ],
        [],
        [
            pltpu.VMEM((4, width, fh), BF),
            pltpu.VMEM((4, width, pieces[0].shape[2] - fh), BF),
            pltpu.VMEM((total, width), F32),
            pltpu.VMEM((total, width), BF),
        ],
        3,
        10 * total * width * fh,
    )


def store_grads(tab, k, src, sent, kept0, kept1, sem):
    rows = src.shape[1] // NBLK
    for b in range(NBLK):
        there = tab[k * NBLK + b]
        piece = src.at[k, pl.ds(b * rows, rows), :]

        @pl.when(k >= 2)
        def _():
            pltpu.make_async_copy(piece, sent.at[there], sem.at[k, b]).start()

        @pl.when((k < 2) & (there < 8))
        def _():
            pltpu.make_async_copy(piece, kept0.at[there], sem.at[k, b]).start()

        @pl.when((k < 2) & (there >= 8))
        def _():
            pltpu.make_async_copy(piece, kept1.at[there - 8], sem.at[k, b]).start()


def wait_grads(src, sent, sem):
    rows = src.shape[1] // NBLK
    for k in range(4):
        for b in range(NBLK):
            pltpu.make_async_copy(
                src.at[k, pl.ds(b * rows, rows), :], sent.at[0], sem.at[k, b]
            ).wait()


def down_grad_kernel(tab, gbr_t, act, sent, kept0, kept1, acc, sem):
    k = pl.program_id(0)
    acc[k] = jnp.dot(gbr_t[...], act[0], preferred_element_type=F32).astype(BF)
    store_grads(tab, k, acc, sent, kept0, kept1, sem)

    @pl.when(k == 3)
    def _():
        wait_grads(acc, sent, sem)


def up_grad_kernel(tab, second_t, gat_t, gh, *rest):
    mixed, (sent, kept0, kept1, acc, sem) = (rest[:4], rest[4:8]), rest[8:]
    k = pl.program_id(0)
    fh = gh.shape[2]
    feats, block = mixed[0][0].shape
    acc[k, :, :fh] = jnp.dot(second_t[...], gh[0], preferred_element_type=F32).astype(BF)
    if acc.shape[2] > fh + feats:
        acc[k, :, fh + feats :] = jnp.zeros((acc.shape[1], acc.shape[2] - fh - feats), BF)
    for r in range(4):

        @pl.when(k == r)
        def _():
            total = None
            for g in range(2):
                term = lax.dot_general(
                    gat_t[:, g * block : (g + 1) * block],
                    mixed[g][MIXED[r]][...],
                    NT,
                    preferred_element_type=F32,
                )
                total = term if total is None else total + term
            acc[k, :, fh : fh + feats] = total.astype(BF)

    store_grads(tab, k, acc, sent, kept0, kept1, sem)

    @pl.when(k == 3)
    def _():
        wait_grads(acc, sent, sem)


def grad_call(kernel, name, tab, fixed, moving, others, lanes):
    width, total = fixed[0].shape
    fh = moving.shape[2]
    rows = width // NBLK
    grid_spec = pltpu.PrefetchScalarGridSpec(
        num_scalar_prefetch=1,
        grid=(4,),
        in_specs=[whole(a.shape) for a in fixed]
        + [spec((1, total, fh), lambda k, _: (k, 0, 0))]
        + [whole(a.shape) for a in others],
        out_specs=[ANY, ANY, ANY],
        scratch_shapes=[
            pltpu.VMEM((4, width, lanes), BF),
            pltpu.SemaphoreType.DMA((4, NBLK)),
        ],
    )
    return pl.pallas_call(
        kernel,
        grid_spec=grid_spec,
        out_shape=[struct((16, rows, lanes), BF)] + [struct((8, rows, lanes), BF)] * 2,
        compiler_params=params(),
        cost_estimate=cost(8 * width * total * lanes, 14 * 2**20),
        name=name,
    )(tab, *fixed, moving, *others)


def norm_back_kernel(t0, t1, t2, tok, after, mod, gain, out):
    normed, inverse = norm_rows(tok[0].astype(F32))
    grad = t0[0, 0].astype(F32) + t1[0, 0].astype(F32) + t2[0].astype(F32)
    scaled = grad * (gain[...] * (1.0 + mod[0, 1:2, :]))
    mean = jnp.mean(scaled, axis=1, keepdims=True)
    along = jnp.mean(scaled * normed, axis=1, keepdims=True)
    out[0] = (after[0] + inverse * (scaled - mean - normed * along)).astype(BF)


def norm_back_call(t0, t1, t2, tok, after, mod, gain):
    groups, block, width = tok.shape
    row = spec((1, block, width), lambda g: (g, 0, 0))
    near = spec((1, 1, block, width), lambda g: (0, g, 0, 0))
    return pl.pallas_call(
        norm_back_kernel,
        grid=(groups,),
        in_specs=[near, near, row, row, row, spec((1, 6, width), lambda g: (g, 0, 0)), whole((1, width))],
        out_specs=row,
        out_shape=jax.ShapeDtypeStruct((groups, block, width), BF),
        compiler_params=params(),
        cost_estimate=cost(40 * groups * block * width, 12 * groups * block * width),
        name="norm_back",
    )(t0, t1, t2, tok, after, mod, gain)


AT = 640


def pack_kernel(one, two, gate_two, upsum, down_bias, mod, gain_one, gain_two, out):
    dp, tp, _, width = out.shape
    groups = one.shape[0]
    lane = lax.broadcasted_iota(jnp.int32, (1, width), 1)

    def window(rows, start, count, at=0):
        row, offset = divmod(start, width)
        first = min(count, width - offset)
        got = rows[row]
        shift = (at - offset) % width
        got = pltpu.roll(got, shift, 1) if shift else got
        if first < count:
            shift = (at + first) % width
            rest = rows[row + 1]
            rest = pltpu.roll(rest, shift, 1) if shift else rest
            got = jnp.where(lane < at + first, got, rest)
        return got

    mods, count_mod = [], 6 * width // dp
    for g in range(groups):
        mods.append(
            [
                one[g, 0:1, :],
                gain_one[...] * one[g, 1:2, :],
                two[g, 2:3, :],
                two[g, 0:1, :],
                gain_two[...] * two[g, 1:2, :],
                gate_two[g : g + 1, :],
            ]
        )
    zero = jnp.zeros((1, width), F32)
    vectors = [zero, zero, zero]
    for g in range(groups):
        vectors[0] += down_bias[g : g + 1, :]
        vectors[1] += (1.0 + mod[g, 1:2, :]) * one[g, 1:2, :]
        vectors[2] += (1.0 + mod[g, 4:5, :]) * two[g, 1:2, :]
    rows_up = [upsum[r : r + 1, :] for r in range(upsum.shape[0])]
    count_up, count = upsum.shape[0] * width // dp, width // dp
    for d in range(dp):
        firsts = [window(mods[g], d * count_mod, count_mod) for g in range(groups)]
        firsts.append(window(rows_up, d * count_up, count_up))
        for r in range(3):
            row = jnp.where(lane < AT, firsts[r], window([vectors[r]], d * count, count, AT))
            for t in range(tp):
                out[d, t, r : r + 1, :] = row


def pack_call(dp, tp, one, two, gate_two, upsum, down_bias, mod, gain_one, gain_two):
    vm = pl.BlockSpec(memory_space=pltpu.VMEM)
    return pl.pallas_call(
        pack_kernel,
        in_specs=[vm] * 8,
        out_specs=vm,
        out_shape=struct((dp, tp, 3, one.shape[2]), F32),
        compiler_params=params(),
        cost_estimate=cost(1024, 1024),
        name="pack",
    )(one, two, gate_two, upsum, down_bias, mod, gain_one, gain_two)


def small_kernel(got, cond_t, adaw, adab, upb, downb, gain_one, gain_two):
    dp = got.shape[0]
    cols = adaw.shape[0]
    total = jnp.sum(got[...], axis=1)
    mods = jnp.concatenate([total[:, 0, :], total[:, 1, :]], axis=0)
    product = lax.dot_general(
        mods,
        cond_t[...],
        (((0,), (1,)), ((), ())),
        precision=lax.Precision.HIGHEST,
        preferred_element_type=F32,
    )
    adaw[...] = product[:cols]
    flat = jnp.sum(total, axis=0)
    adab[...] = (flat[0:1, :cols] + flat[1:2, :cols]).reshape(cols)
    upb[...] = flat[2:3, : upb.shape[0]].reshape(upb.shape[0])
    for row, ref in enumerate((downb, gain_one, gain_two)):
        ref[...] = flat[row : row + 1, AT : AT + ref.shape[0]].reshape(ref.shape[0])


def small_call(got, cond_t, cols, up_count, count):
    shapes = [(cols, cond_t.shape[0]), (cols,), (up_count,)] + [(count,)] * 3
    vm = pl.BlockSpec(memory_space=pltpu.VMEM)
    return pl.pallas_call(
        small_kernel,
        in_specs=[vm, vm],
        out_specs=[vm] * 6,
        out_shape=[jax.ShapeDtypeStruct(shape, F32) for shape in shapes],
        compiler_params=params(),
        cost_estimate=cost(1024, 1024),
        name="small",
    )(got, cond_t)


def time_embedding(time_steps, width_total):
    half_width = width_total // 2
    frequency = jnp.exp(-math.log(10000.0) * jnp.arange(half_width, dtype=F32) / half_width)
    angles = time_steps.astype(F32)[:, None] * frequency[None, :]
    return jnp.concatenate([jnp.cos(angles), jnp.sin(angles)], axis=-1)


def rotary_halves(length_total):
    half = HEAD // 2
    inverse = jnp.exp(-math.log(10000.0) * 2.0 * jnp.arange(half, dtype=F32) / HEAD)
    angles = jnp.arange(length_total, dtype=F32)[:, None] * inverse[None, :]
    return jnp.cos(angles), jnp.sin(angles)


def device_index(z, y, x, c):
    return ((z * 2 + y) * 2 + x) * 2 + c


def permutation(move):
    pairs = []
    for z in range(4):
        for y in range(2):
            for x in range(2):
                for c in range(2):
                    pairs.append((device_index(z, y, x, c), device_index(*move(z, y, x, c))))
    return pairs


CORE = permutation(lambda z, y, x, c: (z, y, x, 1 - c))
FLIP_X = permutation(lambda z, y, x, c: (z, y, 1 - x, c))
FLIP_BOTH = permutation(lambda z, y, x, c: (z, y, 1 - x, 1 - c))
FLIP_Y = permutation(lambda z, y, x, c: (z, 1 - y, x, c))
FIRST = permutation(lambda z, y, x, c: (z, 1 - y, x, c) if c == 0 else (z, y, 1 - x, c))
SECOND = permutation(lambda z, y, x, c: (z, y, 1 - x, c) if c == 0 else (z, 1 - y, x, c))
ALONG_Z = [permutation(lambda z, y, x, c, s=s: ((z + s) % 4, y, x, c)) for s in range(4)]


def send(array, pairs):
    return lax.ppermute(array, ("dp", "tensor"), pairs)


def start_z(shard):
    return [shard] + [send(shard, ALONG_Z[s]) for s in (1, 2, 3)]


def gather_z(shard):
    return jnp.stack(start_z(shard))


def after_all(value, *others):
    flat, tree = jax.tree.flatten(value)
    tied = lax.optimization_barrier((tuple(flat), others))[0]
    return jax.tree.unflatten(tree, tied)


def add_low(*terms):
    return functools.reduce(jnp.add, [term.astype(F32) for term in terms]).astype(BF)


def exchange(arrays, fast):
    if fast:
        perms = (None, CORE, FLIP_X, FLIP_BOTH)
        return [arrays[0]] + [send(arrays[r], perms[r]) for r in (1, 2, 3)]
    return list(lax.all_to_all(jnp.stack(arrays), "tensor", 0, 0, tiled=True))


class Reduce:
    def __init__(self, sent, kept0, kept1):
        shape = (2, 4) + sent.shape[1:]
        self.kept = kept0.reshape(shape), kept1.reshape(shape)
        self.got = send(sent, CORE).reshape((2,) + shape)

    def one(self, *others):
        got = after_all(self.got, *others) if others else self.got
        self.got = got
        self.half = add_low(self.kept[1], got[1])
        return self.half

    def two(self, *others):
        self.got_two = after_all(send(self.half, SECOND), *others)
        self.quarter = add_low(self.kept[0][1], self.got[0, 1], self.got_two[1])
        return self.quarter

    def start_three(self):
        self.got_three = send(self.quarter, FIRST)

    def three(self):
        self.parts = [
            add_low(self.kept[0][0, s], self.got[0, 0, s], self.got_two[0, s], self.got_three[s])
            for s in range(4)
        ]
        return self.parts

    def start_last(self):
        return [send(self.parts[s], ALONG_Z[s]) for s in (1, 2, 3)]

    def end_last(self, got):
        return functools.reduce(jnp.add, [g.astype(F32) for g in [self.parts[0]] + list(got)])


def tables(z, y, x, c):
    far_core = np.array([0, 0, 0, 0, 1, 1, 1, 1])
    kind = np.array([0, 1, 2, 3] * 2)
    core = jnp.bitwise_xor(c, far_core)
    rel_x = jnp.where(kind == 0, 0, jnp.where(kind == 3, 1, jnp.where(kind == 1, core, 1 - core)))
    rel_y = jnp.where(kind == 0, 0, jnp.where(kind == 3, 1, jnp.where(kind == 1, 1 - core, core)))
    slots = far_core * 2 + rel_x
    back = np.arange(4)
    from_z = jnp.remainder(z - back, 4)
    weight_rows = (from_z[None, :] * 2 + jnp.bitwise_xor(y, rel_y)[:, None]).reshape(32)
    slot = np.arange(4)
    parts = jnp.bitwise_xor(x, slot % 2) * 2 + jnp.bitwise_xor(c, slot // 2)
    block = np.arange(NBLK)
    to_z = jnp.remainder(block // 2 - z, 4)
    to_y = jnp.bitwise_xor(block % 2, y)
    slot_core = jnp.bitwise_xor(c, slot // 2)[:, None]
    to_x = (slot % 2)[:, None]
    major = jnp.where(slot_core == 0, to_x, to_y[None, :])
    minor = jnp.where(slot_core == 0, to_y[None, :], to_x)
    targets = (major * 8 + minor * 4 + to_z[None, :]).reshape(4 * NBLK)
    qkv_rows = jnp.concatenate(
        [from_z * 2 + y, from_z * 2 + (1 - y)]
    )
    qkv_targets = to_y * 4 + to_z
    return parts, weight_rows, slots, targets, qkv_rows, qkv_targets


def shards(
    tokens,
    lengths,
    times,
    cotangent,
    w_qkv,
    w_out,
    w_up,
    up_bias,
    w_down,
    down_bias,
    norm1_gain,
    norm2_gain,
    ada_weight,
    ada_bias,
):
    groups, block, width = tokens.shape
    dp, tp = lax.axis_size("dp"), lax.axis_size("tensor")
    seq = block * tp
    t = lax.axis_index("tensor")
    d = lax.axis_index("dp")
    fast = dp == 8 and tp == 4
    feats = w_qkv.shape[2]
    fh = w_up.shape[1]
    rows = width // NBLK
    zero = jnp.zeros((), jnp.int32)
    z, y, x, c = (d // 2, d % 2, t // 2, t % 2) if fast else (zero, zero, zero, zero)
    here = t if fast else zero

    all_times = lax.all_to_all(
        jnp.broadcast_to(times[None, :], (dp, groups)), "dp", 0, 0, tiled=True
    ).reshape(-1)
    pad = (-feats) % 128
    qkv_shard = jnp.pad(w_qkv, ((0, 0), (0, 0), (0, pad)))
    if fast:
        near = gather_z(qkv_shard)
        all_times = after_all(all_times, near)
        qkv_pieces = (near, send(near, FLIP_Y))
    else:
        full = lax.all_gather(qkv_shard, "dp", axis=1, tiled=True)
        full = full.reshape(3, NBLK, rows, feats + pad).transpose(1, 0, 2, 3)
        order = [[(-j) % 4 * 2 + p for j in range(4)] for p in range(2)]
        qkv_pieces = tuple(jnp.stack([full[b] for b in order[p]]) for p in range(2))
    tok_all = lax.all_gather(tokens, "tensor", axis=1, tiled=True)

    condition = time_embedding(all_times, ada_weight.shape[0])
    part = jnp.dot(
        condition, ada_weight.astype(F32), precision=lax.Precision.HIGHEST
    ) + ada_bias.astype(F32)
    cols = part.shape[1]
    vectors = jnp.concatenate([up_bias, down_bias, norm1_gain, norm2_gain]).astype(F32)
    sent_mod = jnp.concatenate(
        [
            part.reshape(dp, groups * cols),
            jnp.broadcast_to(vectors[None, :], (dp, vectors.shape[0])),
        ],
        axis=1,
    )
    payload = lax.all_to_all(sent_mod, "dp", 0, 0, tiled=True)
    lengths, z, y, x, c, t, here, late_condition = after_all(
        (lengths, z, y, x, c, t, here, condition), sent_mod
    )
    parts, weight_rows, slots, targets, qkv_rows, qkv_targets = tables(z, y, x, c)
    cos, sin = rotary_halves(seq)
    ready = (
        qkv_rows.astype(jnp.int32),
        jnp.concatenate([lengths, here.reshape(1)]).astype(jnp.int32),
        jnp.concatenate([lengths, (t * block).reshape(1), parts, weight_rows, slots]).astype(
            jnp.int32
        ),
        targets.astype(jnp.int32),
        jnp.concatenate([qkv_targets, here.reshape(1)]).astype(jnp.int32),
        late_condition.reshape(dp, groups, -1).transpose(2, 1, 0).reshape(-1, dp * groups),
        jnp.concatenate([cos, cos] * 2, axis=1),
        jnp.concatenate([-sin, sin] * 2, axis=1),
        cos.T,
        sin.T,
    )
    payload, ready, qkv_pieces = after_all((payload, ready, qkv_pieces))
    qkv_rows, small_tab, tab, targets, back_tab, cond_t, cos_wide, sin_wide, cos_t, sin_t = ready
    mod = (
        payload[:, : groups * cols]
        .reshape(dp, groups, cols)
        .transpose(1, 0, 2)
        .reshape(groups, 6, width)
    )
    at = groups * cols
    small = []
    for count in (up_bias.shape[0], down_bias.shape[0], norm1_gain.shape[0], norm2_gain.shape[0]):
        small.append(payload[:, at : at + count].reshape(-1))
        at += count
    upb_all = small[0].reshape(tp, fh)
    downb_all, gain_one, gain_two = (v.reshape(1, width) for v in small[1:])

    up_shard = jnp.pad(
        jnp.concatenate([w_up, w_out.T], axis=1), ((0, 0), (0, (-fh - feats) % 128))
    )
    down_shard = w_down.T
    if fast:
        up_shard, down_shard = after_all((up_shard, down_shard), qkv_pieces[1], payload)
        up_parts = start_z(up_shard)
        down_parts = start_z(down_shard)
    else:

        def gather_pieces(shard):
            full = lax.all_gather(shard, "dp", axis=0, tiled=True)
            full = lax.all_gather(full, "tensor", axis=0, tiled=False)
            full = full.reshape(tp, NBLK, rows, full.shape[2])
            return [
                jnp.stack([full[rel_x * 2 + far, b] for b in order[rel_y]])
                for far in range(2)
                for rel_x, rel_y in ((0, 0), (far, 1 - far), (1 - far, far), (1, 1))
            ]

    q, k, v, kt, vt, w_all = qkv_call(
        qkv_rows, tok_all, mod, gain_one, cos_wide, sin_wide, *qkv_pieces
    )
    vt_later = vt
    if fast:
        up_near = jnp.stack(after_all(up_parts, vt))
        vt = after_all(vt, up_near)
        up_one, up_two = send(up_near, FIRST), send(up_near, SECOND)
    *mixed0, probs0, scale0 = attend_call(0, small_tab, q, k, vt)
    if fast:
        mixed0, up_near, up_one, up_two, down_parts = after_all(
            (mixed0, up_near, up_one, up_two, down_parts), probs0
        )
        vt_later = after_all(vt, up_one, up_two)
        mixed0_all = exchange(mixed0, fast)
        up_both = send(up_one, SECOND)
        up_far = [send(piece, CORE) for piece in (up_near, up_one, up_two)]
    *mixed1, probs1, scale1 = attend_call(1, small_tab, q, k, vt_later)
    if fast:
        mixed1, up_both = after_all((mixed1, up_both), probs1, *mixed0_all)
        mixed1 = after_all(mixed1, up_both)
        up_far.append(send(up_both, CORE))
        up_pieces = [up_near, up_one, up_two, up_both] + up_far
    else:
        up_pieces, down_pieces = gather_pieces(up_shard), gather_pieces(down_shard)
        mixed0_all = exchange(mixed0, fast)
    mixed1_all = exchange(mixed1, fast)

    if fast:
        down_near = jnp.stack(after_all(down_parts, probs1))
        mixed1_all, down_near, up_pieces, upb_all, gain_two = after_all(
            (mixed1_all, down_near, up_pieces, upb_all, gain_two)
        )
        down_one, down_two = send(down_near, FIRST), send(down_near, SECOND)
    after, att, second_t, gbr_t, sum_down_bias, act, slope = mlp_in_call(
        tab, tokens, cotangent, mod, gain_two, upb_all, (mixed0_all, mixed1_all), up_pieces
    )
    if fast:
        down_one, down_two, act = after_all((down_one, down_two, act), after)
        act = after_all(act, down_one, down_two)
        down_both = send(down_one, SECOND)
        down_far = [send(piece, CORE) for piece in (down_near, down_one, down_two)]
    gd_s, *gd_k = grad_call(down_grad_kernel, "down_grad", targets, [gbr_t], act, [], fh)
    if fast:
        gd_s, down_both, down_far = after_all((gd_s, down_both, down_far), *gd_k)
        gd_s = after_all(gd_s, down_both, *down_far)
        down_far.append(send(down_both, CORE))
        down_sum = Reduce(after_all(gd_s, down_far[3]), *gd_k)
        down_pieces = [down_near, down_one, down_two, down_both] + down_far
    out, sum_gate_two, upsum, gh = mlp_out_call(
        tab, cotangent, mod, downb_all, after, act, slope, down_pieces
    )
    if fast:
        gh = after_all(gh, down_sum.one(gh))
    *gms, sums_two, grad_after, gat_t = mlp_back_call(
        tab, cotangent, mod, gain_two, after, att, gh, up_pieces, feats
    )
    if fast:
        gms, gh = after_all((gms, gh), grad_after)
    gm = exchange(gms, fast)
    gu_s, *gu_k = grad_call(
        up_grad_kernel,
        "up_grad",
        targets,
        [second_t, gat_t],
        gh,
        [*mixed0_all, *mixed1_all],
        up_pieces[0].shape[2],
    )
    if fast:
        down_sum.two(*gu_k)
        gu_s = after_all(gu_s, down_sum.got_two, *gm)
        up_sum = Reduce(gu_s, *gu_k)
        gm = after_all(gm, up_sum.one(down_sum.quarter))
    grad_t0 = attend_back_call(0, small_tab, q, kt, v, probs0, scale0, gm, cos_t, sin_t)
    if fast:
        down_sum.quarter, quarter = after_all((down_sum.quarter, up_sum.two(grad_t0)), grad_t0)
        up_sum.quarter = quarter
        gm = after_all(gm, quarter, down_sum.quarter)
    grad_t1 = attend_back_call(1, small_tab, q, kt, v, probs1, scale1, gm, cos_t, sin_t)
    if fast:
        down_sum.start_three()
        up_sum.start_three()
        down_sum.got_three, up_sum.got_three = after_all(
            (down_sum.got_three, up_sum.got_three), grad_t1
        )
        down_parts = down_sum.three()
        down_got = down_sum.start_last()
        grad_t1 = after_all(grad_t1, *down_parts)
    fts, ftk, sums_one, dws, dwk = qkv_back_call(
        back_tab,
        grad_t0,
        grad_t1,
        tok_all,
        w_all,
        mod,
        gain_one,
    )

    if fast:
        fts, dws, up_sum.got_three, down_got = after_all((fts, dws, up_sum.got_three, down_got))
        up_sum.three()
        got, got_dw = send(fts, CORE), send(dws, FLIP_Y)
        got = after_all(got, *up_sum.parts)
        up_got = up_sum.start_last()
        far = add_low(ftk[1], got[1])
        sums_one, sums_two = after_all((sums_one, sums_two), far)
        far = send(far, FLIP_X)
    else:

        def absolute(sent, kept):
            lanes = sent.shape[2]
            near = kept.reshape(2, 2, 4, rows, lanes)
            far = sent.reshape(2, 2, 4, rows, lanes).transpose(1, 0, 2, 3, 4)
            both = jnp.stack([near, far], axis=1)
            return both.transpose(0, 1, 3, 2, 4, 5).reshape(tp, width, lanes).astype(F32)

        def reduce_all(sent, kept):
            terms = lax.psum_scatter(
                absolute(sent, kept), "tensor", scatter_dimension=0, tiled=True
            )[0]
            return lax.psum_scatter(terms, "dp", scatter_dimension=0, tiled=True)

        sum_up = reduce_all(gu_s, jnp.concatenate(gu_k))
        sum_down = reduce_all(gd_s, jnp.concatenate(gd_k))
        terms = jnp.stack([dwk, dws]).transpose(2, 1, 0, 3, 4)
        terms = terms.reshape(3, width, feats + pad).astype(F32)
        sum_qkv = lax.psum_scatter(terms, "dp", scatter_dimension=1, tiled=True)
        terms = jnp.stack([ftk, fts], axis=1).reshape(tp, groups, block, width).astype(F32)
        grad_first = lax.psum_scatter(terms, "tensor", scatter_dimension=0, tiled=True)[0]
        nought = jnp.zeros_like(grad_first)
        grad_in = norm_back_call(
            grad_first[None], nought[None], nought, tokens, grad_after, mod, gain_one
        )

    up_count, count = up_bias.shape[0], down_bias.shape[0]
    payload = pack_call(
        dp,
        tp,
        sums_one,
        sums_two,
        sum_gate_two,
        upsum,
        sum_down_bias,
        mod,
        gain_one,
        gain_two,
    ).reshape(dp * tp, 3, width)
    if fast:
        payload = after_all(payload, up_got[0])
    payload = lax.all_to_all(payload, ("dp", "tensor"), 0, 0, tiled=True)
    if fast:
        dw_parts = [add_low(dwk[s], got_dw[s]) for s in range(4)]
        dw_got = [send(dw_parts[s], ALONG_Z[s]) for s in (1, 2, 3)]
        far, up_got = after_all((far, up_got), *dw_parts)
        grad_in = norm_back_call(ftk, got, far, tokens, grad_after, mod, gain_one)
        payload = after_all(payload, grad_in)
    grad_adaw, grad_adab, g_up, g_down, g_one, g_two = small_call(
        payload.reshape(dp, tp, 3, width), cond_t, cols, up_count, count
    )
    if fast:
        dw_got = after_all(dw_got, grad_adaw)
        sum_up = up_sum.end_last(up_got)
        sum_down = down_sum.end_last(down_got)
        sum_qkv = functools.reduce(jnp.add, [g.astype(F32) for g in [dw_parts[0]] + dw_got])

    return (
        out,
        grad_in,
        sum_qkv[:, :, :feats],
        sum_up[:, fh : fh + feats].T,
        sum_up[:, :fh],
        g_up,
        sum_down.T,
        g_down,
        g_one,
        g_two,
        grad_adaw.T,
        grad_adab,
    )


def solution(mesh):
    in_specs = (
        P("dp", "tensor", None),
        P("dp"),
        P("dp"),
        P("dp", "tensor", None),
        P(None, "dp", "tensor"),
        P("tensor", "dp"),
        P("dp", "tensor"),
        P("dp"),
        P("tensor", "dp"),
        P("dp"),
        P("dp"),
        P("dp"),
        P(None, "dp"),
        P("dp"),
    )
    out_specs = (
        P("dp", "tensor", None),
        P("dp", "tensor", None),
        P(None, "dp", "tensor"),
        P("tensor", "dp"),
        P("dp", "tensor"),
        P("dp"),
        P("tensor", "dp"),
        P("dp"),
        P("dp"),
        P("dp"),
        P(None, "dp"),
        P("dp"),
    )
    return jax.shard_map(shards, mesh=mesh, in_specs=in_specs, out_specs=out_specs, check_vma=False)
```

```python
import functools
import math

import jax
import jax.numpy as jnp
import numpy as np
from jax import lax
from jax.experimental import pallas as pl
from jax.experimental.pallas import tpu as pltpu
from jax.sharding import PartitionSpec as P

HEAD = 64
EPS = 1e-05
MASKED = -1e30
BF = jnp.bfloat16
F32 = jnp.float32
VMEM_MAX = 60 * 1024 * 1024
NBLK = 8
NT = (((1,), (1,)), ((), ()))


def spec(block, index_map):
    return pl.BlockSpec(block, index_map)


def whole(shape):
    return pl.BlockSpec(shape, lambda *_: (0,) * len(shape))


ANY = pl.BlockSpec(memory_space=pl.ANY)


def params():
    return pltpu.CompilerParams(vmem_limit_bytes=VMEM_MAX)


def cost(flops, moved, trans=0):
    return pl.CostEstimate(flops=flops, bytes_accessed=moved, transcendentals=trans)


def norm_rows(rows):
    centered = rows - jnp.mean(rows, axis=1, keepdims=True)
    variance = jnp.mean(centered * centered, axis=1, keepdims=True)
    inverse = lax.rsqrt(variance + EPS)
    return centered * inverse, inverse


def first_rows(tok, shift, scale, gain):
    normed, _ = norm_rows(tok.astype(F32))
    return (normed * (gain * (1.0 + scale)) + shift).astype(BF), normed


def qkv_kernel(tab, tok, mod, gain, cos, sin, w0, w1, q, k, v, kt, vt, w, sem):
    groups, heads, block = q.shape[:3]
    rows, wide = w0.shape[2], w.shape[2]

    @pl.when(pl.program_id(0) == 0)
    def _():
        copies = []
        for p, ref in enumerate((w0, w1)):
            for j in range(4):
                row = pl.multiple_of(tab[p * 4 + j] * rows, 16)
                copies.append(
                    pltpu.make_async_copy(
                        ref.at[j], w.at[:, pl.ds(row, rows), :], sem.at[p * 4 + j]
                    )
                )
        for copy in copies:
            copy.start()
        for copy in copies:
            copy.wait()

    low = lax.rem(lax.broadcasted_iota(jnp.int32, (block, wide), 1), HEAD) < HEAD // 2
    cos_wide = jnp.concatenate([cos[...]] * (wide // 128), axis=1)
    sin_wide = jnp.concatenate([sin[...]] * (wide // 128), axis=1)

    def rotate(vec):
        turned = jnp.where(
            low, pltpu.roll(vec, wide - HEAD // 2, 1), pltpu.roll(vec, HEAD // 2, 1)
        )
        return vec * cos_wide + turned * sin_wide

    for g in range(groups):

        def store_heads(ref, vec):
            for h in range(heads):
                shifted = vec if h == 0 else pltpu.roll(vec, wide - h * HEAD, 1)
                ref[g, h] = shifted[:, :HEAD].astype(BF)

        x, _ = first_rows(tok[g], mod[g, 0:1, :], mod[g, 1:2, :], gain[...])
        query = rotate(jnp.dot(x, w[0], preferred_element_type=F32))
        store_heads(q, query * (HEAD**-0.5))
        key = rotate(jnp.dot(x, w[1], preferred_element_type=F32))
        store_heads(k, key)
        kt[g] = key.T[: heads * HEAD].astype(BF)
        value = jnp.dot(x, w[2], preferred_element_type=F32)
        store_heads(v, value)
        vt[g] = value.T[: heads * HEAD].astype(BF)


def qkv_call(tab, tok_all, mod, gain, cos, sin, w0, w1):
    groups, seq, width = tok_all.shape
    block = seq // 4
    wide = w0.shape[3]
    heads = (wide // HEAD) * 3 // 4
    feats = heads * HEAD
    by_head = spec((groups, heads, block, HEAD), lambda j, _: (0, 0, j, 0))
    by_feat = spec((groups, feats, block), lambda j, _: (0, 0, j))
    grid_spec = pltpu.PrefetchScalarGridSpec(
        num_scalar_prefetch=1,
        grid=(4,),
        in_specs=[
            spec((groups, block, width), lambda j, _: (0, j, 0)),
            whole((groups, 6, width)),
            whole((1, width)),
            spec((block, 128), lambda j, _: (j, 0)),
            spec((block, 128), lambda j, _: (j, 0)),
            ANY,
            ANY,
        ],
        out_specs=[by_head, by_head, by_head, by_feat, by_feat, whole((3, width, wide))],
        scratch_shapes=[pltpu.SemaphoreType.DMA((8,))],
    )
    head_shape = jax.ShapeDtypeStruct((groups, heads, seq, HEAD), BF)
    turned = jax.ShapeDtypeStruct((groups, feats, seq), BF)
    return pl.pallas_call(
        qkv_kernel,
        grid_spec=grid_spec,
        out_shape=[
            head_shape,
            head_shape,
            head_shape,
            turned,
            turned,
            jax.ShapeDtypeStruct((3, width, wide), BF),
        ],
        compiler_params=params(),
        cost_estimate=cost(2 * groups * seq * width * wide * 3, 16 * 2**20),
        name="qkv",
    )(tab, tok_all, mod, gain, cos, sin, w0, w1)


CHUNK = 128
LEAST = 256


def unrolled(count, step, carried):
    for i in range(count):
        carried = step(i, carried)
    return carried


def eights(rows, op):
    return op(rows.reshape(rows.shape[0] // 8, 8, rows.shape[1]), axis=0)


def attend_kernel(tab, q, k, vt, mix0, mix1, mix2, mix3, probs, inverse, raw, mixed, *, group):
    heads = k.shape[1]
    block = q.shape[2]
    length = tab[group]
    chunks = k.shape[2] // CHUNK
    position = lax.broadcasted_iota(jnp.int32, (CHUNK, block), 0)

    def head(h, _):
        query = q[0, h]

        def score(c, largest):
            rows = slice(c * CHUNK, (c + 1) * CHUNK)
            scores = lax.dot_general(k[0, h, rows, :], query, NT, preferred_element_type=F32)
            if (c + 1) * CHUNK > LEAST:
                scores = jnp.where(position < length - c * CHUNK, scores, MASKED)
            raw[rows, :] = scores
            return jnp.maximum(largest, eights(scores, jnp.max))

        largest = unrolled(chunks, score, jnp.full((8, block), MASKED, F32))
        largest = jnp.max(largest, axis=0, keepdims=True)
        here = pl.ds(pl.multiple_of(h * HEAD, HEAD), HEAD)

        def weigh(c, carried):
            total, out = carried
            rows = slice(c * CHUNK, (c + 1) * CHUNK)
            weights = jnp.exp(raw[rows, :] - largest)
            low = weights.astype(BF)
            probs[h, rows, :] = low
            out = out + jnp.dot(vt[0, here, rows], low, preferred_element_type=F32)
            return total + eights(weights, jnp.sum), out

        total, out = unrolled(
            chunks, weigh, (jnp.zeros((8, block), F32), jnp.zeros((HEAD, block), F32))
        )
        scale = 1.0 / jnp.sum(total, axis=0, keepdims=True)
        inverse[h] = scale
        mixed[here, :] = (out * scale).astype(BF)
        return 0

    unrolled(heads, head, 0)
    for r, ref in enumerate((mix0, mix1, mix2, mix3)):

        @pl.when(turn(pl.program_id(0)) == r)
        def _():
            ref[...] = mixed[...]


def turn(step):
    return lax.rem(step + 1, 4)


def attend_call(group, tab, q, k, vt):
    _, heads, seq, _ = q.shape
    block = seq // 4
    feats = heads * HEAD

    def piece(i, tab):
        return lax.bitwise_xor(tab[2], turn(i))

    grid_spec = pltpu.PrefetchScalarGridSpec(
        num_scalar_prefetch=1,
        grid=(4,),
        in_specs=[
            spec((1, heads, block, HEAD), lambda i, tab: (group, 0, piece(i, tab), 0)),
            spec((1, heads, seq, HEAD), lambda i, tab: (group, 0, 0, 0)),
            spec((1, feats, seq), lambda i, tab: (group, 0, 0)),
        ],
        out_specs=[
            *[whole((feats, block))] * 4,
            spec((heads, seq, block), lambda i, tab: (0, 0, piece(i, tab))),
            spec((heads, 1, block), lambda i, tab: (0, 0, piece(i, tab))),
        ],
        scratch_shapes=[pltpu.VMEM((seq, block), F32), pltpu.VMEM((feats, block), BF)],
    )
    return pl.pallas_call(
        functools.partial(attend_kernel, group=group),
        grid_spec=grid_spec,
        out_shape=[
            *[jax.ShapeDtypeStruct((feats, block), BF)] * 4,
            jax.ShapeDtypeStruct((heads, seq, seq), BF),
            jax.ShapeDtypeStruct((heads, 1, seq), F32),
        ],
        compiler_params=params(),
        cost_estimate=cost(16 * heads * seq * seq * HEAD, 10 * 2**20, heads * seq * seq),
        name="attend",
    )(tab, q, k, vt)


def attend_back_kernel(
    tab, q, kt, v, probs, inverse, gm0, gm1, gm2, gm3, cos, sin, out, dk, dv, gm
):
    heads, block = q.shape[1], q.shape[2]
    half = HEAD // 2
    step = pl.program_id(0)
    j = lax.bitwise_xor(tab[2], step)

    @pl.when(step == 0)
    def _():
        dk[...] = jnp.zeros_like(dk)
        dv[...] = jnp.zeros_like(dv)
        for r, ref in enumerate((gm0, gm1, gm2, gm3)):
            gm[r] = ref[...]

    columns = pl.ds(pl.multiple_of(j * block, 128), block)
    cos_here, sin_here = cos[:, columns], sin[:, columns]

    def store_turned(plane, h, vec, c, s, where):
        low, high = vec[:half], vec[half:]
        base = pl.multiple_of(h * HEAD, HEAD)
        out[plane, pl.ds(base, half), where] = (low * c + high * s).astype(BF)
        out[plane, pl.ds(base + half, half), where] = (high * c - low * s).astype(BF)

    def head(h, _):
        here = pl.ds(pl.multiple_of(h * HEAD, HEAD), HEAD)
        scale = inverse[h]
        grad = (gm[step, here, :].astype(F32) * scale).astype(BF)
        query = q[0, h]

        low = probs[h]
        dp = jnp.dot(v[0, h], grad, preferred_element_type=F32)
        soft = low.astype(F32)
        prod = soft * dp
        inner = jnp.sum(prod, axis=0, keepdims=True) * scale
        ds = (prod - soft * inner).astype(BF)
        dv[h] += lax.dot_general(low, grad, NT, preferred_element_type=F32)
        dk[h] += jnp.dot(ds, query, preferred_element_type=F32)
        dq = jnp.dot(kt[0, here, :], ds, preferred_element_type=F32)
        store_turned(0, h, dq * (HEAD**-0.5), cos_here, sin_here, columns)
        return 0

    unrolled(heads, head, 0)

    @pl.when(step == pl.num_programs(0) - 1)
    def _():
        def turn_keys(h, _):
            store_turned(1, h, dk[h].T, cos[...], sin[...], slice(None))
            out[2, pl.ds(pl.multiple_of(h * HEAD, HEAD), HEAD), :] = dv[h].T.astype(BF)
            return 0

        unrolled(heads, turn_keys, 0)


def attend_back_call(group, tab, q, kt, v, probs, inverse, gm, cos, sin):
    _, heads, seq, _ = q.shape
    block = seq // 4
    feats = heads * HEAD
    half = HEAD // 2

    def piece(i, tab):
        return lax.bitwise_xor(tab[2], i)

    grid_spec = pltpu.PrefetchScalarGridSpec(
        num_scalar_prefetch=1,
        grid=(4,),
        in_specs=[
            spec((1, heads, block, HEAD), lambda i, tab: (group, 0, piece(i, tab), 0)),
            spec((1, feats, seq), lambda i, tab: (group, 0, 0)),
            spec((1, heads, seq, HEAD), lambda i, tab: (group, 0, 0, 0)),
            spec((heads, seq, block), lambda i, tab: (0, 0, piece(i, tab))),
            spec((heads, 1, block), lambda i, tab: (0, 0, piece(i, tab))),
            *[spec((feats, block), lambda i, tab: (0, group))] * 4,
            whole((half, seq)),
            whole((half, seq)),
        ],
        out_specs=whole((3, feats, seq)),
        scratch_shapes=[
            pltpu.VMEM((heads, seq, HEAD), F32),
            pltpu.VMEM((heads, seq, HEAD), F32),
            pltpu.VMEM((4, feats, block), BF),
        ],
    )
    return pl.pallas_call(
        attend_back_kernel,
        grid_spec=grid_spec,
        out_shape=jax.ShapeDtypeStruct((3, feats, seq), BF),
        compiler_params=params(),
        cost_estimate=cost(32 * heads * seq * seq * HEAD, 10 * 2**20),
        name="attend_back",
    )(tab, q, kt, v, probs, inverse, *gm, cos, sin)


def qkv_back_kernel(tab, gt0, gt1, tok, w, mod, gain, fts, ftk, sums, dws, dwk, acc):
    i = pl.program_id(0)
    feats, block = gt0.shape[1], gt0.shape[2]
    wide, width = w.shape[2], w.shape[1]
    rows, lanes = dws.shape[1:]

    @pl.when(i == 0)
    def _():
        acc[...] = jnp.zeros_like(acc)
        sums[...] = jnp.zeros_like(sums)

    for g, gt in enumerate((gt0, gt1)):
        first, normed = first_rows(tok[g], mod[g, 0:1, :], mod[g, 1:2, :], gain[...])
        total = None
        for j in range(3):
            part = gt[j]
            tall = part.astype(F32)
            if wide > feats:
                tall = jnp.concatenate([tall, jnp.zeros((wide - feats, block), F32)], axis=0)
            term = lax.dot_general(tall.T.astype(BF), w[j], NT, preferred_element_type=F32)
            total = term if total is None else total + term
            acc[j * feats : (j + 1) * feats] += jnp.dot(part, first, preferred_element_type=F32)
        sums[g, 0:1, :] += jnp.sum(total, axis=0, keepdims=True)
        sums[g, 1:2, :] += jnp.sum(total * normed, axis=0, keepdims=True)
        low = total.astype(BF)

        @pl.when(i < 2)
        def _():
            fts[0, g] = low

        @pl.when(i >= 2)
        def _():
            ftk[0, g] = low

    @pl.when(i == pl.num_programs(0) - 1)
    def _():
        flat = acc[...].T.astype(BF)
        for b in range(NBLK):
            part = flat[b * rows : (b + 1) * rows]
            there = tab[b]

            @pl.when(there < NBLK // 2)
            def _():
                dwk[there] = part

            @pl.when(there >= NBLK // 2)
            def _():
                dws[there - NBLK // 2] = part


def qkv_back_call(tab, gt0, gt1, tok_all, w, mod, gain):
    _, feats, seq = gt0.shape
    groups = tok_all.shape[0]
    block = seq // 4
    width = tok_all.shape[2]
    wide = w.shape[2]
    rows = width // NBLK
    lanes = 3 * feats + (-3 * feats) % 128

    def piece(i, tab):
        return lax.bitwise_xor(tab[NBLK], lax.rem(i, 2) * 2 + (1 - i // 2))

    by_feat = spec((3, feats, block), lambda i, tab: (0, 0, piece(i, tab)))
    grid_spec = pltpu.PrefetchScalarGridSpec(
        num_scalar_prefetch=1,
        grid=(4,),
        in_specs=[
            by_feat,
            by_feat,
            spec((groups, block, width), lambda i, tab: (0, piece(i, tab), 0)),
            whole((3, width, wide)),
            whole((groups, 6, width)),
            whole((1, width)),
        ],
        out_specs=[
            spec((1, groups, block, width), lambda i, tab: (jnp.minimum(i, 1), 0, 0, 0)),
            spec((1, groups, block, width), lambda i, tab: (jnp.maximum(i - 2, 0), 0, 0, 0)),
            whole((groups, 2, width)),
            whole((NBLK // 2, rows, lanes)),
            whole((NBLK // 2, rows, lanes)),
        ],
        scratch_shapes=[pltpu.VMEM((lanes, width), F32)],
    )
    terms = jax.ShapeDtypeStruct((2, groups, block, width), BF)
    share = jax.ShapeDtypeStruct((NBLK // 2, rows, lanes), BF)
    return pl.pallas_call(
        qkv_back_kernel,
        grid_spec=grid_spec,
        out_shape=[terms, terms, jax.ShapeDtypeStruct((groups, 2, width), F32), share, share],
        compiler_params=params(),
        cost_estimate=cost(4 * groups * seq * width * wide * 3, 16 * 2**20),
        name="qkv_back",
    )(tab, gt0, gt1, tok_all, w, mod, gain)


MIXED = (0, 2, 1, 3)
T_PART, T_ROW, T_SLOT = 3, 7, 39


def start_weights(tab, pieces, lanes, target, sem):
    rows = pieces[0].shape[1]
    for p in range(8):
        slot = tab[T_SLOT + p]
        for j in range(4):
            row = pl.multiple_of(tab[T_ROW + p * 4 + j] * rows, 16)
            pltpu.make_async_copy(
                pieces[p].at[j, :, lanes], target.at[slot, pl.ds(row, rows), :], sem.at[slot]
            ).start()


def wait_weights(target, k, sem):
    pltpu.make_async_copy(target.at[k], target.at[k], sem.at[k]).wait()


def live_cotangent(tab, cot, g):
    _, block, width = cot.shape
    position = tab[2] + lax.broadcasted_iota(jnp.int32, (block, width), 0)
    return jnp.where(position < tab[g], cot[g].astype(F32), 0.0)


def mlp_in_kernel(tab, tok, cot, mod, gain, upb, *rest):
    mixed, pieces, rest = (rest[:4], rest[4:8]), rest[8:16], rest[16:]
    sent, rest = rest[:4], rest[4:]
    sums, act, slope, w, wo, second, after, att, second_t, gbr_t, sem, sem_o, sem_s = rest
    groups, block, width = tok.shape
    feats = mixed[0][0].shape[0]
    fh = upb.shape[1]
    k = pl.program_id(0)

    @pl.when(k == 0)
    def _():
        start_weights(tab, pieces, slice(fh, None), wo, sem_o)
        start_weights(tab, pieces, slice(0, fh), w, sem)
        for g in range(groups):
            here = slice(g * block, (g + 1) * block)
            gb = (mod[g, 5:6, :] * live_cotangent(tab, cot, g)).astype(BF)
            gbr_t[:, here] = gb.T
            sums[g : g + 1, :] = jnp.sum(gb.astype(F32), axis=0, keepdims=True)
        for r in range(4):
            wait_weights(wo, r, sem_o)
        for g in range(groups):
            here = slice(g * block, (g + 1) * block)
            total = jnp.zeros((block, width), F32)
            for r in range(4):
                total += lax.dot_general(
                    mixed[g][MIXED[r]][...].T,
                    wo[r, :, :feats],
                    NT,
                    preferred_element_type=F32,
                )
            att[g] = total.astype(BF)
            rows_after = tok[g].astype(F32) + mod[g, 2:3, :] * total
            after[g] = rows_after
            n, _ = norm_rows(rows_after)
            x = n * (gain[...] * (1.0 + mod[g, 4:5, :])) + mod[g, 3:4, :]
            second[here, :] = x.astype(BF)
        second_t[...] = second[...].T
        start_late((after, att, second_t, gbr_t), sent, sem_s)

    @pl.when(k == 3)
    def _():
        wait_late((after, att, second_t, gbr_t), sent, sem_s)

    c1, c3 = math.sqrt(2.0 / math.pi), 0.044715
    wait_weights(w, k, sem)
    bias = upb[pl.ds(tab[T_PART + k], 1), :]
    hidden = jnp.dot(second[...], w[k], preferred_element_type=F32) + bias
    square = hidden * hidden
    th = jnp.tanh(c1 * hidden * (1.0 + c3 * square))
    up = 0.5 * (1.0 + th)
    act[0] = (hidden * up).astype(BF)
    slope[0] = (
        up + (0.5 * c1) * hidden * (1.0 - th * th) * (1.0 + (3.0 * c3) * square)
    ).astype(BF)


def mlp_out_kernel(tab, mod, downb, cot, act, slope, *rest):
    pieces, late, rest = rest[:8], rest[8:9], rest[9:]
    out, sums, upsum, gh, w, branch, gbr, after, sem, sem_late = rest
    groups, block, width = cot.shape
    k = pl.program_id(0)

    @pl.when(k == 0)
    def _():
        start_weights(tab, pieces, slice(None), w, sem)
        start_late(late, (after,), sem_late)
        for g in range(groups):
            grad_branch = mod[g, 5:6, :] * live_cotangent(tab, cot, g)
            gbr[g * block : (g + 1) * block, :] = grad_branch.astype(BF)
        branch[...] = jnp.broadcast_to(downb[...], branch.shape)

    wait_weights(w, k, sem)
    ga = jnp.dot(gbr[...], w[k], preferred_element_type=F32)
    grad = (ga * slope[0].astype(F32)).astype(BF)
    gh[0] = grad
    upsum[pl.ds(tab[T_PART + k], 1), :] = jnp.sum(grad.astype(F32), axis=0, keepdims=True)
    branch[...] += lax.dot_general(act[0], w[k], NT, preferred_element_type=F32)

    @pl.when(k == 3)
    def _():
        wait_late(late, (after,), sem_late)
        for g in range(groups):
            here = slice(g * block, (g + 1) * block)
            out[g] = (after[g] + mod[g, 5:6, :] * branch[here, :]).astype(BF)
            sums[g : g + 1, :] = jnp.sum(
                live_cotangent(tab, cot, g) * branch[here, :], axis=0, keepdims=True
            )


def start_late(sources, targets, sem):
    for i, (source, target) in enumerate(zip(sources, targets)):
        pltpu.make_async_copy(source, target, sem.at[i]).start()


def wait_late(sources, targets, sem):
    for i, (source, target) in enumerate(zip(sources, targets)):
        pltpu.make_async_copy(source, target, sem.at[i]).wait()


def mlp_back_kernel(tab, mod, gain, gh, *rest):
    pieces, late, rest = rest[:8], rest[8:11], rest[11:]
    gmixed, rest = rest[:4], rest[4:]
    sums, gafter, gat_t, w, wo, gsec, gat, cot, after, att, sem, sem_o, sem_late = rest
    groups, block, width = cot.shape
    feats = gmixed[0].shape[0]
    fh = gh.shape[2]
    k = pl.program_id(0)

    @pl.when(k == 0)
    def _():
        start_weights(tab, pieces, slice(0, fh), w, sem)
        start_weights(tab, pieces, slice(fh, None), wo, sem_o)
        start_late(late, (cot, after, att), sem_late)
        gsec[...] = jnp.zeros_like(gsec)

    wait_weights(w, k, sem)
    gsec[...] += lax.dot_general(gh[0], w[k], NT, preferred_element_type=F32)

    @pl.when(k == 3)
    def _():
        wait_late(late, (cot, after, att), sem_late)
        for r in range(4):
            wait_weights(wo, r, sem_o)
        for g in range(groups):
            here = slice(g * block, (g + 1) * block)
            n, inverse = norm_rows(after[g])
            gs = gsec[here, :]
            sums[g, 0:1, :] = jnp.sum(gs, axis=0, keepdims=True)
            sums[g, 1:2, :] = jnp.sum(gs * n, axis=0, keepdims=True)
            scaled = gs * (gain[...] * (1.0 + mod[g, 4:5, :]))
            mean = jnp.mean(scaled, axis=1, keepdims=True)
            along = jnp.mean(scaled * n, axis=1, keepdims=True)
            grad = live_cotangent(tab, cot, g) + inverse * (scaled - mean - n * along)
            gafter[g] = grad
            sums[g, 2:3, :] = jnp.sum(grad * att[g].astype(F32), axis=0, keepdims=True)
            low = (mod[g, 2:3, :] * grad).astype(BF)
            gat[here, :] = low
            for r in range(4):
                gmixed[MIXED[r]][:, here] = (
                    jnp.dot(low, wo[r, :, :feats], preferred_element_type=F32)
                    .astype(BF)
                    .T
                )
        gat_t[...] = gat[...].T


def steps_call(
    kernel, name, tab, arrays, stepped, pieces, late, sent, outs, stepped_outs, scratch, sems, flops
):
    sm = pl.BlockSpec(memory_space=pltpu.SMEM)

    def slot_spec(shape):
        return spec((1,) + shape[1:], lambda k: (k, 0, 0))

    return pl.pallas_call(
        kernel,
        grid=(4,),
        in_specs=[sm]
        + [whole(a.shape) for a in arrays]
        + [slot_spec(a.shape) for a in stepped]
        + [ANY] * (len(pieces) + len(late)),
        out_specs=[ANY] * len(sent)
        + [whole(a.shape) for a in outs]
        + [slot_spec(a.shape) for a in stepped_outs],
        out_shape=list(sent) + list(outs) + list(stepped_outs),
        scratch_shapes=scratch
        + [pltpu.VMEM(a.shape, a.dtype) for a in [*late, *sent]]
        + [pltpu.SemaphoreType.DMA((4,))] * sems,
        compiler_params=params(),
        cost_estimate=cost(flops, 16 * 2**20),
        name=name,
    )(tab, *arrays, *stepped, *pieces, *late)


def struct(shape, dtype):
    return jax.ShapeDtypeStruct(shape, dtype)


def mlp_in_call(tab, tok, cot, mod, gain, upb, mixed, pieces):
    groups, block, width = tok.shape
    total, fh = groups * block, upb.shape[1]
    rows = struct((groups, block, width), F32)
    tall = struct((width, total), BF)
    wide = struct((4, total, fh), BF)

    return steps_call(
        mlp_in_kernel,
        "mlp_in",
        tab,
        [tok, cot, mod, gain, upb, *mixed[0], *mixed[1]],
        [],
        pieces,
        [],
        [rows, struct((groups, block, width), BF), tall, tall],
        [struct((groups, width), F32)],
        [wide, wide],
        [
            pltpu.VMEM((4, width, fh), BF),
            pltpu.VMEM((4, width, pieces[0].shape[2] - fh), BF),
            pltpu.VMEM((total, width), BF),
        ],
        3,
        10 * total * width * fh,
    )


def mlp_out_call(tab, cot, mod, downb, after, act, slope, pieces):
    groups, block, width = cot.shape
    total, fh = groups * block, act.shape[2]
    return steps_call(
        mlp_out_kernel,
        "mlp_out",
        tab,
        [mod, downb, cot],
        [act, slope],
        pieces,
        [after],
        [],
        [
            struct((groups, block, width), BF),
            struct((groups, width), F32),
            struct((4, fh), F32),
        ],
        [struct((4, total, fh), BF)],
        [
            pltpu.VMEM((4, width, fh), BF),
            pltpu.VMEM((total, width), F32),
            pltpu.VMEM((total, width), BF),
        ],
        2,
        16 * total * width * fh,
    )


def mlp_back_call(tab, cot, mod, gain, after, att, gh, pieces, feats):
    groups, block, width = cot.shape
    total, fh = groups * block, gh.shape[2]
    return steps_call(
        mlp_back_kernel,
        "mlp_back",
        tab,
        [mod, gain],
        [gh],
        pieces,
        [cot, after, att],
        [],
        [
            *[struct((feats, groups * block), BF)] * 4,
            struct((groups, 3, width), F32),
            struct((groups, block, width), F32),
            struct((width, total), BF),
        ],
        [],
        [
            pltpu.VMEM((4, width, fh), BF),
            pltpu.VMEM((4, width, pieces[0].shape[2] - fh), BF),
            pltpu.VMEM((total, width), F32),
            pltpu.VMEM((total, width), BF),
        ],
        3,
        10 * total * width * fh,
    )


def store_grads(tab, k, src, sent, kept0, kept1, sem):
    rows = src.shape[1] // NBLK
    for b in range(NBLK):
        there = tab[k * NBLK + b]
        piece = src.at[k, pl.ds(b * rows, rows), :]

        @pl.when(k >= 2)
        def _():
            pltpu.make_async_copy(piece, sent.at[there], sem.at[k, b]).start()

        @pl.when((k < 2) & (there < 8))
        def _():
            pltpu.make_async_copy(piece, kept0.at[there], sem.at[k, b]).start()

        @pl.when((k < 2) & (there >= 8))
        def _():
            pltpu.make_async_copy(piece, kept1.at[there - 8], sem.at[k, b]).start()


def wait_grads(src, sent, sem):
    rows = src.shape[1] // NBLK
    for k in range(4):
        for b in range(NBLK):
            pltpu.make_async_copy(
                src.at[k, pl.ds(b * rows, rows), :], sent.at[0], sem.at[k, b]
            ).wait()


def down_grad_kernel(tab, gbr_t, act, sent, kept0, kept1, acc, sem):
    k = pl.program_id(0)
    acc[k] = jnp.dot(gbr_t[...], act[0], preferred_element_type=F32).astype(BF)
    store_grads(tab, k, acc, sent, kept0, kept1, sem)

    @pl.when(k == 3)
    def _():
        wait_grads(acc, sent, sem)


def up_grad_kernel(tab, second_t, gat_t, gh, *rest):
    mixed, (sent, kept0, kept1, acc, sem) = (rest[:4], rest[4:8]), rest[8:]
    k = pl.program_id(0)
    fh = gh.shape[2]
    feats, block = mixed[0][0].shape
    acc[k, :, :fh] = jnp.dot(second_t[...], gh[0], preferred_element_type=F32).astype(BF)
    if acc.shape[2] > fh + feats:
        acc[k, :, fh + feats :] = jnp.zeros((acc.shape[1], acc.shape[2] - fh - feats), BF)
    for r in range(4):

        @pl.when(k == r)
        def _():
            total = None
            for g in range(2):
                term = lax.dot_general(
                    gat_t[:, g * block : (g + 1) * block],
                    mixed[g][MIXED[r]][...],
                    NT,
                    preferred_element_type=F32,
                )
                total = term if total is None else total + term
            acc[k, :, fh : fh + feats] = total.astype(BF)

    store_grads(tab, k, acc, sent, kept0, kept1, sem)

    @pl.when(k == 3)
    def _():
        wait_grads(acc, sent, sem)


def grad_call(kernel, name, tab, fixed, moving, others, lanes):
    width, total = fixed[0].shape
    fh = moving.shape[2]
    rows = width // NBLK
    grid_spec = pltpu.PrefetchScalarGridSpec(
        num_scalar_prefetch=1,
        grid=(4,),
        in_specs=[whole(a.shape) for a in fixed]
        + [spec((1, total, fh), lambda k, _: (k, 0, 0))]
        + [whole(a.shape) for a in others],
        out_specs=[ANY, ANY, ANY],
        scratch_shapes=[
            pltpu.VMEM((4, width, lanes), BF),
            pltpu.SemaphoreType.DMA((4, NBLK)),
        ],
    )
    return pl.pallas_call(
        kernel,
        grid_spec=grid_spec,
        out_shape=[struct((16, rows, lanes), BF)] + [struct((8, rows, lanes), BF)] * 2,
        compiler_params=params(),
        cost_estimate=cost(8 * width * total * lanes, 14 * 2**20),
        name=name,
    )(tab, *fixed, moving, *others)


def norm_back_kernel(t0, t1, t2, tok, after, mod, gain, out):
    normed, inverse = norm_rows(tok[0].astype(F32))
    grad = t0[0, 0].astype(F32) + t1[0, 0].astype(F32) + t2[0].astype(F32)
    scaled = grad * (gain[...] * (1.0 + mod[0, 1:2, :]))
    mean = jnp.mean(scaled, axis=1, keepdims=True)
    along = jnp.mean(scaled * normed, axis=1, keepdims=True)
    out[0] = (after[0] + inverse * (scaled - mean - normed * along)).astype(BF)


def norm_back_call(t0, t1, t2, tok, after, mod, gain):
    groups, block, width = tok.shape
    row = spec((1, block, width), lambda g: (g, 0, 0))
    near = spec((1, 1, block, width), lambda g: (0, g, 0, 0))
    return pl.pallas_call(
        norm_back_kernel,
        grid=(groups,),
        in_specs=[near, near, row, row, row, spec((1, 6, width), lambda g: (g, 0, 0)), whole((1, width))],
        out_specs=row,
        out_shape=jax.ShapeDtypeStruct((groups, block, width), BF),
        compiler_params=params(),
        cost_estimate=cost(40 * groups * block * width, 12 * groups * block * width),
        name="norm_back",
    )(t0, t1, t2, tok, after, mod, gain)


AT = 640


def pack_kernel(one, two, gate_two, upsum, down_bias, mod, gain_one, gain_two, out):
    dp, tp, _, width = out.shape
    groups = one.shape[0]
    lane = lax.broadcasted_iota(jnp.int32, (1, width), 1)

    def window(rows, start, count, at=0):
        row, offset = divmod(start, width)
        first = min(count, width - offset)
        got = rows[row]
        shift = (at - offset) % width
        got = pltpu.roll(got, shift, 1) if shift else got
        if first < count:
            shift = (at + first) % width
            rest = rows[row + 1]
            rest = pltpu.roll(rest, shift, 1) if shift else rest
            got = jnp.where(lane < at + first, got, rest)
        return got

    mods, count_mod = [], 6 * width // dp
    for g in range(groups):
        mods.append(
            [
                one[g, 0:1, :],
                gain_one[...] * one[g, 1:2, :],
                two[g, 2:3, :],
                two[g, 0:1, :],
                gain_two[...] * two[g, 1:2, :],
                gate_two[g : g + 1, :],
            ]
        )
    zero = jnp.zeros((1, width), F32)
    vectors = [zero, zero, zero]
    for g in range(groups):
        vectors[0] += down_bias[g : g + 1, :]
        vectors[1] += (1.0 + mod[g, 1:2, :]) * one[g, 1:2, :]
        vectors[2] += (1.0 + mod[g, 4:5, :]) * two[g, 1:2, :]
    rows_up = [upsum[r : r + 1, :] for r in range(upsum.shape[0])]
    count_up, count = upsum.shape[0] * width // dp, width // dp
    for d in range(dp):
        firsts = [window(mods[g], d * count_mod, count_mod) for g in range(groups)]
        firsts.append(window(rows_up, d * count_up, count_up))
        for r in range(3):
            row = jnp.where(lane < AT, firsts[r], window([vectors[r]], d * count, count, AT))
            for t in range(tp):
                out[d, t, r : r + 1, :] = row


def pack_call(dp, tp, one, two, gate_two, upsum, down_bias, mod, gain_one, gain_two):
    vm = pl.BlockSpec(memory_space=pltpu.VMEM)
    return pl.pallas_call(
        pack_kernel,
        in_specs=[vm] * 8,
        out_specs=vm,
        out_shape=struct((dp, tp, 3, one.shape[2]), F32),
        compiler_params=params(),
        cost_estimate=cost(1024, 1024),
        name="pack",
    )(one, two, gate_two, upsum, down_bias, mod, gain_one, gain_two)


def small_kernel(got, cond_t, adaw, adab, upb, downb, gain_one, gain_two):
    dp = got.shape[0]
    cols = adaw.shape[0]
    total = jnp.sum(got[...], axis=1)
    mods = jnp.concatenate([total[:, 0, :], total[:, 1, :]], axis=0)
    product = lax.dot_general(
        mods,
        cond_t[...],
        (((0,), (1,)), ((), ())),
        precision=lax.Precision.HIGHEST,
        preferred_element_type=F32,
    )
    adaw[...] = product[:cols]
    flat = jnp.sum(total, axis=0)
    adab[...] = (flat[0:1, :cols] + flat[1:2, :cols]).reshape(cols)
    upb[...] = flat[2:3, : upb.shape[0]].reshape(upb.shape[0])
    for row, ref in enumerate((downb, gain_one, gain_two)):
        ref[...] = flat[row : row + 1, AT : AT + ref.shape[0]].reshape(ref.shape[0])


def small_call(got, cond_t, cols, up_count, count):
    shapes = [(cols, cond_t.shape[0]), (cols,), (up_count,)] + [(count,)] * 3
    vm = pl.BlockSpec(memory_space=pltpu.VMEM)
    return pl.pallas_call(
        small_kernel,
        in_specs=[vm, vm],
        out_specs=[vm] * 6,
        out_shape=[jax.ShapeDtypeStruct(shape, F32) for shape in shapes],
        compiler_params=params(),
        cost_estimate=cost(1024, 1024),
        name="small",
    )(got, cond_t)


def time_embedding(time_steps, width_total):
    half_width = width_total // 2
    frequency = jnp.exp(-math.log(10000.0) * jnp.arange(half_width, dtype=F32) / half_width)
    angles = time_steps.astype(F32)[:, None] * frequency[None, :]
    return jnp.concatenate([jnp.cos(angles), jnp.sin(angles)], axis=-1)


def rotary_halves(length_total):
    half = HEAD // 2
    inverse = jnp.exp(-math.log(10000.0) * 2.0 * jnp.arange(half, dtype=F32) / HEAD)
    angles = jnp.arange(length_total, dtype=F32)[:, None] * inverse[None, :]
    return jnp.cos(angles), jnp.sin(angles)


def device_index(z, y, x, c):
    return ((z * 2 + y) * 2 + x) * 2 + c


def permutation(move):
    pairs = []
    for z in range(4):
        for y in range(2):
            for x in range(2):
                for c in range(2):
                    pairs.append((device_index(z, y, x, c), device_index(*move(z, y, x, c))))
    return pairs


CORE = permutation(lambda z, y, x, c: (z, y, x, 1 - c))
FLIP_X = permutation(lambda z, y, x, c: (z, y, 1 - x, c))
FLIP_BOTH = permutation(lambda z, y, x, c: (z, y, 1 - x, 1 - c))
FLIP_Y = permutation(lambda z, y, x, c: (z, 1 - y, x, c))
FIRST = permutation(lambda z, y, x, c: (z, 1 - y, x, c) if c == 0 else (z, y, 1 - x, c))
SECOND = permutation(lambda z, y, x, c: (z, y, 1 - x, c) if c == 0 else (z, 1 - y, x, c))
ALONG_Z = [permutation(lambda z, y, x, c, s=s: ((z + s) % 4, y, x, c)) for s in range(4)]


def send(array, pairs):
    return lax.ppermute(array, ("dp", "tensor"), pairs)


def start_z(shard):
    return [shard] + [send(shard, ALONG_Z[s]) for s in (1, 2, 3)]


def gather_z(shard):
    return jnp.stack(start_z(shard))


def after_all(value, *others):
    flat, tree = jax.tree.flatten(value)
    tied = lax.optimization_barrier((tuple(flat), others))[0]
    return jax.tree.unflatten(tree, tied)


def add_low(*terms):
    return functools.reduce(jnp.add, [term.astype(F32) for term in terms]).astype(BF)


def exchange(arrays, fast):
    if fast:
        perms = (None, CORE, FLIP_X, FLIP_BOTH)
        return [arrays[0]] + [send(arrays[r], perms[r]) for r in (1, 2, 3)]
    return list(lax.all_to_all(jnp.stack(arrays), "tensor", 0, 0, tiled=True))


class Reduce:
    def __init__(self, sent, kept0, kept1):
        shape = (2, 4) + sent.shape[1:]
        self.kept = kept0.reshape(shape), kept1.reshape(shape)
        self.got = send(sent, CORE).reshape((2,) + shape)

    def one(self, *others):
        got = after_all(self.got, *others) if others else self.got
        self.got = got
        self.half = add_low(self.kept[1], got[1])
        return self.half

    def two(self, *others):
        self.got_two = after_all(send(self.half, SECOND), *others)
        self.quarter = add_low(self.kept[0][1], self.got[0, 1], self.got_two[1])
        return self.quarter

    def start_three(self):
        self.got_three = send(self.quarter, FIRST)

    def three(self):
        self.parts = [
            add_low(self.kept[0][0, s], self.got[0, 0, s], self.got_two[0, s], self.got_three[s])
            for s in range(4)
        ]
        return self.parts

    def start_last(self):
        return [send(self.parts[s], ALONG_Z[s]) for s in (1, 2, 3)]

    def end_last(self, got):
        return functools.reduce(jnp.add, [g.astype(F32) for g in [self.parts[0]] + list(got)])


def tables(z, y, x, c):
    far_core = np.array([0, 0, 0, 0, 1, 1, 1, 1])
    kind = np.array([0, 1, 2, 3] * 2)
    core = jnp.bitwise_xor(c, far_core)
    rel_x = jnp.where(kind == 0, 0, jnp.where(kind == 3, 1, jnp.where(kind == 1, core, 1 - core)))
    rel_y = jnp.where(kind == 0, 0, jnp.where(kind == 3, 1, jnp.where(kind == 1, 1 - core, core)))
    slots = far_core * 2 + rel_x
    back = np.arange(4)
    from_z = jnp.remainder(z - back, 4)
    weight_rows = (from_z[None, :] * 2 + jnp.bitwise_xor(y, rel_y)[:, None]).reshape(32)
    slot = np.arange(4)
    parts = jnp.bitwise_xor(x, slot % 2) * 2 + jnp.bitwise_xor(c, slot // 2)
    block = np.arange(NBLK)
    to_z = jnp.remainder(block // 2 - z, 4)
    to_y = jnp.bitwise_xor(block % 2, y)
    slot_core = jnp.bitwise_xor(c, slot // 2)[:, None]
    to_x = (slot % 2)[:, None]
    major = jnp.where(slot_core == 0, to_x, to_y[None, :])
    minor = jnp.where(slot_core == 0, to_y[None, :], to_x)
    targets = (major * 8 + minor * 4 + to_z[None, :]).reshape(4 * NBLK)
    qkv_rows = jnp.concatenate(
        [from_z * 2 + y, from_z * 2 + (1 - y)]
    )
    qkv_targets = to_y * 4 + to_z
    return parts, weight_rows, slots, targets, qkv_rows, qkv_targets


def shards(
    tokens,
    lengths,
    times,
    cotangent,
    w_qkv,
    w_out,
    w_up,
    up_bias,
    w_down,
    down_bias,
    norm1_gain,
    norm2_gain,
    ada_weight,
    ada_bias,
):
    groups, block, width = tokens.shape
    dp, tp = lax.axis_size("dp"), lax.axis_size("tensor")
    seq = block * tp
    t = lax.axis_index("tensor")
    d = lax.axis_index("dp")
    fast = dp == 8 and tp == 4
    feats = w_qkv.shape[2]
    fh = w_up.shape[1]
    rows = width // NBLK
    zero = jnp.zeros((), jnp.int32)
    z, y, x, c = (d // 2, d % 2, t // 2, t % 2) if fast else (zero, zero, zero, zero)
    here = t if fast else zero

    all_times = lax.all_to_all(
        jnp.broadcast_to(times[None, :], (dp, groups)), "dp", 0, 0, tiled=True
    ).reshape(-1)
    pad = (-feats) % 128
    qkv_shard = jnp.pad(w_qkv, ((0, 0), (0, 0), (0, pad)))
    if fast:
        near = gather_z(qkv_shard)
        all_times = after_all(all_times, near)
        qkv_pieces = (near, send(near, FLIP_Y))
    else:
        full = lax.all_gather(qkv_shard, "dp", axis=1, tiled=True)
        full = full.reshape(3, NBLK, rows, feats + pad).transpose(1, 0, 2, 3)
        order = [[(-j) % 4 * 2 + p for j in range(4)] for p in range(2)]
        qkv_pieces = tuple(jnp.stack([full[b] for b in order[p]]) for p in range(2))
    tok_all = lax.all_gather(tokens, "tensor", axis=1, tiled=True)

    condition = time_embedding(all_times, ada_weight.shape[0])
    part = jnp.dot(
        condition, ada_weight.astype(F32), precision=lax.Precision.HIGHEST
    ) + ada_bias.astype(F32)
    cols = part.shape[1]
    vectors = jnp.concatenate([up_bias, down_bias, norm1_gain, norm2_gain]).astype(F32)
    sent_mod = jnp.concatenate(
        [
            part.reshape(dp, groups * cols),
            jnp.broadcast_to(vectors[None, :], (dp, vectors.shape[0])),
        ],
        axis=1,
    )
    payload = lax.all_to_all(sent_mod, "dp", 0, 0, tiled=True)
    lengths, z, y, x, c, t, here, late_condition = after_all(
        (lengths, z, y, x, c, t, here, condition), sent_mod
    )
    parts, weight_rows, slots, targets, qkv_rows, qkv_targets = tables(z, y, x, c)
    cos, sin = rotary_halves(seq)
    ready = (
        qkv_rows.astype(jnp.int32),
        jnp.concatenate([lengths, here.reshape(1)]).astype(jnp.int32),
        jnp.concatenate([lengths, (t * block).reshape(1), parts, weight_rows, slots]).astype(
            jnp.int32
        ),
        targets.astype(jnp.int32),
        jnp.concatenate([qkv_targets, here.reshape(1)]).astype(jnp.int32),
        late_condition.reshape(dp, groups, -1).transpose(2, 1, 0).reshape(-1, dp * groups),
        jnp.concatenate([cos, cos] * 2, axis=1),
        jnp.concatenate([-sin, sin] * 2, axis=1),
        cos.T,
        sin.T,
    )
    payload, ready, qkv_pieces = after_all((payload, ready, qkv_pieces))
    qkv_rows, small_tab, tab, targets, back_tab, cond_t, cos_wide, sin_wide, cos_t, sin_t = ready
    mod = (
        payload[:, : groups * cols]
        .reshape(dp, groups, cols)
        .transpose(1, 0, 2)
        .reshape(groups, 6, width)
    )
    at = groups * cols
    small = []
    for count in (up_bias.shape[0], down_bias.shape[0], norm1_gain.shape[0], norm2_gain.shape[0]):
        small.append(payload[:, at : at + count].reshape(-1))
        at += count
    upb_all = small[0].reshape(tp, fh)
    downb_all, gain_one, gain_two = (v.reshape(1, width) for v in small[1:])

    up_shard = jnp.pad(
        jnp.concatenate([w_up, w_out.T], axis=1), ((0, 0), (0, (-fh - feats) % 128))
    )
    down_shard = w_down.T
    if fast:
        up_shard, down_shard = after_all((up_shard, down_shard), qkv_pieces[1], payload)
        up_parts = start_z(up_shard)
        down_parts = start_z(down_shard)
    else:

        def gather_pieces(shard):
            full = lax.all_gather(shard, "dp", axis=0, tiled=True)
            full = lax.all_gather(full, "tensor", axis=0, tiled=False)
            full = full.reshape(tp, NBLK, rows, full.shape[2])
            return [
                jnp.stack([full[rel_x * 2 + far, b] for b in order[rel_y]])
                for far in range(2)
                for rel_x, rel_y in ((0, 0), (far, 1 - far), (1 - far, far), (1, 1))
            ]

    q, k, v, kt, vt, w_all = qkv_call(
        qkv_rows, tok_all, mod, gain_one, cos_wide, sin_wide, *qkv_pieces
    )
    vt_later = vt
    if fast:
        up_near = jnp.stack(after_all(up_parts, vt))
        vt = after_all(vt, up_near)
        up_one, up_two = send(up_near, FIRST), send(up_near, SECOND)
    *mixed0, probs0, scale0 = attend_call(0, small_tab, q, k, vt)
    if fast:
        mixed0, up_near, up_one, up_two, down_parts = after_all(
            (mixed0, up_near, up_one, up_two, down_parts), probs0
        )
        vt_later = after_all(vt, up_one, up_two)
        mixed0_all = exchange(mixed0, fast)
        up_both = send(up_one, SECOND)
        up_far = [send(piece, CORE) for piece in (up_near, up_one, up_two)]
    *mixed1, probs1, scale1 = attend_call(1, small_tab, q, k, vt_later)
    if fast:
        mixed1, up_both = after_all((mixed1, up_both), probs1, *mixed0_all)
        mixed1 = after_all(mixed1, up_both)
        up_far.append(send(up_both, CORE))
        up_pieces = [up_near, up_one, up_two, up_both] + up_far
    else:
        up_pieces, down_pieces = gather_pieces(up_shard), gather_pieces(down_shard)
        mixed0_all = exchange(mixed0, fast)
    mixed1_all = exchange(mixed1, fast)

    if fast:
        down_near = jnp.stack(after_all(down_parts, probs1))
        mixed1_all, down_near, up_pieces, upb_all, gain_two = after_all(
            (mixed1_all, down_near, up_pieces, upb_all, gain_two)
        )
        down_one, down_two = send(down_near, FIRST), send(down_near, SECOND)
    after, att, second_t, gbr_t, sum_down_bias, act, slope = mlp_in_call(
        tab, tokens, cotangent, mod, gain_two, upb_all, (mixed0_all, mixed1_all), up_pieces
    )
    if fast:
        down_one, down_two, act = after_all((down_one, down_two, act), after)
        act = after_all(act, down_one, down_two)
        down_both = send(down_one, SECOND)
        down_far = [send(piece, CORE) for piece in (down_near, down_one, down_two)]
    gd_s, *gd_k = grad_call(down_grad_kernel, "down_grad", targets, [gbr_t], act, [], fh)
    if fast:
        gd_s, down_both, down_far = after_all((gd_s, down_both, down_far), *gd_k)
        gd_s = after_all(gd_s, down_both, *down_far)
        down_far.append(send(down_both, CORE))
        down_sum = Reduce(after_all(gd_s, down_far[3]), *gd_k)
        down_pieces = [down_near, down_one, down_two, down_both] + down_far
    out, sum_gate_two, upsum, gh = mlp_out_call(
        tab, cotangent, mod, downb_all, after, act, slope, down_pieces
    )
    if fast:
        gh = after_all(gh, down_sum.one(gh))
    *gms, sums_two, grad_after, gat_t = mlp_back_call(
        tab, cotangent, mod, gain_two, after, att, gh, up_pieces, feats
    )
    if fast:
        gms, gh = after_all((gms, gh), grad_after)
    gm = exchange(gms, fast)
    gu_s, *gu_k = grad_call(
        up_grad_kernel,
        "up_grad",
        targets,
        [second_t, gat_t],
        gh,
        [*mixed0_all, *mixed1_all],
        up_pieces[0].shape[2],
    )
    if fast:
        down_sum.two(*gu_k)
        gu_s = after_all(gu_s, down_sum.got_two, *gm)
        up_sum = Reduce(gu_s, *gu_k)
        gm = after_all(gm, up_sum.one(down_sum.quarter))
    grad_t0 = attend_back_call(0, small_tab, q, kt, v, probs0, scale0, gm, cos_t, sin_t)
    if fast:
        down_sum.quarter, quarter = after_all((down_sum.quarter, up_sum.two(grad_t0)), grad_t0)
        up_sum.quarter = quarter
        gm = after_all(gm, quarter, down_sum.quarter)
    grad_t1 = attend_back_call(1, small_tab, q, kt, v, probs1, scale1, gm, cos_t, sin_t)
    if fast:
        down_sum.start_three()
        up_sum.start_three()
        down_sum.got_three, up_sum.got_three = after_all(
            (down_sum.got_three, up_sum.got_three), grad_t1
        )
        down_parts = down_sum.three()
        down_got = down_sum.start_last()
        grad_t1 = after_all(grad_t1, *down_parts)
    fts, ftk, sums_one, dws, dwk = qkv_back_call(
        back_tab,
        grad_t0,
        grad_t1,
        tok_all,
        w_all,
        mod,
        gain_one,
    )

    if fast:
        fts, dws, up_sum.got_three, down_got = after_all((fts, dws, up_sum.got_three, down_got))
        up_sum.three()
        got, got_dw = send(fts, CORE), send(dws, FLIP_Y)
        got = after_all(got, *up_sum.parts)
        up_got = up_sum.start_last()
        far = add_low(ftk[1], got[1])
        sums_one, sums_two = after_all((sums_one, sums_two), far)
        far = send(far, FLIP_X)
    else:

        def absolute(sent, kept):
            lanes = sent.shape[2]
            near = kept.reshape(2, 2, 4, rows, lanes)
            far = sent.reshape(2, 2, 4, rows, lanes).transpose(1, 0, 2, 3, 4)
            both = jnp.stack([near, far], axis=1)
            return both.transpose(0, 1, 3, 2, 4, 5).reshape(tp, width, lanes).astype(F32)

        def reduce_all(sent, kept):
            terms = lax.psum_scatter(
                absolute(sent, kept), "tensor", scatter_dimension=0, tiled=True
            )[0]
            return lax.psum_scatter(terms, "dp", scatter_dimension=0, tiled=True)

        sum_up = reduce_all(gu_s, jnp.concatenate(gu_k))
        sum_down = reduce_all(gd_s, jnp.concatenate(gd_k))
        terms = jnp.stack([dwk, dws]).transpose(1, 0, 2, 3).reshape(width, -1).astype(F32)
        sum_qkv = lax.psum_scatter(terms, "dp", scatter_dimension=0, tiled=True)
        terms = jnp.stack([ftk, fts], axis=1).reshape(tp, groups, block, width).astype(F32)
        grad_first = lax.psum_scatter(terms, "tensor", scatter_dimension=0, tiled=True)[0]
        nought = jnp.zeros_like(grad_first)
        grad_in = norm_back_call(
            grad_first[None], nought[None], nought, tokens, grad_after, mod, gain_one
        )

    up_count, count = up_bias.shape[0], down_bias.shape[0]
    payload = pack_call(
        dp,
        tp,
        sums_one,
        sums_two,
        sum_gate_two,
        upsum,
        sum_down_bias,
        mod,
        gain_one,
        gain_two,
    ).reshape(dp * tp, 3, width)
    if fast:
        payload = after_all(payload, up_got[0])
    payload = lax.all_to_all(payload, ("dp", "tensor"), 0, 0, tiled=True)
    if fast:
        dw_parts = [add_low(dwk[s], got_dw[s]) for s in range(4)]
        dw_got = [send(dw_parts[s], ALONG_Z[s]) for s in (1, 2, 3)]
        far, up_got = after_all((far, up_got), *dw_parts)
        grad_in = norm_back_call(ftk, got, far, tokens, grad_after, mod, gain_one)
        payload = after_all(payload, grad_in)
    grad_adaw, grad_adab, g_up, g_down, g_one, g_two = small_call(
        payload.reshape(dp, tp, 3, width), cond_t, cols, up_count, count
    )
    if fast:
        dw_got = after_all(dw_got, grad_adaw)
        sum_up = up_sum.end_last(up_got)
        sum_down = down_sum.end_last(down_got)
        sum_qkv = functools.reduce(jnp.add, [g.astype(F32) for g in [dw_parts[0]] + dw_got])

    return (
        out,
        grad_in,
        jnp.stack([sum_qkv[:, j * feats : (j + 1) * feats] for j in range(3)]),
        sum_up[:, fh : fh + feats].T,
        sum_up[:, :fh],
        g_up,
        sum_down.T,
        g_down,
        g_one,
        g_two,
        grad_adaw.T,
        grad_adab,
    )


def solution(mesh):
    in_specs = (
        P("dp", "tensor", None),
        P("dp"),
        P("dp"),
        P("dp", "tensor", None),
        P(None, "dp", "tensor"),
        P("tensor", "dp"),
        P("dp", "tensor"),
        P("dp"),
        P("tensor", "dp"),
        P("dp"),
        P("dp"),
        P("dp"),
        P(None, "dp"),
        P("dp"),
    )
    out_specs = (
        P("dp", "tensor", None),
        P("dp", "tensor", None),
        P(None, "dp", "tensor"),
        P("tensor", "dp"),
        P("dp", "tensor"),
        P("dp"),
        P("tensor", "dp"),
        P("dp"),
        P("dp"),
        P("dp"),
        P(None, "dp"),
        P("dp"),
    )
    return jax.shard_map(shards, mesh=mesh, in_specs=in_specs, out_specs=out_specs, check_vma=False)
```

```python
import functools
import math

import jax
import jax.numpy as jnp
import numpy as np
from jax import lax
from jax.experimental import pallas as pl
from jax.experimental.pallas import tpu as pltpu
from jax.sharding import PartitionSpec as P

HEAD = 64
EPS = 1e-05
MASKED = -1e30
BF = jnp.bfloat16
F32 = jnp.float32
VMEM_MAX = 60 * 1024 * 1024
NBLK = 8
NT = (((1,), (1,)), ((), ()))


def spec(block, index_map):
    return pl.BlockSpec(block, index_map)


def whole(shape):
    return pl.BlockSpec(shape, lambda *_: (0,) * len(shape))


ANY = pl.BlockSpec(memory_space=pl.ANY)


def params():
    return pltpu.CompilerParams(vmem_limit_bytes=VMEM_MAX)


def cost(flops, moved, trans=0):
    return pl.CostEstimate(flops=flops, bytes_accessed=moved, transcendentals=trans)


def norm_rows(rows):
    centered = rows - jnp.mean(rows, axis=1, keepdims=True)
    variance = jnp.mean(centered * centered, axis=1, keepdims=True)
    inverse = lax.rsqrt(variance + EPS)
    return centered * inverse, inverse


def first_rows(tok, shift, scale, gain):
    normed, _ = norm_rows(tok.astype(F32))
    return (normed * (gain * (1.0 + scale)) + shift).astype(BF), normed


def qkv_kernel(tab, tok, mod, gain, cos, sin, w0, w1, q, k, v, kt, vt, w, sem):
    groups, heads, block = q.shape[:3]
    rows, wide = w0.shape[2], w.shape[2]

    @pl.when(pl.program_id(0) == 0)
    def _():
        copies = []
        for p, ref in enumerate((w0, w1)):
            for j in range(4):
                row = pl.multiple_of(tab[p * 4 + j] * rows, 16)
                copies.append(
                    pltpu.make_async_copy(
                        ref.at[j], w.at[:, pl.ds(row, rows), :], sem.at[p * 4 + j]
                    )
                )
        for copy in copies:
            copy.start()
        for copy in copies:
            copy.wait()

    low = lax.rem(lax.broadcasted_iota(jnp.int32, (block, wide), 1), HEAD) < HEAD // 2
    cos_wide = jnp.concatenate([cos[...]] * (wide // 128), axis=1)
    sin_wide = jnp.concatenate([sin[...]] * (wide // 128), axis=1)

    def rotate(vec):
        turned = jnp.where(
            low, pltpu.roll(vec, wide - HEAD // 2, 1), pltpu.roll(vec, HEAD // 2, 1)
        )
        return vec * cos_wide + turned * sin_wide

    for g in range(groups):

        def store_heads(ref, vec):
            for h in range(heads):
                shifted = vec if h == 0 else pltpu.roll(vec, wide - h * HEAD, 1)
                ref[g, h] = shifted[:, :HEAD].astype(BF)

        x, _ = first_rows(tok[g], mod[g, 0:1, :], mod[g, 1:2, :], gain[...])
        query = rotate(jnp.dot(x, w[0], preferred_element_type=F32))
        store_heads(q, query * (HEAD**-0.5))
        key = rotate(jnp.dot(x, w[1], preferred_element_type=F32))
        store_heads(k, key)
        kt[g] = key.T[: heads * HEAD].astype(BF)
        value = jnp.dot(x, w[2], preferred_element_type=F32)
        store_heads(v, value)
        vt[g] = value.T[: heads * HEAD].astype(BF)


def qkv_call(tab, tok_all, mod, gain, cos, sin, w0, w1):
    groups, seq, width = tok_all.shape
    block = seq // 4
    wide = w0.shape[3]
    heads = (wide // HEAD) * 3 // 4
    feats = heads * HEAD
    by_head = spec((groups, heads, block, HEAD), lambda j, _: (0, 0, j, 0))
    by_feat = spec((groups, feats, block), lambda j, _: (0, 0, j))
    grid_spec = pltpu.PrefetchScalarGridSpec(
        num_scalar_prefetch=1,
        grid=(4,),
        in_specs=[
            spec((groups, block, width), lambda j, _: (0, j, 0)),
            whole((groups, 6, width)),
            whole((1, width)),
            spec((block, 128), lambda j, _: (j, 0)),
            spec((block, 128), lambda j, _: (j, 0)),
            ANY,
            ANY,
        ],
        out_specs=[by_head, by_head, by_head, by_feat, by_feat, whole((3, width, wide))],
        scratch_shapes=[pltpu.SemaphoreType.DMA((8,))],
    )
    head_shape = jax.ShapeDtypeStruct((groups, heads, seq, HEAD), BF)
    turned = jax.ShapeDtypeStruct((groups, feats, seq), BF)
    return pl.pallas_call(
        qkv_kernel,
        grid_spec=grid_spec,
        out_shape=[
            head_shape,
            head_shape,
            head_shape,
            turned,
            turned,
            jax.ShapeDtypeStruct((3, width, wide), BF),
        ],
        compiler_params=params(),
        cost_estimate=cost(2 * groups * seq * width * wide * 3, 16 * 2**20),
        name="qkv",
    )(tab, tok_all, mod, gain, cos, sin, w0, w1)


CHUNK = 128
LEAST = 256


def unrolled(count, step, carried):
    for i in range(count):
        carried = step(i, carried)
    return carried


def eights(rows, op):
    return op(rows.reshape(rows.shape[0] // 8, 8, rows.shape[1]), axis=0)


def attend_kernel(tab, q, k, vt, mix0, mix1, mix2, mix3, probs, inverse, raw, mixed, *, group):
    heads = k.shape[1]
    block = q.shape[2]
    length = tab[group]
    chunks = k.shape[2] // CHUNK
    position = lax.broadcasted_iota(jnp.int32, (CHUNK, block), 0)

    def head(h, _):
        query = q[0, h]

        def score(c, largest):
            rows = slice(c * CHUNK, (c + 1) * CHUNK)
            scores = lax.dot_general(k[0, h, rows, :], query, NT, preferred_element_type=F32)
            if (c + 1) * CHUNK > LEAST:
                scores = jnp.where(position < length - c * CHUNK, scores, MASKED)
            raw[rows, :] = scores
            return jnp.maximum(largest, eights(scores, jnp.max))

        largest = unrolled(chunks, score, jnp.full((8, block), MASKED, F32))
        largest = jnp.max(largest, axis=0, keepdims=True)
        here = pl.ds(pl.multiple_of(h * HEAD, HEAD), HEAD)

        def weigh(c, carried):
            total, out = carried
            rows = slice(c * CHUNK, (c + 1) * CHUNK)
            weights = jnp.exp(raw[rows, :] - largest)
            low = weights.astype(BF)
            probs[h, rows, :] = low
            out = out + jnp.dot(vt[0, here, rows], low, preferred_element_type=F32)
            return total + eights(weights, jnp.sum), out

        total, out = unrolled(
            chunks, weigh, (jnp.zeros((8, block), F32), jnp.zeros((HEAD, block), F32))
        )
        scale = 1.0 / jnp.sum(total, axis=0, keepdims=True)
        inverse[h] = scale
        mixed[here, :] = (out * scale).astype(BF)
        return 0

    unrolled(heads, head, 0)
    for r, ref in enumerate((mix0, mix1, mix2, mix3)):

        @pl.when(turn(pl.program_id(0)) == r)
        def _():
            ref[...] = mixed[...]


def turn(step):
    return lax.rem(step + 1, 4)


def attend_call(group, tab, q, k, vt):
    _, heads, seq, _ = q.shape
    block = seq // 4
    feats = heads * HEAD

    def piece(i, tab):
        return lax.bitwise_xor(tab[2], turn(i))

    grid_spec = pltpu.PrefetchScalarGridSpec(
        num_scalar_prefetch=1,
        grid=(4,),
        in_specs=[
            spec((1, heads, block, HEAD), lambda i, tab: (group, 0, piece(i, tab), 0)),
            spec((1, heads, seq, HEAD), lambda i, tab: (group, 0, 0, 0)),
            spec((1, feats, seq), lambda i, tab: (group, 0, 0)),
        ],
        out_specs=[
            *[whole((feats, block))] * 4,
            spec((heads, seq, block), lambda i, tab: (0, 0, piece(i, tab))),
            spec((heads, 1, block), lambda i, tab: (0, 0, piece(i, tab))),
        ],
        scratch_shapes=[pltpu.VMEM((seq, block), F32), pltpu.VMEM((feats, block), BF)],
    )
    return pl.pallas_call(
        functools.partial(attend_kernel, group=group),
        grid_spec=grid_spec,
        out_shape=[
            *[jax.ShapeDtypeStruct((feats, block), BF)] * 4,
            jax.ShapeDtypeStruct((heads, seq, seq), BF),
            jax.ShapeDtypeStruct((heads, 1, seq), F32),
        ],
        compiler_params=params(),
        cost_estimate=cost(16 * heads * seq * seq * HEAD, 10 * 2**20, heads * seq * seq),
        name="attend",
    )(tab, q, k, vt)


def attend_back_kernel(
    tab, q, kt, v, probs, inverse, gm0, gm1, gm2, gm3, cos, sin, out, dk, dv, gm
):
    heads, block = q.shape[1], q.shape[2]
    half = HEAD // 2
    step = pl.program_id(0)
    j = lax.bitwise_xor(tab[2], step)

    @pl.when(step == 0)
    def _():
        dk[...] = jnp.zeros_like(dk)
        dv[...] = jnp.zeros_like(dv)
        for r, ref in enumerate((gm0, gm1, gm2, gm3)):
            gm[r] = ref[...]

    columns = pl.ds(pl.multiple_of(j * block, 128), block)
    cos_here, sin_here = cos[:, columns], sin[:, columns]

    def store_turned(plane, h, vec, c, s, where):
        low, high = vec[:half], vec[half:]
        base = pl.multiple_of(h * HEAD, HEAD)
        out[plane, pl.ds(base, half), where] = (low * c + high * s).astype(BF)
        out[plane, pl.ds(base + half, half), where] = (high * c - low * s).astype(BF)

    def head(h, _):
        here = pl.ds(pl.multiple_of(h * HEAD, HEAD), HEAD)
        scale = inverse[h]
        grad = (gm[step, here, :].astype(F32) * scale).astype(BF)
        query = q[0, h]

        low = probs[h]
        dp = jnp.dot(v[0, h], grad, preferred_element_type=F32)
        soft = low.astype(F32)
        prod = soft * dp
        inner = jnp.sum(prod, axis=0, keepdims=True) * scale
        ds = (prod - soft * inner).astype(BF)
        dv[h] += lax.dot_general(low, grad, NT, preferred_element_type=F32)
        dk[h] += jnp.dot(ds, query, preferred_element_type=F32)
        dq = jnp.dot(kt[0, here, :], ds, preferred_element_type=F32)
        store_turned(0, h, dq * (HEAD**-0.5), cos_here, sin_here, columns)
        return 0

    unrolled(heads, head, 0)

    @pl.when(step == pl.num_programs(0) - 1)
    def _():
        def turn_keys(h, _):
            store_turned(1, h, dk[h].T, cos[...], sin[...], slice(None))
            out[2, pl.ds(pl.multiple_of(h * HEAD, HEAD), HEAD), :] = dv[h].T.astype(BF)
            return 0

        unrolled(heads, turn_keys, 0)


def attend_back_call(group, tab, q, kt, v, probs, inverse, gm, cos, sin):
    _, heads, seq, _ = q.shape
    block = seq // 4
    feats = heads * HEAD
    half = HEAD // 2

    def piece(i, tab):
        return lax.bitwise_xor(tab[2], i)

    grid_spec = pltpu.PrefetchScalarGridSpec(
        num_scalar_prefetch=1,
        grid=(4,),
        in_specs=[
            spec((1, heads, block, HEAD), lambda i, tab: (group, 0, piece(i, tab), 0)),
            spec((1, feats, seq), lambda i, tab: (group, 0, 0)),
            spec((1, heads, seq, HEAD), lambda i, tab: (group, 0, 0, 0)),
            spec((heads, seq, block), lambda i, tab: (0, 0, piece(i, tab))),
            spec((heads, 1, block), lambda i, tab: (0, 0, piece(i, tab))),
            *[spec((feats, block), lambda i, tab: (0, group))] * 4,
            whole((half, seq)),
            whole((half, seq)),
        ],
        out_specs=whole((3, feats, seq)),
        scratch_shapes=[
            pltpu.VMEM((heads, seq, HEAD), F32),
            pltpu.VMEM((heads, seq, HEAD), F32),
            pltpu.VMEM((4, feats, block), BF),
        ],
    )
    return pl.pallas_call(
        attend_back_kernel,
        grid_spec=grid_spec,
        out_shape=jax.ShapeDtypeStruct((3, feats, seq), BF),
        compiler_params=params(),
        cost_estimate=cost(32 * heads * seq * seq * HEAD, 10 * 2**20),
        name="attend_back",
    )(tab, q, kt, v, probs, inverse, *gm, cos, sin)


def qkv_back_kernel(tab, gt0, gt1, tok, w, mod, gain, fts, ftk, sums, dws, dwk, acc):
    i = pl.program_id(0)
    feats, block = gt0.shape[1], gt0.shape[2]
    wide, width = w.shape[2], w.shape[1]
    rows, lanes = dws.shape[1:]

    @pl.when(i == 0)
    def _():
        acc[...] = jnp.zeros_like(acc)
        sums[...] = jnp.zeros_like(sums)

    for g, gt in enumerate((gt0, gt1)):
        first, normed = first_rows(tok[g], mod[g, 0:1, :], mod[g, 1:2, :], gain[...])
        total = None
        for j in range(3):
            part = gt[j]
            tall = part.astype(F32)
            if wide > feats:
                tall = jnp.concatenate([tall, jnp.zeros((wide - feats, block), F32)], axis=0)
            term = lax.dot_general(tall.T.astype(BF), w[j], NT, preferred_element_type=F32)
            total = term if total is None else total + term
            acc[j * feats : (j + 1) * feats] += jnp.dot(part, first, preferred_element_type=F32)
        sums[g, 0:1, :] += jnp.sum(total, axis=0, keepdims=True)
        sums[g, 1:2, :] += jnp.sum(total * normed, axis=0, keepdims=True)
        low = total.astype(BF)

        @pl.when(i < 2)
        def _():
            fts[0, g] = low

        @pl.when(i >= 2)
        def _():
            ftk[0, g] = low

    @pl.when(i == pl.num_programs(0) - 1)
    def _():
        flat = acc[...].T.astype(BF)
        for b in range(NBLK):
            part = flat[b * rows : (b + 1) * rows]
            there = tab[b]

            @pl.when(there < NBLK // 2)
            def _():
                dwk[there] = part

            @pl.when(there >= NBLK // 2)
            def _():
                dws[there - NBLK // 2] = part


def qkv_back_call(tab, gt0, gt1, tok_all, w, mod, gain):
    _, feats, seq = gt0.shape
    groups = tok_all.shape[0]
    block = seq // 4
    width = tok_all.shape[2]
    wide = w.shape[2]
    rows = width // NBLK
    lanes = 3 * feats + (-3 * feats) % 128

    def piece(i, tab):
        return lax.bitwise_xor(tab[NBLK], lax.rem(i, 2) * 2 + (1 - i // 2))

    by_feat = spec((3, feats, block), lambda i, tab: (0, 0, piece(i, tab)))
    grid_spec = pltpu.PrefetchScalarGridSpec(
        num_scalar_prefetch=1,
        grid=(4,),
        in_specs=[
            by_feat,
            by_feat,
            spec((groups, block, width), lambda i, tab: (0, piece(i, tab), 0)),
            whole((3, width, wide)),
            whole((groups, 6, width)),
            whole((1, width)),
        ],
        out_specs=[
            spec((1, groups, block, width), lambda i, tab: (jnp.minimum(i, 1), 0, 0, 0)),
            spec((1, groups, block, width), lambda i, tab: (jnp.maximum(i - 2, 0), 0, 0, 0)),
            whole((groups, 2, width)),
            whole((NBLK // 2, rows, lanes)),
            whole((NBLK // 2, rows, lanes)),
        ],
        scratch_shapes=[pltpu.VMEM((lanes, width), F32)],
    )
    terms = jax.ShapeDtypeStruct((2, groups, block, width), BF)
    share = jax.ShapeDtypeStruct((NBLK // 2, rows, lanes), BF)
    return pl.pallas_call(
        qkv_back_kernel,
        grid_spec=grid_spec,
        out_shape=[terms, terms, jax.ShapeDtypeStruct((groups, 2, width), F32), share, share],
        compiler_params=params(),
        cost_estimate=cost(4 * groups * seq * width * wide * 3, 16 * 2**20),
        name="qkv_back",
    )(tab, gt0, gt1, tok_all, w, mod, gain)


MIXED = (0, 2, 1, 3)
T_PART, T_ROW, T_SLOT = 3, 7, 39


def start_weights(tab, pieces, lanes, target, sem):
    rows = pieces[0].shape[1]
    for p in range(8):
        slot = tab[T_SLOT + p]
        for j in range(4):
            row = pl.multiple_of(tab[T_ROW + p * 4 + j] * rows, 16)
            pltpu.make_async_copy(
                pieces[p].at[j, :, lanes], target.at[slot, pl.ds(row, rows), :], sem.at[slot]
            ).start()


def wait_weights(target, k, sem):
    pltpu.make_async_copy(target.at[k], target.at[k], sem.at[k]).wait()


def live_cotangent(tab, cot, g):
    _, block, width = cot.shape
    position = tab[2] + lax.broadcasted_iota(jnp.int32, (block, width), 0)
    return jnp.where(position < tab[g], cot[g].astype(F32), 0.0)


def mlp_in_kernel(tab, tok, cot, mod, gain, upb, *rest):
    mixed, pieces, rest = (rest[:4], rest[4:8]), rest[8:16], rest[16:]
    sent, rest = rest[:4], rest[4:]
    sums, act, slope, w, wo, second, after, att, second_t, gbr_t, sem, sem_o, sem_s = rest
    groups, block, width = tok.shape
    feats = mixed[0][0].shape[0]
    fh = upb.shape[1]
    k = pl.program_id(0)

    @pl.when(k == 0)
    def _():
        start_weights(tab, pieces, slice(fh, None), wo, sem_o)
        start_weights(tab, pieces, slice(0, fh), w, sem)
        for g in range(groups):
            here = slice(g * block, (g + 1) * block)
            gb = (mod[g, 5:6, :] * live_cotangent(tab, cot, g)).astype(BF)
            gbr_t[:, here] = gb.T
            sums[g : g + 1, :] = jnp.sum(gb.astype(F32), axis=0, keepdims=True)
        for r in range(4):
            wait_weights(wo, r, sem_o)
        for g in range(groups):
            here = slice(g * block, (g + 1) * block)
            total = jnp.zeros((block, width), F32)
            for r in range(4):
                total += lax.dot_general(
                    mixed[g][MIXED[r]][...].T,
                    wo[r, :, :feats],
                    NT,
                    preferred_element_type=F32,
                )
            att[g] = total.astype(BF)
            rows_after = tok[g].astype(F32) + mod[g, 2:3, :] * total
            after[g] = rows_after
            n, _ = norm_rows(rows_after)
            x = n * (gain[...] * (1.0 + mod[g, 4:5, :])) + mod[g, 3:4, :]
            second[here, :] = x.astype(BF)
        second_t[...] = second[...].T
        start_late((after, att, second_t, gbr_t), sent, sem_s)

    @pl.when(k == 3)
    def _():
        wait_late((after, att, second_t, gbr_t), sent, sem_s)

    c1, c3 = math.sqrt(2.0 / math.pi), 0.044715
    wait_weights(w, k, sem)
    bias = upb[pl.ds(tab[T_PART + k], 1), :]
    hidden = jnp.dot(second[...], w[k], preferred_element_type=F32) + bias
    square = hidden * hidden
    th = jnp.tanh(c1 * hidden * (1.0 + c3 * square))
    up = 0.5 * (1.0 + th)
    act[0] = (hidden * up).astype(BF)
    slope[0] = (
        up + (0.5 * c1) * hidden * (1.0 - th * th) * (1.0 + (3.0 * c3) * square)
    ).astype(BF)


def mlp_out_kernel(tab, mod, downb, cot, act, slope, *rest):
    pieces, late, rest = rest[:8], rest[8:9], rest[9:]
    out, sums, upsum, gh, w, branch, gbr, after, sem, sem_late = rest
    groups, block, width = cot.shape
    k = pl.program_id(0)

    @pl.when(k == 0)
    def _():
        start_weights(tab, pieces, slice(None), w, sem)
        start_late(late, (after,), sem_late)
        for g in range(groups):
            grad_branch = mod[g, 5:6, :] * live_cotangent(tab, cot, g)
            gbr[g * block : (g + 1) * block, :] = grad_branch.astype(BF)
        branch[...] = jnp.broadcast_to(downb[...], branch.shape)

    wait_weights(w, k, sem)
    ga = jnp.dot(gbr[...], w[k], preferred_element_type=F32)
    grad = (ga * slope[0].astype(F32)).astype(BF)
    gh[0] = grad
    upsum[pl.ds(tab[T_PART + k], 1), :] = jnp.sum(grad.astype(F32), axis=0, keepdims=True)
    branch[...] += lax.dot_general(act[0], w[k], NT, preferred_element_type=F32)

    @pl.when(k == 3)
    def _():
        wait_late(late, (after,), sem_late)
        for g in range(groups):
            here = slice(g * block, (g + 1) * block)
            out[g] = (after[g] + mod[g, 5:6, :] * branch[here, :]).astype(BF)
            sums[g : g + 1, :] = jnp.sum(
                live_cotangent(tab, cot, g) * branch[here, :], axis=0, keepdims=True
            )


def start_late(sources, targets, sem):
    for i, (source, target) in enumerate(zip(sources, targets)):
        pltpu.make_async_copy(source, target, sem.at[i]).start()


def wait_late(sources, targets, sem):
    for i, (source, target) in enumerate(zip(sources, targets)):
        pltpu.make_async_copy(source, target, sem.at[i]).wait()


def mlp_back_kernel(tab, mod, gain, gh, *rest):
    pieces, late, rest = rest[:8], rest[8:11], rest[11:]
    gmixed, rest = rest[:4], rest[4:]
    sums, gafter, gat_t, w, wo, gsec, gat, cot, after, att, sem, sem_o, sem_late = rest
    groups, block, width = cot.shape
    feats = gmixed[0].shape[0]
    fh = gh.shape[2]
    k = pl.program_id(0)

    @pl.when(k == 0)
    def _():
        start_weights(tab, pieces, slice(0, fh), w, sem)
        start_weights(tab, pieces, slice(fh, None), wo, sem_o)
        start_late(late, (cot, after, att), sem_late)
        gsec[...] = jnp.zeros_like(gsec)

    wait_weights(w, k, sem)
    gsec[...] += lax.dot_general(gh[0], w[k], NT, preferred_element_type=F32)

    @pl.when(k == 3)
    def _():
        wait_late(late, (cot, after, att), sem_late)
        for r in range(4):
            wait_weights(wo, r, sem_o)
        for g in range(groups):
            here = slice(g * block, (g + 1) * block)
            n, inverse = norm_rows(after[g])
            gs = gsec[here, :]
            sums[g, 0:1, :] = jnp.sum(gs, axis=0, keepdims=True)
            sums[g, 1:2, :] = jnp.sum(gs * n, axis=0, keepdims=True)
            scaled = gs * (gain[...] * (1.0 + mod[g, 4:5, :]))
            mean = jnp.mean(scaled, axis=1, keepdims=True)
            along = jnp.mean(scaled * n, axis=1, keepdims=True)
            grad = live_cotangent(tab, cot, g) + inverse * (scaled - mean - n * along)
            gafter[g] = grad.astype(BF)
            sums[g, 2:3, :] = jnp.sum(grad * att[g].astype(F32), axis=0, keepdims=True)
            low = (mod[g, 2:3, :] * grad).astype(BF)
            gat[here, :] = low
            for r in range(4):
                gmixed[MIXED[r]][:, here] = (
                    jnp.dot(low, wo[r, :, :feats], preferred_element_type=F32)
                    .astype(BF)
                    .T
                )
        gat_t[...] = gat[...].T


def steps_call(
    kernel, name, tab, arrays, stepped, pieces, late, sent, outs, stepped_outs, scratch, sems, flops
):
    sm = pl.BlockSpec(memory_space=pltpu.SMEM)

    def slot_spec(shape):
        return spec((1,) + shape[1:], lambda k: (k, 0, 0))

    return pl.pallas_call(
        kernel,
        grid=(4,),
        in_specs=[sm]
        + [whole(a.shape) for a in arrays]
        + [slot_spec(a.shape) for a in stepped]
        + [ANY] * (len(pieces) + len(late)),
        out_specs=[ANY] * len(sent)
        + [whole(a.shape) for a in outs]
        + [slot_spec(a.shape) for a in stepped_outs],
        out_shape=list(sent) + list(outs) + list(stepped_outs),
        scratch_shapes=scratch
        + [pltpu.VMEM(a.shape, a.dtype) for a in [*late, *sent]]
        + [pltpu.SemaphoreType.DMA((4,))] * sems,
        compiler_params=params(),
        cost_estimate=cost(flops, 16 * 2**20),
        name=name,
    )(tab, *arrays, *stepped, *pieces, *late)


def struct(shape, dtype):
    return jax.ShapeDtypeStruct(shape, dtype)


def mlp_in_call(tab, tok, cot, mod, gain, upb, mixed, pieces):
    groups, block, width = tok.shape
    total, fh = groups * block, upb.shape[1]
    rows = struct((groups, block, width), F32)
    tall = struct((width, total), BF)
    wide = struct((4, total, fh), BF)

    return steps_call(
        mlp_in_kernel,
        "mlp_in",
        tab,
        [tok, cot, mod, gain, upb, *mixed[0], *mixed[1]],
        [],
        pieces,
        [],
        [rows, struct((groups, block, width), BF), tall, tall],
        [struct((groups, width), F32)],
        [wide, wide],
        [
            pltpu.VMEM((4, width, fh), BF),
            pltpu.VMEM((4, width, pieces[0].shape[2] - fh), BF),
            pltpu.VMEM((total, width), BF),
        ],
        3,
        10 * total * width * fh,
    )


def mlp_out_call(tab, cot, mod, downb, after, act, slope, pieces):
    groups, block, width = cot.shape
    total, fh = groups * block, act.shape[2]
    return steps_call(
        mlp_out_kernel,
        "mlp_out",
        tab,
        [mod, downb, cot],
        [act, slope],
        pieces,
        [after],
        [],
        [
            struct((groups, block, width), BF),
            struct((groups, width), F32),
            struct((4, fh), F32),
        ],
        [struct((4, total, fh), BF)],
        [
            pltpu.VMEM((4, width, fh), BF),
            pltpu.VMEM((total, width), F32),
            pltpu.VMEM((total, width), BF),
        ],
        2,
        16 * total * width * fh,
    )


def mlp_back_call(tab, cot, mod, gain, after, att, gh, pieces, feats):
    groups, block, width = cot.shape
    total, fh = groups * block, gh.shape[2]
    return steps_call(
        mlp_back_kernel,
        "mlp_back",
        tab,
        [mod, gain],
        [gh],
        pieces,
        [cot, after, att],
        [],
        [
            *[struct((feats, groups * block), BF)] * 4,
            struct((groups, 3, width), F32),
            struct((groups, block, width), BF),
            struct((width, total), BF),
        ],
        [],
        [
            pltpu.VMEM((4, width, fh), BF),
            pltpu.VMEM((4, width, pieces[0].shape[2] - fh), BF),
            pltpu.VMEM((total, width), F32),
            pltpu.VMEM((total, width), BF),
        ],
        3,
        10 * total * width * fh,
    )


def store_grads(tab, k, src, sent, kept0, kept1, sem):
    rows = src.shape[1] // NBLK
    for b in range(NBLK):
        there = tab[k * NBLK + b]
        piece = src.at[k, pl.ds(b * rows, rows), :]

        @pl.when(k >= 2)
        def _():
            pltpu.make_async_copy(piece, sent.at[there], sem.at[k, b]).start()

        @pl.when((k < 2) & (there < 8))
        def _():
            pltpu.make_async_copy(piece, kept0.at[there], sem.at[k, b]).start()

        @pl.when((k < 2) & (there >= 8))
        def _():
            pltpu.make_async_copy(piece, kept1.at[there - 8], sem.at[k, b]).start()


def wait_grads(src, sent, sem):
    rows = src.shape[1] // NBLK
    for k in range(4):
        for b in range(NBLK):
            pltpu.make_async_copy(
                src.at[k, pl.ds(b * rows, rows), :], sent.at[0], sem.at[k, b]
            ).wait()


def down_grad_kernel(tab, gbr_t, act, sent, kept0, kept1, acc, sem):
    k = pl.program_id(0)
    acc[k] = jnp.dot(gbr_t[...], act[0], preferred_element_type=F32).astype(BF)
    store_grads(tab, k, acc, sent, kept0, kept1, sem)

    @pl.when(k == 3)
    def _():
        wait_grads(acc, sent, sem)


def up_grad_kernel(tab, second_t, gat_t, gh, *rest):
    mixed, (sent, kept0, kept1, acc, sem) = (rest[:4], rest[4:8]), rest[8:]
    k = pl.program_id(0)
    fh = gh.shape[2]
    feats, block = mixed[0][0].shape
    acc[k, :, :fh] = jnp.dot(second_t[...], gh[0], preferred_element_type=F32).astype(BF)
    if acc.shape[2] > fh + feats:
        acc[k, :, fh + feats :] = jnp.zeros((acc.shape[1], acc.shape[2] - fh - feats), BF)
    for r in range(4):

        @pl.when(k == r)
        def _():
            total = None
            for g in range(2):
                term = lax.dot_general(
                    gat_t[:, g * block : (g + 1) * block],
                    mixed[g][MIXED[r]][...],
                    NT,
                    preferred_element_type=F32,
                )
                total = term if total is None else total + term
            acc[k, :, fh : fh + feats] = total.astype(BF)

    store_grads(tab, k, acc, sent, kept0, kept1, sem)

    @pl.when(k == 3)
    def _():
        wait_grads(acc, sent, sem)


def grad_call(kernel, name, tab, fixed, moving, others, lanes):
    width, total = fixed[0].shape
    fh = moving.shape[2]
    rows = width // NBLK
    grid_spec = pltpu.PrefetchScalarGridSpec(
        num_scalar_prefetch=1,
        grid=(4,),
        in_specs=[whole(a.shape) for a in fixed]
        + [spec((1, total, fh), lambda k, _: (k, 0, 0))]
        + [whole(a.shape) for a in others],
        out_specs=[ANY, ANY, ANY],
        scratch_shapes=[
            pltpu.VMEM((4, width, lanes), BF),
            pltpu.SemaphoreType.DMA((4, NBLK)),
        ],
    )
    return pl.pallas_call(
        kernel,
        grid_spec=grid_spec,
        out_shape=[struct((16, rows, lanes), BF)] + [struct((8, rows, lanes), BF)] * 2,
        compiler_params=params(),
        cost_estimate=cost(8 * width * total * lanes, 14 * 2**20),
        name=name,
    )(tab, *fixed, moving, *others)


def norm_back_kernel(t0, t1, t2, tok, after, mod, gain, out):
    normed, inverse = norm_rows(tok[0].astype(F32))
    grad = t0[0, 0].astype(F32) + t1[0, 0].astype(F32) + t2[0].astype(F32)
    scaled = grad * (gain[...] * (1.0 + mod[0, 1:2, :]))
    mean = jnp.mean(scaled, axis=1, keepdims=True)
    along = jnp.mean(scaled * normed, axis=1, keepdims=True)
    out[0] = (after[0].astype(F32) + inverse * (scaled - mean - normed * along)).astype(BF)


def norm_back_call(t0, t1, t2, tok, after, mod, gain):
    groups, block, width = tok.shape
    row = spec((1, block, width), lambda g: (g, 0, 0))
    near = spec((1, 1, block, width), lambda g: (0, g, 0, 0))
    return pl.pallas_call(
        norm_back_kernel,
        grid=(groups,),
        in_specs=[near, near, row, row, row, spec((1, 6, width), lambda g: (g, 0, 0)), whole((1, width))],
        out_specs=row,
        out_shape=jax.ShapeDtypeStruct((groups, block, width), BF),
        compiler_params=params(),
        cost_estimate=cost(40 * groups * block * width, 12 * groups * block * width),
        name="norm_back",
    )(t0, t1, t2, tok, after, mod, gain)


AT = 640


def pack_kernel(one, two, gate_two, upsum, down_bias, mod, gain_one, gain_two, out):
    dp, tp, _, width = out.shape
    groups = one.shape[0]
    lane = lax.broadcasted_iota(jnp.int32, (1, width), 1)

    def window(rows, start, count, at=0):
        row, offset = divmod(start, width)
        first = min(count, width - offset)
        got = rows[row]
        shift = (at - offset) % width
        got = pltpu.roll(got, shift, 1) if shift else got
        if first < count:
            shift = (at + first) % width
            rest = rows[row + 1]
            rest = pltpu.roll(rest, shift, 1) if shift else rest
            got = jnp.where(lane < at + first, got, rest)
        return got

    mods, count_mod = [], 6 * width // dp
    for g in range(groups):
        mods.append(
            [
                one[g, 0:1, :],
                gain_one[...] * one[g, 1:2, :],
                two[g, 2:3, :],
                two[g, 0:1, :],
                gain_two[...] * two[g, 1:2, :],
                gate_two[g : g + 1, :],
            ]
        )
    zero = jnp.zeros((1, width), F32)
    vectors = [zero, zero, zero]
    for g in range(groups):
        vectors[0] += down_bias[g : g + 1, :]
        vectors[1] += (1.0 + mod[g, 1:2, :]) * one[g, 1:2, :]
        vectors[2] += (1.0 + mod[g, 4:5, :]) * two[g, 1:2, :]
    rows_up = [upsum[r : r + 1, :] for r in range(upsum.shape[0])]
    count_up, count = upsum.shape[0] * width // dp, width // dp
    for d in range(dp):
        firsts = [window(mods[g], d * count_mod, count_mod) for g in range(groups)]
        firsts.append(window(rows_up, d * count_up, count_up))
        for r in range(3):
            row = jnp.where(lane < AT, firsts[r], window([vectors[r]], d * count, count, AT))
            for t in range(tp):
                out[d, t, r : r + 1, :] = row


def pack_call(dp, tp, one, two, gate_two, upsum, down_bias, mod, gain_one, gain_two):
    vm = pl.BlockSpec(memory_space=pltpu.VMEM)
    return pl.pallas_call(
        pack_kernel,
        in_specs=[vm] * 8,
        out_specs=vm,
        out_shape=struct((dp, tp, 3, one.shape[2]), F32),
        compiler_params=params(),
        cost_estimate=cost(1024, 1024),
        name="pack",
    )(one, two, gate_two, upsum, down_bias, mod, gain_one, gain_two)


def small_kernel(got, cond_t, adaw, adab, upb, downb, gain_one, gain_two):
    dp = got.shape[0]
    cols = adaw.shape[0]
    total = jnp.sum(got[...], axis=1)
    mods = jnp.concatenate([total[:, 0, :], total[:, 1, :]], axis=0)
    product = lax.dot_general(
        mods,
        cond_t[...],
        (((0,), (1,)), ((), ())),
        precision=lax.Precision.HIGHEST,
        preferred_element_type=F32,
    )
    adaw[...] = product[:cols]
    flat = jnp.sum(total, axis=0)
    adab[...] = (flat[0:1, :cols] + flat[1:2, :cols]).reshape(cols)
    upb[...] = flat[2:3, : upb.shape[0]].reshape(upb.shape[0])
    for row, ref in enumerate((downb, gain_one, gain_two)):
        ref[...] = flat[row : row + 1, AT : AT + ref.shape[0]].reshape(ref.shape[0])


def small_call(got, cond_t, cols, up_count, count):
    shapes = [(cols, cond_t.shape[0]), (cols,), (up_count,)] + [(count,)] * 3
    vm = pl.BlockSpec(memory_space=pltpu.VMEM)
    return pl.pallas_call(
        small_kernel,
        in_specs=[vm, vm],
        out_specs=[vm] * 6,
        out_shape=[jax.ShapeDtypeStruct(shape, F32) for shape in shapes],
        compiler_params=params(),
        cost_estimate=cost(1024, 1024),
        name="small",
    )(got, cond_t)


def time_embedding(time_steps, width_total):
    half_width = width_total // 2
    frequency = jnp.exp(-math.log(10000.0) * jnp.arange(half_width, dtype=F32) / half_width)
    angles = time_steps.astype(F32)[:, None] * frequency[None, :]
    return jnp.concatenate([jnp.cos(angles), jnp.sin(angles)], axis=-1)


def rotary_halves(length_total):
    half = HEAD // 2
    inverse = jnp.exp(-math.log(10000.0) * 2.0 * jnp.arange(half, dtype=F32) / HEAD)
    angles = jnp.arange(length_total, dtype=F32)[:, None] * inverse[None, :]
    return jnp.cos(angles), jnp.sin(angles)


def device_index(z, y, x, c):
    return ((z * 2 + y) * 2 + x) * 2 + c


def permutation(move):
    pairs = []
    for z in range(4):
        for y in range(2):
            for x in range(2):
                for c in range(2):
                    pairs.append((device_index(z, y, x, c), device_index(*move(z, y, x, c))))
    return pairs


CORE = permutation(lambda z, y, x, c: (z, y, x, 1 - c))
FLIP_X = permutation(lambda z, y, x, c: (z, y, 1 - x, c))
FLIP_BOTH = permutation(lambda z, y, x, c: (z, y, 1 - x, 1 - c))
FLIP_Y = permutation(lambda z, y, x, c: (z, 1 - y, x, c))
FIRST = permutation(lambda z, y, x, c: (z, 1 - y, x, c) if c == 0 else (z, y, 1 - x, c))
SECOND = permutation(lambda z, y, x, c: (z, y, 1 - x, c) if c == 0 else (z, 1 - y, x, c))
ALONG_Z = [permutation(lambda z, y, x, c, s=s: ((z + s) % 4, y, x, c)) for s in range(4)]


def send(array, pairs):
    return lax.ppermute(array, ("dp", "tensor"), pairs)


def start_z(shard):
    return [shard] + [send(shard, ALONG_Z[s]) for s in (1, 2, 3)]


def gather_z(shard):
    return jnp.stack(start_z(shard))


def after_all(value, *others):
    flat, tree = jax.tree.flatten(value)
    tied = lax.optimization_barrier((tuple(flat), others))[0]
    return jax.tree.unflatten(tree, tied)


def add_low(*terms):
    return functools.reduce(jnp.add, [term.astype(F32) for term in terms]).astype(BF)


def exchange(arrays, fast):
    if fast:
        perms = (None, CORE, FLIP_X, FLIP_BOTH)
        return [arrays[0]] + [send(arrays[r], perms[r]) for r in (1, 2, 3)]
    return list(lax.all_to_all(jnp.stack(arrays), "tensor", 0, 0, tiled=True))


class Reduce:
    def __init__(self, sent, kept0, kept1):
        shape = (2, 4) + sent.shape[1:]
        self.kept = kept0.reshape(shape), kept1.reshape(shape)
        self.got = send(sent, CORE).reshape((2,) + shape)

    def one(self, *others):
        got = after_all(self.got, *others) if others else self.got
        self.got = got
        self.half = add_low(self.kept[1], got[1])
        return self.half

    def two(self, *others):
        self.got_two = after_all(send(self.half, SECOND), *others)
        self.quarter = add_low(self.kept[0][1], self.got[0, 1], self.got_two[1])
        return self.quarter

    def start_three(self):
        self.got_three = send(self.quarter, FIRST)

    def three(self):
        self.parts = [
            add_low(self.kept[0][0, s], self.got[0, 0, s], self.got_two[0, s], self.got_three[s])
            for s in range(4)
        ]
        return self.parts

    def start_last(self):
        return [send(self.parts[s], ALONG_Z[s]) for s in (1, 2, 3)]

    def end_last(self, got):
        return functools.reduce(jnp.add, [g.astype(F32) for g in [self.parts[0]] + list(got)])


def tables(z, y, x, c):
    far_core = np.array([0, 0, 0, 0, 1, 1, 1, 1])
    kind = np.array([0, 1, 2, 3] * 2)
    core = jnp.bitwise_xor(c, far_core)
    rel_x = jnp.where(kind == 0, 0, jnp.where(kind == 3, 1, jnp.where(kind == 1, core, 1 - core)))
    rel_y = jnp.where(kind == 0, 0, jnp.where(kind == 3, 1, jnp.where(kind == 1, 1 - core, core)))
    slots = far_core * 2 + rel_x
    back = np.arange(4)
    from_z = jnp.remainder(z - back, 4)
    weight_rows = (from_z[None, :] * 2 + jnp.bitwise_xor(y, rel_y)[:, None]).reshape(32)
    slot = np.arange(4)
    parts = jnp.bitwise_xor(x, slot % 2) * 2 + jnp.bitwise_xor(c, slot // 2)
    block = np.arange(NBLK)
    to_z = jnp.remainder(block // 2 - z, 4)
    to_y = jnp.bitwise_xor(block % 2, y)
    slot_core = jnp.bitwise_xor(c, slot // 2)[:, None]
    to_x = (slot % 2)[:, None]
    major = jnp.where(slot_core == 0, to_x, to_y[None, :])
    minor = jnp.where(slot_core == 0, to_y[None, :], to_x)
    targets = (major * 8 + minor * 4 + to_z[None, :]).reshape(4 * NBLK)
    qkv_rows = jnp.concatenate(
        [from_z * 2 + y, from_z * 2 + (1 - y)]
    )
    qkv_targets = to_y * 4 + to_z
    return parts, weight_rows, slots, targets, qkv_rows, qkv_targets


def shards(
    tokens,
    lengths,
    times,
    cotangent,
    w_qkv,
    w_out,
    w_up,
    up_bias,
    w_down,
    down_bias,
    norm1_gain,
    norm2_gain,
    ada_weight,
    ada_bias,
):
    groups, block, width = tokens.shape
    dp, tp = lax.axis_size("dp"), lax.axis_size("tensor")
    seq = block * tp
    t = lax.axis_index("tensor")
    d = lax.axis_index("dp")
    fast = dp == 8 and tp == 4
    feats = w_qkv.shape[2]
    fh = w_up.shape[1]
    rows = width // NBLK
    zero = jnp.zeros((), jnp.int32)
    z, y, x, c = (d // 2, d % 2, t // 2, t % 2) if fast else (zero, zero, zero, zero)
    here = t if fast else zero

    all_times = lax.all_to_all(
        jnp.broadcast_to(times[None, :], (dp, groups)), "dp", 0, 0, tiled=True
    ).reshape(-1)
    pad = (-feats) % 128
    qkv_shard = jnp.pad(w_qkv, ((0, 0), (0, 0), (0, pad)))
    if fast:
        near = gather_z(qkv_shard)
        all_times = after_all(all_times, near)
        qkv_pieces = (near, send(near, FLIP_Y))
    else:
        full = lax.all_gather(qkv_shard, "dp", axis=1, tiled=True)
        full = full.reshape(3, NBLK, rows, feats + pad).transpose(1, 0, 2, 3)
        order = [[(-j) % 4 * 2 + p for j in range(4)] for p in range(2)]
        qkv_pieces = tuple(jnp.stack([full[b] for b in order[p]]) for p in range(2))
    tok_all = lax.all_gather(tokens, "tensor", axis=1, tiled=True)

    condition = time_embedding(all_times, ada_weight.shape[0])
    part = jnp.dot(
        condition, ada_weight.astype(F32), precision=lax.Precision.HIGHEST
    ) + ada_bias.astype(F32)
    cols = part.shape[1]
    vectors = jnp.concatenate([up_bias, down_bias, norm1_gain, norm2_gain]).astype(F32)
    sent_mod = jnp.concatenate(
        [
            part.reshape(dp, groups * cols),
            jnp.broadcast_to(vectors[None, :], (dp, vectors.shape[0])),
        ],
        axis=1,
    )
    payload = lax.all_to_all(sent_mod, "dp", 0, 0, tiled=True)
    lengths, z, y, x, c, t, here, late_condition = after_all(
        (lengths, z, y, x, c, t, here, condition), sent_mod
    )
    parts, weight_rows, slots, targets, qkv_rows, qkv_targets = tables(z, y, x, c)
    cos, sin = rotary_halves(seq)
    ready = (
        qkv_rows.astype(jnp.int32),
        jnp.concatenate([lengths, here.reshape(1)]).astype(jnp.int32),
        jnp.concatenate([lengths, (t * block).reshape(1), parts, weight_rows, slots]).astype(
            jnp.int32
        ),
        targets.astype(jnp.int32),
        jnp.concatenate([qkv_targets, here.reshape(1)]).astype(jnp.int32),
        late_condition.reshape(dp, groups, -1).transpose(2, 1, 0).reshape(-1, dp * groups),
        jnp.concatenate([cos, cos] * 2, axis=1),
        jnp.concatenate([-sin, sin] * 2, axis=1),
        cos.T,
        sin.T,
    )
    payload, ready, qkv_pieces = after_all((payload, ready, qkv_pieces))
    qkv_rows, small_tab, tab, targets, back_tab, cond_t, cos_wide, sin_wide, cos_t, sin_t = ready
    mod = (
        payload[:, : groups * cols]
        .reshape(dp, groups, cols)
        .transpose(1, 0, 2)
        .reshape(groups, 6, width)
    )
    at = groups * cols
    small = []
    for count in (up_bias.shape[0], down_bias.shape[0], norm1_gain.shape[0], norm2_gain.shape[0]):
        small.append(payload[:, at : at + count].reshape(-1))
        at += count
    upb_all = small[0].reshape(tp, fh)
    downb_all, gain_one, gain_two = (v.reshape(1, width) for v in small[1:])

    up_shard = jnp.pad(
        jnp.concatenate([w_up, w_out.T], axis=1), ((0, 0), (0, (-fh - feats) % 128))
    )
    down_shard = w_down.T
    if fast:
        up_shard, down_shard = after_all((up_shard, down_shard), qkv_pieces[1], payload)
        up_parts = start_z(up_shard)
        down_parts = start_z(down_shard)
    else:

        def gather_pieces(shard):
            full = lax.all_gather(shard, "dp", axis=0, tiled=True)
            full = lax.all_gather(full, "tensor", axis=0, tiled=False)
            full = full.reshape(tp, NBLK, rows, full.shape[2])
            return [
                jnp.stack([full[rel_x * 2 + far, b] for b in order[rel_y]])
                for far in range(2)
                for rel_x, rel_y in ((0, 0), (far, 1 - far), (1 - far, far), (1, 1))
            ]

    q, k, v, kt, vt, w_all = qkv_call(
        qkv_rows, tok_all, mod, gain_one, cos_wide, sin_wide, *qkv_pieces
    )
    vt_later = vt
    if fast:
        up_near = jnp.stack(after_all(up_parts, vt))
        vt = after_all(vt, up_near)
        up_one, up_two = send(up_near, FIRST), send(up_near, SECOND)
    *mixed0, probs0, scale0 = attend_call(0, small_tab, q, k, vt)
    if fast:
        mixed0, up_near, up_one, up_two, down_parts = after_all(
            (mixed0, up_near, up_one, up_two, down_parts), probs0
        )
        vt_later = after_all(vt, up_one, up_two)
        mixed0_all = exchange(mixed0, fast)
        up_both = send(up_one, SECOND)
        up_far = [send(piece, CORE) for piece in (up_near, up_one, up_two)]
    *mixed1, probs1, scale1 = attend_call(1, small_tab, q, k, vt_later)
    if fast:
        mixed1, up_both = after_all((mixed1, up_both), probs1, *mixed0_all)
        mixed1 = after_all(mixed1, up_both)
        up_far.append(send(up_both, CORE))
        up_pieces = [up_near, up_one, up_two, up_both] + up_far
    else:
        up_pieces, down_pieces = gather_pieces(up_shard), gather_pieces(down_shard)
        mixed0_all = exchange(mixed0, fast)
    mixed1_all = exchange(mixed1, fast)

    if fast:
        down_near = jnp.stack(after_all(down_parts, probs1))
        mixed1_all, down_near, up_pieces, upb_all, gain_two = after_all(
            (mixed1_all, down_near, up_pieces, upb_all, gain_two)
        )
        down_one, down_two = send(down_near, FIRST), send(down_near, SECOND)
    after, att, second_t, gbr_t, sum_down_bias, act, slope = mlp_in_call(
        tab, tokens, cotangent, mod, gain_two, upb_all, (mixed0_all, mixed1_all), up_pieces
    )
    if fast:
        down_one, down_two, act = after_all((down_one, down_two, act), after)
        act = after_all(act, down_one, down_two)
        down_both = send(down_one, SECOND)
        down_far = [send(piece, CORE) for piece in (down_near, down_one, down_two)]
    gd_s, *gd_k = grad_call(down_grad_kernel, "down_grad", targets, [gbr_t], act, [], fh)
    if fast:
        gd_s, down_both, down_far = after_all((gd_s, down_both, down_far), *gd_k)
        gd_s = after_all(gd_s, down_both, *down_far)
        down_far.append(send(down_both, CORE))
        down_sum = Reduce(after_all(gd_s, down_far[3]), *gd_k)
        down_pieces = [down_near, down_one, down_two, down_both] + down_far
    out, sum_gate_two, upsum, gh = mlp_out_call(
        tab, cotangent, mod, downb_all, after, act, slope, down_pieces
    )
    if fast:
        gh = after_all(gh, down_sum.one(gh))
    *gms, sums_two, grad_after, gat_t = mlp_back_call(
        tab, cotangent, mod, gain_two, after, att, gh, up_pieces, feats
    )
    if fast:
        gms, gh = after_all((gms, gh), grad_after)
    gm = exchange(gms, fast)
    gu_s, *gu_k = grad_call(
        up_grad_kernel,
        "up_grad",
        targets,
        [second_t, gat_t],
        gh,
        [*mixed0_all, *mixed1_all],
        up_pieces[0].shape[2],
    )
    if fast:
        down_sum.two(*gu_k)
        gu_s = after_all(gu_s, down_sum.got_two, *gm)
        up_sum = Reduce(gu_s, *gu_k)
        gm = after_all(gm, up_sum.one(down_sum.quarter))
    grad_t0 = attend_back_call(0, small_tab, q, kt, v, probs0, scale0, gm, cos_t, sin_t)
    if fast:
        down_sum.quarter, quarter = after_all((down_sum.quarter, up_sum.two(grad_t0)), grad_t0)
        up_sum.quarter = quarter
        gm = after_all(gm, quarter, down_sum.quarter)
    grad_t1 = attend_back_call(1, small_tab, q, kt, v, probs1, scale1, gm, cos_t, sin_t)
    if fast:
        down_sum.start_three()
        up_sum.start_three()
        down_sum.got_three, up_sum.got_three = after_all(
            (down_sum.got_three, up_sum.got_three), grad_t1
        )
        down_parts = down_sum.three()
        down_got = down_sum.start_last()
        grad_t1 = after_all(grad_t1, *down_parts)
    fts, ftk, sums_one, dws, dwk = qkv_back_call(
        back_tab,
        grad_t0,
        grad_t1,
        tok_all,
        w_all,
        mod,
        gain_one,
    )

    if fast:
        fts, dws, up_sum.got_three, down_got = after_all((fts, dws, up_sum.got_three, down_got))
        up_sum.three()
        got, got_dw = send(fts, CORE), send(dws, FLIP_Y)
        got = after_all(got, *up_sum.parts)
        up_got = up_sum.start_last()
        far = add_low(ftk[1], got[1])
        sums_one, sums_two = after_all((sums_one, sums_two), far)
        far = send(far, FLIP_X)
    else:

        def absolute(sent, kept):
            lanes = sent.shape[2]
            near = kept.reshape(2, 2, 4, rows, lanes)
            far = sent.reshape(2, 2, 4, rows, lanes).transpose(1, 0, 2, 3, 4)
            both = jnp.stack([near, far], axis=1)
            return both.transpose(0, 1, 3, 2, 4, 5).reshape(tp, width, lanes).astype(F32)

        def reduce_all(sent, kept):
            terms = lax.psum_scatter(
                absolute(sent, kept), "tensor", scatter_dimension=0, tiled=True
            )[0]
            return lax.psum_scatter(terms, "dp", scatter_dimension=0, tiled=True)

        sum_up = reduce_all(gu_s, jnp.concatenate(gu_k))
        sum_down = reduce_all(gd_s, jnp.concatenate(gd_k))
        terms = jnp.stack([dwk, dws]).transpose(1, 0, 2, 3).reshape(width, -1).astype(F32)
        sum_qkv = lax.psum_scatter(terms, "dp", scatter_dimension=0, tiled=True)
        terms = jnp.stack([ftk, fts], axis=1).reshape(tp, groups, block, width).astype(F32)
        grad_first = lax.psum_scatter(terms, "tensor", scatter_dimension=0, tiled=True)[0]
        nought = jnp.zeros_like(grad_first)
        grad_in = norm_back_call(
            grad_first[None], nought[None], nought, tokens, grad_after, mod, gain_one
        )

    up_count, count = up_bias.shape[0], down_bias.shape[0]
    payload = pack_call(
        dp,
        tp,
        sums_one,
        sums_two,
        sum_gate_two,
        upsum,
        sum_down_bias,
        mod,
        gain_one,
        gain_two,
    ).reshape(dp * tp, 3, width)
    payload = lax.all_to_all(payload, ("dp", "tensor"), 0, 0, tiled=True)
    if fast:
        dw_parts = [add_low(dwk[s], got_dw[s]) for s in range(4)]
        dw_got = [send(dw_parts[s], ALONG_Z[s]) for s in (1, 2, 3)]
        far, up_got = after_all((far, up_got), *dw_parts)
        grad_in = norm_back_call(ftk, got, far, tokens, grad_after, mod, gain_one)
        payload = after_all(payload, grad_in)
    grad_adaw, grad_adab, g_up, g_down, g_one, g_two = small_call(
        payload.reshape(dp, tp, 3, width), cond_t, cols, up_count, count
    )
    if fast:
        dw_got = after_all(dw_got, grad_adaw)
        sum_up = up_sum.end_last(up_got)
        sum_down = down_sum.end_last(down_got)
        sum_qkv = functools.reduce(jnp.add, [g.astype(F32) for g in [dw_parts[0]] + dw_got])

    return (
        out,
        grad_in,
        jnp.stack([sum_qkv[:, j * feats : (j + 1) * feats] for j in range(3)]),
        sum_up[:, fh : fh + feats].T,
        sum_up[:, :fh],
        g_up,
        sum_down.T,
        g_down,
        g_one,
        g_two,
        grad_adaw.T,
        grad_adab,
    )


def solution(mesh):
    in_specs = (
        P("dp", "tensor", None),
        P("dp"),
        P("dp"),
        P("dp", "tensor", None),
        P(None, "dp", "tensor"),
        P("tensor", "dp"),
        P("dp", "tensor"),
        P("dp"),
        P("tensor", "dp"),
        P("dp"),
        P("dp"),
        P("dp"),
        P(None, "dp"),
        P("dp"),
    )
    out_specs = (
        P("dp", "tensor", None),
        P("dp", "tensor", None),
        P(None, "dp", "tensor"),
        P("tensor", "dp"),
        P("dp", "tensor"),
        P("dp"),
        P("tensor", "dp"),
        P("dp"),
        P("dp"),
        P("dp"),
        P(None, "dp"),
        P("dp"),
    )
    return jax.shard_map(shards, mesh=mesh, in_specs=in_specs, out_specs=out_specs, check_vma=False)
```
